32 devices in a mesh: dp: 2 (over y), mem: 16 (over z, x, core).
Axes of the slice: x: 2, y: 2, z: 4, core: 2. Of those that a mesh axis runs over, the one named last changes fastest.
Arguments:
- tokens: bfloat16 [4096, 1024], P(('dp', 'mem')), may hold values from -6 to 6
- gain_attn: bfloat16 [1024], P(('dp', 'mem')), may hold values from 0.5 to 1.5
- w_query: bfloat16 [1024, 1024], P(('dp', 'mem')), may hold values from -0.1875 to 0.1875
- w_key: bfloat16 [1024, 1024], P(('dp', 'mem')), may hold values from -0.1875 to 0.1875
- w_value: bfloat16 [1024, 1024], P(('dp', 'mem')), may hold values from -0.1875 to 0.1875
- w_out: bfloat16 [1024, 1024], P(('dp', 'mem')), may hold values from -3 to 3
- gain_ffn: bfloat16 [1024], P(('dp', 'mem')), may hold values from 0.5 to 1.5
- w_gate: bfloat16 [1024, 2816], P(('dp', 'mem')), may hold values from -0.1875 to 0.1875
- w_up: bfloat16 [1024, 2816], P(('dp', 'mem')), may hold values from -0.1875 to 0.1875
- w_down: bfloat16 [2816, 1024], P(('dp', 'mem')), may hold values from -0.109375 to 0.109375
- mem_keys: bfloat16 [16384, 1024], P(('dp', 'mem')), may hold values from -6 to 6
- mem_values: bfloat16 [16384, 1024], P(('dp', 'mem')), may hold values from -6 to 6
- out_grad: bfloat16 [4096, 1024], P(('dp', 'mem')), may hold values from -6 to 6
- key_mask: int32 [2, 8192], P('dp', 'mem'), may hold values 0 or 1
- mem_sizes: int32 [2, 4], P('dp'), may hold values from 1 to 4096, 8192 in all within a row
- seg_doc: int32 [2, 16], P('dp'), may hold values from 0 to 3, never falling along the last dimension, each value on 1 to 8 neighbouring positions
- seg_len: int32 [2, 16], P('dp', 'mem'), may hold values from 64 to 128
Outputs:
- output: bfloat16 [4096, 1024], P(('dp', 'mem'))
- input_grad: bfloat16 [4096, 1024], P(('dp', 'mem'))
- grad_gain_attn: float32 [1024], P(('dp', 'mem'))
- grad_query: float32 [1024, 1024], P(('dp', 'mem'))
- grad_key: float32 [1024, 1024], P(('dp', 'mem'))
- grad_value: float32 [1024, 1024], P(('dp', 'mem'))
- grad_out: float32 [1024, 1024], P(('dp', 'mem'))
- grad_gain_ffn: float32 [1024], P(('dp', 'mem'))
- grad_gate: float32 [1024, 2816], P(('dp', 'mem'))
- grad_up: float32 [1024, 2816], P(('dp', 'mem'))
- grad_down: float32 [2816, 1024], P(('dp', 'mem'))
The draws below stay inside these ranges and needn't reach their ends.
Inputs may be any that keep to these rules, and one draw needn't show every extreme that they name: `seg_doc`: a group's segments take documents in order; each document has 1 to 8 segments, one exactly that many. `mem_sizes`: a group's memory sizes add up to 8192; the largest is exactly 4096.
All inputs are finite; a program needn't handle non-finite values. No bound on the sum of `key_mask` on one device may be relied on, other than what follows from the above.
Results may differ from the reference program's by a relative error of at most 0.03.
Values may be sent and summed in bfloat16 or wider, within the bound.
A program may use at most 384 MiB of HBM per device.

```python
import math
import jax
import jax.numpy as jnp
import numpy as np
from jax import lax

D = 1024
HEADS = 8
HEAD_DIM = 128
FF = 2816
TOK_DEV = 128
TOKENS = 4096
MEM_KEYS = 8192
DOCS = 4
N_DP = 2
N_MEM = 16


def touch_ends(entries, own_key, low, high):
    longest = entries.shape.index(max(entries.shape))
    spots = []
    for shift in (0, 1):
        where = [jax.random.randint(jax.random.fold_in(own_key, axis), (), 0, length) for axis, length in enumerate(entries.shape)]
        where[longest] = (where[longest] + shift) % entries.shape[longest]
        spots.append(tuple(where))
    return entries.at[spots[0]].set(low).at[spots[1]].set(high)


def steps_of(key, extent, shards, least, top_value):
    factor_of = 1.0
    for dim, parts in shards:
        draws = jax.random.uniform(jax.random.fold_in(jax.random.fold_in(key, 6), dim), (parts,), jnp.float32, least / len(shards), top_value / len(shards))
        factor_of = factor_of * jnp.repeat(jnp.exp(draws), extent[dim] // parts).reshape((-1,) + (1,) * (len(extent) - 1 - dim))
    return factor_of


def length_profile(amount, total, most, lean):
    weights = [(1 << 20) // math.isqrt(standing ** lean) + 1 for standing in range(2, amount + 1)]
    rest, holding = total - most - (amount - 1), [1] * (amount - 1)
    while rest > 0:
        free = [i for i in range(amount - 1) if holding[i] < most]
        whole, left = sum([weights[i] for i in free]), rest
        for i in free:
            extra = min(most - holding[i], max(1, left * weights[i] // whole), rest)
            holding[i] = holding[i] + extra
            rest = rest - extra
    return np.array([most] + holding)


def ragged_sizes(key, amount, total, limit, slope):
    if amount == 2:
        one = jax.random.randint(key, (), max(1, total - limit), min(limit, total - 1) + 1)
        return jnp.stack([one, total - one])
    lengths = jnp.asarray(length_profile(amount, total, limit, slope), jnp.int32)
    couples = (amount - 1) // 2
    giver, receiver = lengths[1:1 + 2 * couples:2], lengths[2:2 + 2 * couples:2]
    margin = jnp.minimum(giver - 1, limit - receiver)
    moved = jax.random.randint(jax.random.fold_in(key, 1), (couples,), 0, 1 << 20) % (margin + 1)
    lengths = lengths.at[1:1 + 2 * couples:2].set(giver - moved).at[2:2 + 2 * couples:2].set(receiver + moved)
    return lengths[jax.random.permutation(jax.random.fold_in(key, 2), amount)]


def gaussian(stream_key, dims, scale, most, shards=(), held_as=jnp.bfloat16):
    loudness = steps_of(stream_key, dims, shards, -0.22, 0.18) if shards else 1.0
    array = jax.random.normal(stream_key, dims, jnp.float32) * scale * loudness
    return jnp.minimum(jnp.maximum(array, -most), most).astype(held_as)


def setup_inputs(seed: int = 0) -> dict:
    keys = jax.random.split(jax.random.key(seed), 18)
    return {
        "tokens": gaussian(keys[0], (TOKENS, D), 1.0, 6.0, ((0, 32),)),
        "gain_attn": jnp.clip(1.0 + 0.1 * jax.random.normal(keys[1], (D,), jnp.float32), 0.5, 1.5).astype(jnp.bfloat16),
        "w_query": gaussian(keys[2], (D, D), D ** -0.5, 0.1875, ((0, 32),)),
        "w_key": gaussian(keys[3], (D, D), D ** -0.5, 0.1875, ((0, 32),)),
        "w_value": gaussian(keys[4], (D, D), D ** -0.5, 0.1875, ((0, 32),)),
        "w_out": gaussian(keys[5], (D, D), (D // 256) ** -0.5, 3.0, ((0, 32),)),
        "gain_ffn": jnp.clip(1.0 + 0.1 * jax.random.normal(keys[6], (D,), jnp.float32), 0.5, 1.5).astype(jnp.bfloat16),
        "w_gate": gaussian(keys[7], (D, FF), D ** -0.5, 0.1875, ((0, 32),)),
        "w_up": gaussian(keys[8], (D, FF), D ** -0.5, 0.1875, ((0, 32),)),
        "w_down": gaussian(keys[9], (FF, D), FF ** -0.5, 0.109375, ((0, 32),)),
        "mem_keys": gaussian(keys[10], (N_DP * MEM_KEYS, D), 1.0, 6.0, ((0, 32),)),
        "mem_values": gaussian(keys[11], (N_DP * MEM_KEYS, D), 1.0, 6.0, ((0, 32),)),
        "out_grad": gaussian(keys[12], (TOKENS, D), 1.0, 6.0, ((0, 32),)),
        "key_mask": touch_ends((jax.random.randint(keys[13], (N_DP, MEM_KEYS), 0, 4) < 3).astype(jnp.int32), jax.random.fold_in(keys[13], 1), 0, 1),
        "mem_sizes": jax.vmap(lambda own: ragged_sizes(own, DOCS, MEM_KEYS, MEM_KEYS // 2, 2))(jax.random.split(keys[14], N_DP)).reshape((N_DP, DOCS)).astype(jnp.int32),
        "seg_doc": jax.vmap(lambda own: jnp.searchsorted(jnp.cumsum(ragged_sizes(own, DOCS, N_MEM, N_MEM // 2, 2)), jnp.arange(N_MEM), side="right"))(jax.random.split(keys[15], N_DP)).reshape((N_DP, N_MEM)).astype(jnp.int32),
        "seg_len": touch_ends(jax.random.randint(keys[16], (N_DP, N_MEM), TOK_DEV // 2, TOK_DEV + 1), jax.random.fold_in(keys[16], 1), TOK_DEV // 2, TOK_DEV).astype(jnp.int32),
    }


@jax.custom_vjp
def low(v):
    return lax.optimization_barrier(v.astype(jnp.bfloat16)).astype(jnp.float32)

@jax.custom_vjp
def low_back(v):
    return v

def low_keep(v):
    return (low(v), None)

def low_pass(kept, grad):
    return (grad,)

def back_keep(v):
    return (v, None)

def back_low(kept, grad):
    return (low(grad),)
low.defvjp(low_keep, low_pass)
low_back.defvjp(back_keep, back_low)
epsilon = 1e-05
neg_big = -1e+30
highest = lax.Precision.HIGHEST

def rms_norm(values, gain_row):
    return values * lax.rsqrt(lax.optimization_barrier(jnp.mean(values * values, axis=-1, keepdims=True)) + epsilon) * gain_row

def segment_attention(query_seg, key_seg, value_seg, seg_length, seg_docid, mem_heads, memval_heads, key_doc, key_live):
    row_count = query_seg.shape[0]
    query_heads = query_seg.reshape(row_count, HEADS, HEAD_DIM)
    key_heads = key_seg.reshape(row_count, HEADS, HEAD_DIM)
    value_heads = value_seg.reshape(row_count, HEADS, HEAD_DIM)
    factor = HEAD_DIM ** (-0.5)
    local_scores = jnp.einsum('ihd,jhd->hij', query_heads, key_heads, precision=highest) * factor
    memory_scores = jnp.einsum('ihd,khd->hik', query_heads, mem_heads, precision=highest) * factor
    scores = low_back(jnp.concatenate([local_scores, memory_scores], axis=2))
    positions = jnp.arange(row_count, dtype=jnp.int32)
    local_ok = (positions[None, :] <= positions[:, None]) & (positions[None, :] < seg_length)
    memory_ok = (key_doc == seg_docid) & key_live
    allowed = jnp.concatenate([local_ok, jnp.broadcast_to(memory_ok[None, :], (row_count, memory_ok.shape[0]))], axis=1)
    masked = jnp.where(allowed[None], scores, neg_big)
    largest = lax.optimization_barrier(jnp.max(masked, axis=2, keepdims=True))
    powers = jnp.where(allowed[None], jnp.exp(masked - largest), 0.0)
    probs = low(powers / lax.optimization_barrier(jnp.sum(powers, axis=2, keepdims=True)))
    all_values = jnp.concatenate([value_heads, memval_heads], axis=0)
    attended = jnp.einsum('hik,khd->ihd', probs, all_values, precision=highest)
    return attended.reshape(row_count, HEADS * HEAD_DIM)

def group_forward(group_x, weights, mem_heads, memval_heads, key_doc, key_live, docs_group, lengths_group):
    gain_one, query_w, key_w, value_w, out_w, gain_two, gate_w, up_w, down_w = weights
    normed = low(rms_norm(group_x, gain_one))
    queries = low_back(low(jnp.dot(normed, query_w, precision=highest)))
    keys_all = low_back(low(jnp.dot(normed, key_w, precision=highest)))
    values_all = low_back(low(jnp.dot(normed, value_w, precision=highest)))
    shape_seg = (N_MEM, TOK_DEV, D)

    def attend(packed):
        return segment_attention(packed[0], packed[1], packed[2], packed[3], packed[4], mem_heads, memval_heads, key_doc, key_live)
    attended = lax.map(jax.checkpoint(attend), (queries.reshape(shape_seg), keys_all.reshape(shape_seg), values_all.reshape(shape_seg), lengths_group, docs_group))
    attended = low_back(low(attended.reshape(N_MEM * TOK_DEV, D)))
    branch = low_back(jnp.dot(attended, out_w, precision=highest))
    first = group_x + branch
    normed_two = low(rms_norm(first, gain_two))
    gate = low_back(jnp.dot(normed_two, gate_w, precision=highest))
    upward = low_back(jnp.dot(normed_two, up_w, precision=highest))
    hidden = low(jax.nn.silu(gate) * upward)
    return first + jnp.dot(hidden, down_w, precision=highest)

def reference(tokens, gain_attn, w_query, w_key, w_value, w_out, gain_ffn, w_gate, w_up, w_down, mem_keys, mem_values, out_grad, key_mask, mem_sizes, seg_doc, seg_len):
    weights = tuple((member.astype(jnp.float32) for member in (gain_attn, w_query, w_key, w_value, w_out, gain_ffn, w_gate, w_up, w_down)))
    inputs_grouped = tokens.astype(jnp.float32).reshape(N_DP, N_MEM * TOK_DEV, D)
    cotangent = out_grad.astype(jnp.float32).reshape(N_DP, N_MEM * TOK_DEV, D)
    memory_k = mem_keys.astype(jnp.float32).reshape(N_DP, MEM_KEYS, HEADS, HEAD_DIM)
    memory_v = mem_values.astype(jnp.float32).reshape(N_DP, MEM_KEYS, HEADS, HEAD_DIM)
    places = jnp.arange(MEM_KEYS, dtype=jnp.int32)

    def group_step(totals, packed):
        group_x, group_cot, group_k, group_v, live_row, sizes_row, docs_row, lengths_row = packed
        ends = jnp.cumsum(sizes_row, dtype=jnp.int32)
        key_doc = lax.optimization_barrier(jnp.sum((places[:, None] >= ends[None, :]).astype(jnp.int32), axis=1, dtype=jnp.int32))

        def forward(x_value, w_value_tuple):
            return group_forward(x_value, w_value_tuple, group_k, group_v, key_doc, live_row == 1, docs_row, lengths_row)
        result, pullback = jax.vjp(forward, group_x, weights)
        grad_x, grad_w = pullback(group_cot)
        totals = jax.tree.map(lambda first, second: first + second, totals, grad_w)
        return (totals, (result.astype(jnp.bfloat16), grad_x.astype(jnp.bfloat16)))
    zeros = tuple((jnp.zeros_like(member) for member in weights))
    grads, (outputs, input_grads) = lax.scan(group_step, zeros, (inputs_grouped, cotangent, memory_k, memory_v, key_mask, mem_sizes, seg_doc, seg_len))
    return (outputs.reshape(TOKENS, D), input_grads.reshape(TOKENS, D), grads[0], grads[1], grads[2], grads[3], grads[4], grads[5], grads[6], grads[7], grads[8])
```

```python
import functools
import math

import jax
import jax.numpy as jnp
from jax import lax
from jax.experimental import pallas as pl
from jax.experimental.pallas import tpu as pltpu
from jax.sharding import PartitionSpec as P

HEADS = 8
WIDTH = 128
epsilon = 1e-05
neg_big = -1e30
LOG2E = 1.4426950408889634
VMEM_MAX = 67043328
MESH = pl.DeviceIdType.MESH
F32 = jnp.float32
BF16 = jnp.bfloat16

ANY = pl.BlockSpec(memory_space=pl.ANY)
VM = pl.BlockSpec(memory_space=pltpu.VMEM)
SM = pl.BlockSpec(memory_space=pltpu.SMEM)


def place():
    m = lax.axis_index("mem")
    return lax.axis_index("dp"), m // 4, (m // 2) % 2, m % 2


def device(y, z, x, c):
    return {"dp": y, "mem": z * 4 + x * 2 + c}


def flip_z(z, d):
    return (z, z + 1 - 2 * (z % 2), (z + 2) % 4, 3 - z)[d]


def greet(targets):
    barrier = pltpu.get_barrier_semaphore()
    for target in targets:
        pl.semaphore_signal(barrier, inc=1, device_id=target, device_id_type=MESH)
    pl.semaphore_wait(barrier, len(targets))


def remote(src, dst, send, recv, target):
    return pltpu.make_async_remote_copy(
        src_ref=src, dst_ref=dst, send_sem=send, recv_sem=recv, device_id=target, device_id_type=MESH
    )


FIRST = (False, True, True, False, True)


def gather_kernel(*refs):
    src = refs[:5]
    keys, vals, bias = refs[5:8]
    dst = refs[8:13]
    kh, vh, bh = refs[13:16]
    own_sem, rs, zs, ys, xs, cs, ko, kr, ks, kcs = refs[16:]
    y, z, x, c = place()
    m = z * 4 + x * 2 + c
    n = 5
    y_peer, x_peer, c_peer = device(1 - y, z, x, c), device(y, z, 1 - x, c), device(y, z, x, 1 - c)
    chip = z * 2 + x
    plane = []
    for dz in range(4):
        for dx in range(2):
            if dz or dx:
                plane.append((flip_z(z, dz), x if dx == 0 else 1 - x))
    greet([device(y, a, b, c) for a, b in plane] + [y_peer, c_peer])

    def shard(yy, zz, xx, cc):
        return yy * 16 + zz * 4 + xx * 2 + cc

    me = shard(y, z, x, c)
    pending = []

    def push(p, s, source, target, sem):
        copy = remote(source, dst[p].at[s], sem, rs.at[s, p], target)
        copy.start()
        pending.append(copy)

    def arrived(p, s):
        remote(dst[p].at[s], dst[p].at[s], own_sem.at[p], rs.at[s, p], c_peer).wait_recv()

    for d in (2, 3, 1):
        for p in range(n):
            push(p, me, src[p], device(y, flip_z(z, d), x, c), zs.at[d - 1, p])
    for p in range(n):
        push(p, me, src[p], y_peer, ys.at[0, p])
        push(p, me, src[p], x_peer, xs.at[0, p])
        push(p, me, src[p], c_peer, cs.at[0, p])
    locals_ = []
    for p in range(n):
        copy = pltpu.make_async_copy(src[p], dst[p].at[me], own_sem.at[p])
        copy.start()
        locals_.append(copy)

    for i, (zz, xx) in enumerate(plane):
        head = zz * 2 + xx
        lanes = pl.ds(pl.multiple_of(head * WIDTH, WIDTH), WIDTH)
        target = device(y, zz, xx, c)
        for p, (a, b) in enumerate(((keys.at[:, lanes], kh), (vals.at[:, lanes], vh), (bias, bh))):
            copy = remote(a, b.at[m], ks.at[i, p], kr.at[m, p], target)
            copy.start()
            pending.append(copy)
    mine = pl.ds(pl.multiple_of(chip * WIDTH, WIDTH), WIDTH)
    for p, (a, b) in enumerate(((keys.at[:, mine], kh), (vals.at[:, mine], vh), (bias, bh))):
        copy = pltpu.make_async_copy(a, b.at[m], ko.at[p])
        copy.start()
        locals_.append(copy)
        copy = remote(a, b.at[m], kcs.at[7, p], kr.at[m, p], c_peer)
        copy.start()
        pending.append(copy)

    hops = 1
    for d in (1, 2, 3):
        s = shard(y, flip_z(z, d), x, c)
        for p in range(n):
            arrived(p, s)
            push(p, s, dst[p].at[s], y_peer, ys.at[d, p])
            push(p, s, dst[p].at[s], x_peer, xs.at[d, p])
            push(p, s, dst[p].at[s], c_peer, cs.at[hops, p])
        hops += 1
    for d in range(4):
        zz = flip_z(z, d)
        s = shard(1 - y, zz, x, c)
        for p in range(n):
            arrived(p, s)
            if FIRST[p]:
                push(p, s, dst[p].at[s], x_peer, xs.at[4 + d, p])
            push(p, s, dst[p].at[s], c_peer, cs.at[hops, p])
        hops += 1
        s = shard(y, zz, 1 - x, c)
        for p in range(n):
            arrived(p, s)
            if not FIRST[p]:
                push(p, s, dst[p].at[s], y_peer, ys.at[4 + d, p])
            push(p, s, dst[p].at[s], c_peer, cs.at[hops, p])
        hops += 1
    for i, (zz, xx) in enumerate(plane):
        other = zz * 4 + xx * 2 + c
        for p, b in enumerate((kh, vh, bh)):
            remote(b.at[other], b.at[other], ko.at[p], kr.at[other, p], c_peer).wait_recv()
            copy = remote(b.at[other], b.at[other], kcs.at[i, p], kr.at[other, p], c_peer)
            copy.start()
            pending.append(copy)
    for d in range(4):
        s = shard(1 - y, flip_z(z, d), 1 - x, c)
        for p in range(n):
            arrived(p, s)
            push(p, s, dst[p].at[s], c_peer, cs.at[hops, p])
        hops += 1
    for yy in (y, 1 - y):
        for d in range(4):
            for xx in (x, 1 - x):
                for p in range(n):
                    arrived(p, shard(yy, flip_z(z, d), xx, 1 - c))
    for zz, xx in plane + [(z, x)]:
        other = zz * 4 + xx * 2 + 1 - c
        for p, b in enumerate((kh, vh, bh)):
            remote(b.at[other], b.at[other], ko.at[p], kr.at[other, p], c_peer).wait_recv()
    for copy in locals_:
        copy.wait()
    for copy in pending:
        copy.wait_send()


def gather_kernel_call(pieces, keys, values, bias):
    dma = pltpu.SemaphoreType.DMA
    rows = keys.shape[0]
    outs = [jax.ShapeDtypeStruct((32,) + a.shape, a.dtype) for a in pieces]
    outs += [jax.ShapeDtypeStruct((16, rows, WIDTH), BF16)] * 2
    outs += [jax.ShapeDtypeStruct((16,) + bias.shape, bias.dtype)]
    return pl.pallas_call(
        gather_kernel,
        out_shape=outs,
        in_specs=[VM] * 8,
        out_specs=[ANY] * 8,
        scratch_shapes=[
            dma((5,)),
            dma((32, 5)),
            dma((3, 5)),
            dma((8, 5)),
            dma((8, 5)),
            dma((16, 5)),
            dma((3,)),
            dma((16, 3)),
            dma((7, 3)),
            dma((8, 3)),
        ],
        compiler_params=pltpu.CompilerParams(
            collective_id=0, has_side_effects=True, vmem_limit_bytes=32 << 20
        ),
        name="gather",
    )(*pieces, keys, values, bias)


def swap_kernel(kinds, ranks, *refs):
    n = len(kinds)
    srcs, dsts, (own, send, recv) = refs[:n], refs[n : 2 * n], refs[2 * n :]
    m = lax.axis_index("mem")
    y = lax.axis_index("dp")
    count = lax.axis_size("mem") // ranks
    rank, me = m % ranks, m // ranks

    def at(kind, ref, i, outside):
        wide = (kind == "heads") == outside
        if wide and len(ref.shape) == 2:
            return ref.at[:, pl.ds(pl.multiple_of(i * WIDTH, WIDTH), WIDTH)]
        return ref.at[i]

    others = [(me + d) % count for d in range(1, count)]
    targets = [{"dp": y, "mem": o * ranks + rank} for o in others]
    greet(targets)
    copies = []
    for d, (o, target) in enumerate(zip(others, targets)):
        for p, kind in enumerate(kinds):
            copy = remote(
                at(kind, srcs[p], o, True), at(kind, dsts[p], me, False), send.at[d, p], recv.at[me, p], target
            )
            copy.start()
            copies.append(copy)
    mine = []
    for p, kind in enumerate(kinds):
        copy = pltpu.make_async_copy(at(kind, srcs[p], me, True), at(kind, dsts[p], me, False), own.at[p])
        copy.start()
        mine.append(copy)
    for o, target in zip(others, targets):
        for p, kind in enumerate(kinds):
            view = at(kind, dsts[p], o, False)
            remote(view, view, own.at[p], recv.at[o, p], target).wait_recv()
    for copy in mine:
        copy.wait()
    for copy in copies:
        copy.wait_send()


def swap(kinds, arrays, outs, ranks, ident):
    dma = pltpu.SemaphoreType.DMA
    count = lax.axis_size("mem") // ranks
    n = len(kinds)
    return pl.pallas_call(
        functools.partial(swap_kernel, kinds, ranks),
        out_shape=outs,
        in_specs=[VM] * n,
        out_specs=[VM] * n,
        scratch_shapes=[dma((n,)), dma((count - 1, n)), dma((count, n))],
        compiler_params=pltpu.CompilerParams(
            collective_id=ident, has_side_effects=True, vmem_limit_bytes=16 << 20
        ),
        name=f"swap{ident}",
    )(*arrays)


def key_span(j, ranks, docs, sizes, rank_ref):
    doc = docs[0, j * ranks + rank_ref[0]]
    start = jnp.int32(0)
    stop = jnp.int32(0)
    for i in range(sizes.shape[1]):
        size = sizes[0, i]
        start = start + jnp.where(i < doc, size, 0)
        stop = stop + jnp.where(i <= doc, size, 0)
    return start, stop


def block_bias(bias_ref, b, per, block, start, stop):
    width = bias_ref.shape[2]
    rows = []
    for i in range(per):
        spots = b * block + i * width + lax.broadcasted_iota(jnp.int32, (8, width), 1)
        inside = (spots >= start) & (spots < stop)
        rows.append(jnp.where(inside, bias_ref[b * per + i], neg_big))
    return jnp.concatenate(rows, axis=1)[0:1] if per > 1 else rows[0][0:1]


def forward_kernel(ranks, block, docs, sizes, rank_ref, q_ref, k_ref, v_ref, bias_ref, o_ref, lse_ref):
    j = pl.program_id(0)
    per = block // bias_ref.shape[2]
    start, stop = key_span(j, ranks, docs, sizes, rank_ref)
    q = q_ref[0]
    factor = WIDTH ** (-0.5) * LOG2E

    def step(b, carry):
        top, total, acc = carry
        rows = pl.ds(pl.multiple_of(b * block, block), block)
        s = lax.dot_general(q, k_ref[rows, :], (((1,), (1,)), ((), ())), preferred_element_type=F32)
        s = s * factor + block_bias(bias_ref, b, per, block, start, stop)
        best = jnp.maximum(top, jnp.max(s, axis=1, keepdims=True))
        p = jnp.exp2(s - best)
        keep = jnp.exp2(top - best)
        total = total * keep + jnp.sum(p, axis=1, keepdims=True)
        acc = acc * keep + jnp.dot(p.astype(BF16), v_ref[rows, :], preferred_element_type=F32)
        return best, total, acc

    rows = q.shape[0]
    top, total, acc = lax.fori_loop(
        start // block,
        (stop + block - 1) // block,
        step,
        (jnp.full((rows, 1), neg_big, F32), jnp.zeros((rows, 1), F32), jnp.zeros((rows, WIDTH), F32)),
    )
    o_ref[0] = (acc / total).astype(BF16)
    lse = jnp.broadcast_to(top + jnp.log2(total), (rows, rows))
    lse_ref[0] = lse.T[0:8]


def backward_kernel(
    ranks, block, docs, sizes, rank_ref, q_ref, do_ref, stat_ref, k_ref, v_ref, bias_ref, dq_ref
):
    j = pl.program_id(0)
    per = block // bias_ref.shape[2]
    start, stop = key_span(j, ranks, docs, sizes, rank_ref)
    q, do = q_ref[0], do_ref[0]
    rows = q.shape[0]
    factor = WIDTH ** (-0.5) * LOG2E
    stat = stat_ref[0]
    lse = jnp.broadcast_to(stat[0:1], (rows, rows)).T[:, 0:1]
    delta = jnp.broadcast_to(stat[1:2], (rows, rows)).T[:, 0:1]

    def step(b, acc):
        span = pl.ds(pl.multiple_of(b * block, block), block)
        keys = k_ref[span, :]
        s = lax.dot_general(q, keys, (((1,), (1,)), ((), ())), preferred_element_type=F32)
        p = jnp.exp2(s * factor + (block_bias(bias_ref, b, per, block, start, stop) - lse))
        dp = lax.dot_general(do, v_ref[span, :], (((1,), (1,)), ((), ())), preferred_element_type=F32)
        ds = (p * (dp - delta)).astype(BF16)
        return acc + jnp.dot(ds, keys, preferred_element_type=F32)

    acc = lax.fori_loop(
        start // block, (stop + block - 1) // block, step, jnp.zeros((rows, WIDTH), F32)
    )
    dq_ref[0] = (acc * WIDTH ** (-0.5)).astype(BF16)


def memory_forward(ranks, docs, sizes, rank, q, kh, vh, bh):
    count, rows, _ = q.shape
    seg = pl.BlockSpec((1, rows, WIDTH), lambda j: (j, 0, 0))
    stat = pl.BlockSpec((1, 8, rows), lambda j: (j, 0, 0))
    block = 2 * bh.shape[2]
    return pl.pallas_call(
        functools.partial(forward_kernel, ranks, block),
        grid=(count,),
        out_shape=[
            jax.ShapeDtypeStruct((count, rows, WIDTH), BF16),
            jax.ShapeDtypeStruct((count, 8, rows), F32),
        ],
        in_specs=[SM, SM, SM, seg, VM, VM, VM],
        out_specs=[seg, stat],
        compiler_params=pltpu.CompilerParams(vmem_limit_bytes=48 << 20),
        name="memory_forward",
    )(docs, sizes, rank, q, kh, vh, bh)


def memory_backward(ranks, docs, sizes, rank, q, do, stats, kh, vh, bh):
    count, rows, _ = q.shape
    seg = pl.BlockSpec((1, rows, WIDTH), lambda j: (j, 0, 0))
    stat = pl.BlockSpec((1, 8, rows), lambda j: (j, 0, 0))
    block = 2 * bh.shape[2]
    return pl.pallas_call(
        functools.partial(backward_kernel, ranks, block),
        grid=(count,),
        out_shape=jax.ShapeDtypeStruct((count, rows, WIDTH), BF16),
        in_specs=[SM, SM, SM, seg, seg, stat, VM, VM, VM],
        out_specs=seg,
        compiler_params=pltpu.CompilerParams(vmem_limit_bytes=48 << 20),
        name="memory_backward",
    )(docs, sizes, rank, q, do, stats, kh, vh, bh)


def reduce_kernel(*refs):
    h, dqkv, o, da, h2, dgu, hid, og, small = refs[:9]
    outs = refs[9:14]
    grads = refs[14:19]
    cores = refs[19:24]
    firsts = refs[24:29]
    seconds = refs[29:34]
    lines = refs[34:39]
    ht, ot, h2t, hidt = refs[39:43]
    cs, cr, fs, fr, ss, sr, zs, zr = refs[43:]
    n = 5
    y, z, x, c = place()
    y_peer, x_peer, c_peer = device(1 - y, z, x, c), device(y, z, 1 - x, c), device(y, z, x, 1 - c)
    greet([y_peer, x_peer, c_peer] + [device(y, flip_z(z, d), x, c) for d in (1, 2, 3)])
    ht[...] = h[...].T
    ot[...] = o[...].T
    h2t[...] = h2[...].T
    hidt[...] = hid[...].T
    pending = []

    def start(copy):
        copy.start()
        pending.append(copy)

    left = (ht, ot, h2t, hidt)
    right = (dqkv, da, dgu, og)
    order = [(k, d) for d in (3, 2, 1, 0) for k in (1, 0)]

    def unit(k, d):
        return (1 - y if k else y), flip_z(z, d)

    def produce(i):
        k, d = order[i]
        yy, zz = unit(k, d)
        u = yy * 4 + zz
        for p in range(4):
            rows = 4 * grads[p].shape[2]
            block = left[p][pl.ds(pl.multiple_of(u * rows, 32), rows), :]
            width = grads[p].shape[3]
            tile = 1024 if width % 1024 == 0 else 1408
            for t in range(0, width, tile):
                part = jnp.dot(block, right[p][:, t : t + tile], preferred_element_type=F32)
                grads[p][i, :, :, t : t + tile] = part.astype(BF16).reshape(4, rows // 4, tile)
        for q in range(4):
            grads[4][i, q] = small[u * 4 + q]
        for p in range(n):
            for xx in range(2):
                start(remote(grads[p].at[i, xx * 2 + 1 - c], cores[p].at[i, xx], cs.at[i, xx, p], cr.at[i, xx, p], c_peer))

    def wait(dst, sem):
        remote(dst, dst, cs.at[0, 0, 0], sem, c_peer).wait_recv()

    def merge(own, other):
        own[...] = (own[...].astype(F32) + other[...].astype(F32)).astype(own.dtype)

    def after_core(i):
        k, d = order[i]
        for p in range(n):
            for xx in (1 - x, x):
                own = grads[p].at[i, xx * 2 + c]
                wait(cores[p].at[i, xx], cr.at[i, xx, p])
                merge(own, cores[p].at[i, xx])
            if FIRST_BACK[p] == "x":
                start(remote(grads[p].at[i, (1 - x) * 2 + c], firsts[p].at[i], fs.at[i, 0, p], fr.at[i, 0, p], x_peer))
            elif k == 1:
                for xx in range(2):
                    start(remote(grads[p].at[i, xx * 2 + c], firsts[p].at[(i + 1) // 2 * 2 // 2 + 4 * xx], fs.at[i, xx, p], fr.at[i // 2, xx, p], y_peer))

    def after_first(i):
        k, d = order[i]
        for p in range(n):
            own = grads[p].at[i, x * 2 + c]
            if FIRST_BACK[p] == "x":
                wait(firsts[p].at[i], fr.at[i, 0, p])
                merge(own, firsts[p].at[i])
                if k == 1:
                    start(remote(own, seconds[p].at[i // 2], ss.at[i // 2, p], sr.at[i // 2, p], y_peer))
            elif k == 0:
                for xx in range(2):
                    wait(firsts[p].at[i // 2 + 4 * xx], fr.at[i // 2, xx, p])
                    merge(grads[p].at[i, xx * 2 + c], firsts[p].at[i // 2 + 4 * xx])
                start(remote(grads[p].at[i, (1 - x) * 2 + c], seconds[p].at[i // 2], ss.at[i // 2, p], sr.at[i // 2, p], x_peer))

    def after_second(i):
        k, d = order[i]
        if k == 1:
            return
        for p in range(n):
            own = grads[p].at[i, x * 2 + c]
            wait(seconds[p].at[i // 2], sr.at[i // 2, p])
            merge(own, seconds[p].at[i // 2])
            if d:
                start(remote(own, lines[p].at[d - 1], zs.at[d - 1, p], zr.at[d - 1, p], device(y, flip_z(z, d), x, c)))

    for t in range(8 + 6):
        if t < 8:
            produce(t)
        if 0 <= t - 1 < 8:
            after_core(t - 1)
        if 0 <= t - 3 < 8:
            after_first(t - 3)
        if 0 <= t - 5 < 8:
            after_second(t - 5)
    for p in range(n):
        total = grads[p][7, x * 2 + c].astype(F32)
        for d in (1, 2, 3):
            wait(lines[p].at[d - 1], zr.at[d - 1, p])
            total = total + lines[p][d - 1].astype(F32)
        outs[p][...] = total
    for copy in pending:
        copy.wait_send()


FIRST_BACK = ("y", "y", "x", "y", "x")


def reduce_call(h, dqkv, o, da, h2, dgu, hid, og, small):
    dma = pltpu.SemaphoreType.DMA
    rows, width = h.shape
    down = hid.shape[1] // 32
    own = width // 32
    shapes = [
        ((own, dqkv.shape[1]), BF16),
        ((own, da.shape[1]), BF16),
        ((own, dgu.shape[1]), BF16),
        ((down, og.shape[1]), BF16),
        (small.shape[1:], F32),
    ]

    def buffers(lead):
        return [
            pltpu.VMEM((lead(p) if isinstance(lead(p), tuple) else (lead(p),)) + s, t)
            for p, (s, t) in enumerate(shapes)
        ]

    return pl.pallas_call(
        reduce_kernel,
        out_shape=[jax.ShapeDtypeStruct(s, F32) for s, _ in shapes],
        in_specs=[VM] * 9,
        out_specs=[VM] * 5,
        scratch_shapes=buffers(lambda p: (8, 4))
        + buffers(lambda p: (8, 2))
        + buffers(lambda p: 8)
        + buffers(lambda p: 4)
        + buffers(lambda p: 3)
        + [
            pltpu.VMEM((width, rows), BF16),
            pltpu.VMEM((width, rows), BF16),
            pltpu.VMEM((width, rows), BF16),
            pltpu.VMEM((hid.shape[1], rows), BF16),
            dma((8, 2, 5)),
            dma((8, 2, 5)),
            dma((8, 2, 5)),
            dma((8, 2, 5)),
            dma((4, 5)),
            dma((4, 5)),
            dma((3, 5)),
            dma((3, 5)),
        ],
        compiler_params=pltpu.CompilerParams(
            collective_id=5, has_side_effects=True, vmem_limit_bytes=VMEM_MAX
        ),
        name="reduce",
    )(h, dqkv, o, da, h2, dgu, hid, og, small)


def gather_plain(pieces, keys, values, bias, ranks):
    full = [lax.all_gather(a, ("dp", "mem"), axis=0, tiled=False) for a in pieces]

    def spread(a):
        blocks = a.reshape(a.shape[0], HEADS, WIDTH).transpose(1, 0, 2)
        return lax.all_to_all(jnp.repeat(blocks, ranks, axis=0), "mem", 0, 0, tiled=True)

    return full + [spread(keys), spread(values), lax.all_gather(bias, "mem", axis=0, tiled=False)]


def to_heads_plain(x, ranks):
    rank = lax.axis_index("mem") % ranks
    blocks = x if x.ndim == 3 else x.reshape(x.shape[0], HEADS, WIDTH).transpose(1, 0, 2)
    wide = jnp.where((jnp.arange(ranks) == rank)[None, :, None, None], blocks[:, None], 0)
    wide = wide.reshape((-1,) + blocks.shape[1:])
    got = lax.all_to_all(wide, "mem", 0, 0, tiled=True)
    return lax.dynamic_index_in_dim(got.reshape((-1, ranks) + blocks.shape[1:]), rank, 1, keepdims=False)


def to_tokens_plain(x, ranks, wide_out):
    rank = lax.axis_index("mem") % ranks
    wide = jnp.where((jnp.arange(ranks) == rank)[None, :, None, None], x[:, None], 0)
    got = lax.all_to_all(wide.reshape((-1,) + x.shape[1:]), "mem", 0, 0, tiled=True)
    got = lax.dynamic_index_in_dim(got.reshape((-1, ranks) + x.shape[1:]), rank, 1, keepdims=False)
    return got.transpose(1, 0, 2).reshape(x.shape[1], -1) if wide_out else got


def reduce_plain(h, dqkv, o, da, h2, dgu, hid, og, small):
    outs = []
    for a, b in ((h, dqkv), (o, da), (h2, dgu), (hid, og)):
        full = jnp.dot(a.T, b, preferred_element_type=F32)
        outs.append(lax.psum_scatter(full, ("dp", "mem"), scatter_dimension=0, tiled=True))
    outs.append(lax.psum_scatter(small, ("dp", "mem"), scatter_dimension=0, tiled=False))
    return outs


def normalize(values):
    inverse = lax.rsqrt(jnp.mean(values * values, axis=-1, keepdims=True) + epsilon)
    return (values * inverse, inverse)


def norm_back(grad_scaled, normed, inverse, gain_full):
    gain_grad = jnp.sum(grad_scaled * normed, axis=0)
    grad_normed = grad_scaled * gain_full
    grad_values = inverse * (
        grad_normed - normed * jnp.mean(grad_normed * normed, axis=-1, keepdims=True)
    )
    return (gain_grad, grad_values)


def shards(
    tokens,
    gain_attn,
    w_query,
    w_key,
    w_value,
    w_out,
    gain_ffn,
    w_gate,
    w_up,
    w_down,
    mem_keys,
    mem_values,
    out_grad,
    key_mask,
    mem_sizes,
    seg_doc,
    seg_len,
):
    seg_rows, model_width = tokens.shape
    mem_count = lax.axis_size("mem")
    dp_count = lax.axis_size("dp")
    devices = mem_count * dp_count
    ranks = mem_count // HEADS
    direct = dp_count == 2 and mem_count == 16
    factor = WIDTH ** (-0.5)
    ff_width = w_gate.shape[1]
    own = gain_attn.shape[0]
    down_rows = w_down.shape[0]

    pieces = [
        jnp.concatenate([w_query, w_key, w_value], axis=1),
        w_out,
        jnp.concatenate([w_gate, w_up], axis=1),
        w_down,
        jnp.pad(jnp.stack([gain_attn, gain_ffn]), ((0, 14), (0, 128 - own))),
    ]
    bias = jnp.broadcast_to(jnp.where(key_mask == 1, 0.0, neg_big).astype(F32), (8, key_mask.shape[1]))
    if direct:
        gathered = gather_kernel_call(pieces, mem_keys, mem_values, bias)
    else:
        gathered = gather_plain(pieces, mem_keys, mem_values, bias, ranks)
    joined_w, out_full, gate_up, down_full, gains, kh, vh, bh = gathered
    joined_w = joined_w.reshape(model_width, -1)
    out_full = out_full.reshape(model_width, -1)
    gate_up = gate_up.reshape(model_width, -1)
    down_full = down_full.reshape(ff_width, -1)
    kh = kh.reshape(-1, WIDTH)
    vh = vh.reshape(-1, WIDTH)
    gain_one = gains[:, 0, :own].reshape(-1).astype(F32)
    gain_two = gains[:, 1, :own].reshape(-1).astype(F32)
    rank = (lax.axis_index("mem") % ranks).reshape(1).astype(jnp.int32)

    inputs = tokens.astype(F32)
    normed_one, inverse_one = normalize(inputs)
    normed_low = (normed_one * gain_one).astype(BF16)
    projected = jnp.dot(normed_low, joined_w, preferred_element_type=F32).astype(BF16)
    queries = projected[:, :model_width]
    keys_local = projected[:, model_width : 2 * model_width]
    values_local = projected[:, 2 * model_width :]

    seg_count = mem_count // ranks
    block_shape = jax.ShapeDtypeStruct((seg_count, seg_rows, WIDTH), BF16)
    stat_shape = jax.ShapeDtypeStruct((seg_count, 8, seg_rows), F32)
    wide_shape = jax.ShapeDtypeStruct((seg_rows, model_width), BF16)

    if direct:
        (q_heads,) = swap(("heads",), (queries,), (block_shape,), ranks, 1)
    else:
        q_heads = to_heads_plain(queries, ranks)
    o_mem, lse_mem = memory_forward(ranks, seg_doc, mem_sizes, rank, q_heads, kh, vh, bh)
    if direct:
        mem_o, mem_lse = swap(("tokens", "tokens"), (o_mem, lse_mem), (wide_shape, stat_shape), ranks, 2)
    else:
        mem_o = to_tokens_plain(o_mem, ranks, True)
        mem_lse = to_tokens_plain(lse_mem, ranks, False)
    mem_o = mem_o.reshape(seg_rows, HEADS, WIDTH).astype(F32)
    mem_lse = mem_lse[:, 0, :] / LOG2E

    query_heads = queries.reshape(seg_rows, HEADS, WIDTH)
    key_heads = keys_local.reshape(seg_rows, HEADS, WIDTH)
    value_heads = values_local.reshape(seg_rows, HEADS, WIDTH)
    positions = lax.iota(jnp.int32, seg_rows)
    local_ok = ((positions[None, :] <= positions[:, None]) & (positions[None, :] < seg_len[0, 0]))[
        None
    ]
    local_scores = (
        jnp.einsum("ihd,jhd->hij", query_heads, key_heads, preferred_element_type=F32) * factor
    )
    local_masked = jnp.where(local_ok, local_scores, neg_big)
    local_top = jnp.max(local_masked, axis=2)
    local_total = jnp.sum(jnp.where(local_ok, jnp.exp(local_masked - local_top[:, :, None]), 0.0), axis=2)
    local_lse = local_top + jnp.log(local_total)
    best = jnp.maximum(local_lse, mem_lse)
    log_total = best + jnp.log(jnp.exp(local_lse - best) + jnp.exp(mem_lse - best))
    local_probs = jnp.where(local_ok, jnp.exp(local_masked - log_total[:, :, None]), 0.0)
    local_low = local_probs.astype(BF16)
    attended = (
        jnp.einsum("hij,jhd->ihd", local_low, value_heads, preferred_element_type=F32)
        + mem_o * jnp.exp(mem_lse - log_total).T[..., None]
    )
    attended_low = attended.reshape(seg_rows, model_width).astype(BF16)
    first = inputs + jnp.dot(attended_low, out_full, preferred_element_type=F32)

    normed_two, inverse_two = normalize(first)
    normed_two_low = (normed_two * gain_two).astype(BF16)
    gate_upward = jnp.dot(normed_two_low, gate_up, preferred_element_type=F32)
    gate, upward = gate_upward[:, :ff_width], gate_upward[:, ff_width:]
    sigmoid_gate = jax.nn.sigmoid(gate)
    activated = gate * sigmoid_gate
    hidden = (activated * upward).astype(BF16)
    output = (first + jnp.dot(hidden, down_full, preferred_element_type=F32)).astype(BF16)
    grad_hidden = jnp.dot(out_grad, down_full.T, preferred_element_type=F32)
    grad_gate_up = jnp.concatenate(
        [
            (grad_hidden * upward * sigmoid_gate * (1.0 + gate * (1.0 - sigmoid_gate))).astype(BF16),
            (grad_hidden * activated).astype(BF16),
        ],
        axis=1,
    )
    grad_normed_two = jnp.dot(grad_gate_up, gate_up.T, preferred_element_type=F32)
    grad_gain_two, grad_first_norm = norm_back(grad_normed_two, normed_two, inverse_two, gain_two)
    grad_first = out_grad.astype(F32) + grad_first_norm

    grad_branch = grad_first.astype(BF16)
    grad_attended = jnp.dot(grad_branch, out_full.T, preferred_element_type=F32).astype(BF16)
    grad_att_heads = grad_attended.reshape(seg_rows, HEADS, WIDTH)
    delta = jnp.sum(grad_att_heads.astype(F32) * attended, axis=-1).T
    stats = jnp.pad(jnp.stack([log_total * LOG2E, delta], axis=1), ((0, 0), (0, 6), (0, 0)))
    if direct:
        do_heads, stat_heads = swap(
            ("heads", "heads"), (grad_attended, stats), (block_shape, stat_shape), ranks, 3
        )
    else:
        do_heads = to_heads_plain(grad_attended, ranks)
        stat_heads = to_heads_plain(stats, ranks)
    dq_heads = memory_backward(
        ranks, seg_doc, mem_sizes, rank, q_heads, do_heads, stat_heads, kh, vh, bh
    )
    if direct:
        (grad_query_memory,) = swap(("tokens",), (dq_heads,), (wide_shape,), ranks, 4)
    else:
        grad_query_memory = to_tokens_plain(dq_heads, ranks, True)

    grad_value_heads = jnp.einsum(
        "hij,ihd->jhd", local_low, grad_att_heads, preferred_element_type=F32
    )
    grad_local_probs = jnp.einsum(
        "ihd,jhd->hij", grad_att_heads, value_heads, preferred_element_type=F32
    )
    grad_local_scores = (local_probs * (grad_local_probs - delta[:, :, None])).astype(BF16)
    grad_query_heads = (
        jnp.einsum("hij,jhd->ihd", grad_local_scores, key_heads, preferred_element_type=F32)
        * factor
    )
    grad_key_heads = (
        jnp.einsum("hij,ihd->jhd", grad_local_scores, query_heads, preferred_element_type=F32)
        * factor
    )
    grad_queries = grad_query_heads.reshape(seg_rows, model_width) + grad_query_memory.astype(F32)
    grad_joined = jnp.concatenate(
        [
            grad_queries,
            grad_key_heads.reshape(seg_rows, model_width),
            grad_value_heads.reshape(seg_rows, model_width),
        ],
        axis=1,
    ).astype(BF16)
    grad_normed_one = jnp.dot(grad_joined, joined_w.T, preferred_element_type=F32)
    grad_gain_one, grad_input_norm = norm_back(grad_normed_one, normed_one, inverse_one, gain_one)
    input_grad = (grad_first + grad_input_norm).astype(BF16)

    small = jnp.stack([grad_gain_one.reshape(devices, own), grad_gain_two.reshape(devices, own)], axis=1)
    small = jnp.pad(small, ((0, 0), (0, 6), (0, 128 - own)))
    reducer = reduce_call if direct else reduce_plain
    attn_sums, out_sums, ffn_sums, down_sums, small_sums = reducer(
        normed_low, grad_joined, attended_low, grad_branch, normed_two_low, grad_gate_up, hidden, out_grad, small
    )
    return (
        output,
        input_grad,
        small_sums[0, :own],
        attn_sums[:, :model_width],
        attn_sums[:, model_width : 2 * model_width],
        attn_sums[:, 2 * model_width : 3 * model_width],
        out_sums,
        small_sums[1, :own],
        ffn_sums[:, :ff_width],
        ffn_sums[:, ff_width:],
        down_sums,
    )


def solution(mesh):
    rows = P(("dp", "mem"), None)
    vector = P(("dp", "mem"))
    in_specs = (
        (rows, vector) + (rows,) * 4 + (vector,) + (rows,) * 6
        + (P("dp", "mem"), P("dp", None), P("dp", None), P("dp", "mem"))
    )
    out_specs = (rows, rows, vector) + (rows,) * 4 + (vector,) + (rows,) * 3
    return jax.shard_map(shards, mesh=mesh, in_specs=in_specs, out_specs=out_specs, check_vma=False)
```

```python
import functools
import math

import jax
import jax.numpy as jnp
from jax import lax
from jax.experimental import pallas as pl
from jax.experimental.pallas import tpu as pltpu
from jax.sharding import PartitionSpec as P

HEADS = 8
WIDTH = 128
KEYS = 128
epsilon = 1e-05
neg_big = -1e30
LOG2E = 1.4426950408889634
VMEM_MAX = 67043328
MESH = pl.DeviceIdType.MESH
F32 = jnp.float32
BF16 = jnp.bfloat16

ANY = pl.BlockSpec(memory_space=pl.ANY)
VM = pl.BlockSpec(memory_space=pltpu.VMEM)
SM = pl.BlockSpec(memory_space=pltpu.SMEM)


def place():
    m = lax.axis_index("mem")
    return lax.axis_index("dp"), m // 4, (m // 2) % 2, m % 2


def device(y, z, x, c):
    return {"dp": y, "mem": z * 4 + x * 2 + c}


def flip_z(z, d):
    return (z, z + 1 - 2 * (z % 2), (z + 2) % 4, 3 - z)[d]


def greet(targets):
    barrier = pltpu.get_barrier_semaphore()
    for target in targets:
        pl.semaphore_signal(barrier, inc=1, device_id=target, device_id_type=MESH)
    pl.semaphore_wait(barrier, len(targets))


def remote(src, dst, send, recv, target):
    return pltpu.make_async_remote_copy(
        src_ref=src, dst_ref=dst, send_sem=send, recv_sem=recv, device_id=target, device_id_type=MESH
    )


Y_FIRST = (False, True, False, True, False)
EARLY, LATE = (0, 4), (1, 2, 3)


def line_of(z):
    inner = ((z + 1) // 2) % 2
    near = flip_z(z, 1)
    second = 3 - (inner * z + (1 - inner) * near)
    third = 3 - (inner * near + (1 - inner) * z)
    return inner, (z, near, second, third)


def expand(packed, first, count):
    rows, lanes = packed.shape
    width = rows // 16 * count
    lane = lax.broadcasted_iota(jnp.int32, (lanes, width), 0)
    column = lax.broadcasted_iota(jnp.int32, (lanes, width), 1)
    pick = (lane == first + column % count).astype(BF16)
    wide = jnp.dot(packed, pick, preferred_element_type=F32)
    shard = lax.broadcasted_iota(jnp.int32, (rows, width), 0) // 16
    column = lax.broadcasted_iota(jnp.int32, (rows, width), 1) // count
    return jnp.sum(jnp.where(shard == column, wide, 0.0), axis=0, keepdims=True)


def rows_of(ref, block, count):
    return jnp.concatenate([ref[block + i] for i in range(count)], axis=0)


def window_bias(ref, block, count, start, stop):
    size = ref.shape[2]
    parts = []
    for i in range(count):
        spots = (block + i) * size + lax.broadcasted_iota(jnp.int32, (8, size), 1)
        inside = (spots >= start) & (spots < stop)
        parts.append(jnp.where(inside, ref[block + i], neg_big))
    return jnp.concatenate(parts, axis=1)[0:1]


def key_window(j, ranks, rank, docs, sizes, blocks):
    window = blocks // 2 + 1
    doc = docs[0, j * ranks + rank]
    start = 0
    stop = 0
    for i in range(sizes.shape[1]):
        size = sizes[0, i]
        start = start + size * (i < doc).astype(jnp.int32)
        stop = stop + size * (i <= doc).astype(jnp.int32)
    base = lax.min(lax.div(start, jnp.int32(KEYS)), jnp.int32(blocks - window))
    return start, stop, base, window


def columns(block):
    rows = block.shape[1]
    return jnp.concatenate([block, jnp.zeros((rows - 8, rows), F32)], axis=0).T


def front_kernel(own_rows, *refs):
    docs, sizes, lens = refs[:3]
    x_ref = refs[3]
    src = refs[4:9]
    keys, vals, bias = refs[9:12]
    first_out, o_low, att, tot, h_ref, q_ref, k_ref, v_ref, qh, gain_out = refs[12:22]
    dst = refs[22:27]
    kh, vh, bh = refs[27:30]
    oh, lh, mo, ml, loc, st = refs[30:36]
    own_sem, rs, zs, ys, xs, cs, ko, kr, ks, kcs, qs, qr, os_, or_ = refs[36:]
    y, z, x, c = place()
    m = z * 4 + x * 2 + c
    ranks = 2
    chip = z * 2 + x
    rows = x_ref.shape[0]
    width = x_ref.shape[1]
    total = kh.shape[0]
    per = keys.shape[0]
    factor = WIDTH ** (-0.5) * LOG2E
    inner, line = line_of(z)
    y_peer, x_peer, c_peer = device(1 - y, z, x, c), device(y, z, 1 - x, c), device(y, z, x, 1 - c)
    near, across = device(y, flip_z(z, 1), x, c), device(y, 3 - z, x, c)
    plane = [
        (flip_z(z, dz), x if dx == 0 else 1 - x) for dz in (3, 2, 1, 0) for dx in (1, 0) if dz or dx
    ]
    pending = []
    inner_pending = []

    def shard(yy, zz, xx, cc):
        return yy * 16 + zz * 4 + xx * 2 + cc

    def slot(p, s):
        return dst[p].at[s]

    me = shard(y, z, x, c)

    def go(copy):
        copy.start()
        pending.append(copy)

    def push(p, s, target, sem, source=None):
        go(remote(slot(p, s) if source is None else source, slot(p, s), sem, rs.at[s, p], target))

    def push_inner(jobs):
        copies = [
            remote(slot(p, s) if source is None else source, slot(p, s), sem, rs.at[s, p], target)
            for p, s, target, sem, source in jobs
        ]
        inner_pending.extend(copies)

        @pl.when(inner == 1)
        def _():
            for copy in copies:
                copy.start()

    def arrived(p, s):
        remote(slot(p, s), slot(p, s), own_sem.at[p], rs.at[s, p], c_peer).wait_recv()

    def own_sends(group):
        push_inner([(p, me, across, zs.at[0, p], src[p]) for p in group])
        for p in group:
            push(p, me, near, zs.at[1, p], src[p])
        for p in group:
            push(p, me, y_peer, ys.at[0, p], src[p])
            push(p, me, x_peer, xs.at[0, p], src[p])
            push(p, me, c_peer, cs.at[0, p], src[p])

    def line_event(i, group):
        s = shard(y, line[i], x, c)
        for p in group:
            arrived(p, s)
        if i == 1:
            push_inner([(p, s, across, zs.at[2, p], None) for p in group])
        else:
            push_inner([(p, s, near, zs.at[i + 1, p], None) for p in group])
        for p in group:
            push(p, s, y_peer, ys.at[i, p])
            push(p, s, x_peer, xs.at[i, p])
            push(p, s, c_peer, cs.at[i, p])

    def side_event(i, group):
        for p in group:
            s = shard(1 - y, line[i], x, c)
            arrived(p, s)
            if Y_FIRST[p]:
                push(p, s, x_peer, xs.at[4 + i, p])
            push(p, s, c_peer, cs.at[4 + i, p])
        for p in group:
            s = shard(y, line[i], 1 - x, c)
            arrived(p, s)
            if not Y_FIRST[p]:
                push(p, s, y_peer, ys.at[4 + i, p])
            push(p, s, c_peer, cs.at[8 + i, p])

    def corner_event(i, group):
        s = shard(1 - y, line[i], 1 - x, c)
        for p in group:
            arrived(p, s)
            push(p, s, c_peer, cs.at[12 + i, p])

    def core_events(group):
        for yy in (y, 1 - y):
            for zz in line:
                for xx in (x, 1 - x):
                    for p in group:
                        arrived(p, shard(yy, zz, xx, 1 - c))

    def block(ref, i):
        return ref.at[pl.ds(i * per, per)]

    def lanes(ref, i):
        at = pl.ds(pl.multiple_of(i * WIDTH, WIDTH), WIDTH)
        return ref.at[:, at] if len(ref.shape) == 2 else ref.at[:, :, at]

    greet([device(y, a, b, c) for a, b in plane] + [y_peer, c_peer])
    own_sends(EARLY)
    homes = []
    for p in range(5):
        homes.append(pltpu.make_async_copy(src[p], slot(p, me), own_sem.at[p]))
    for p, (a, b) in enumerate(((lanes(keys, chip), kh), (lanes(vals, chip), vh), (bias, bh))):
        homes.append(pltpu.make_async_copy(a, block(b, m), ko.at[p]))
    for copy in homes:
        copy.start()

    inputs = x_ref[...].astype(F32)
    normed = inputs * lax.rsqrt(jnp.mean(inputs * inputs, axis=-1, keepdims=True) + epsilon)

    for i in (1, 2, 3):
        line_event(i, EARLY)
    own_sends(LATE)
    for i, (zz, xx) in enumerate(plane):
        head = zz * 2 + xx
        for p, (a, b) in enumerate(((lanes(keys, head), kh), (lanes(vals, head), vh), (bias, bh))):
            go(remote(a, block(b, m), ks.at[i, p], kr.at[m, p], device(y, zz, xx, c)))
    for p, (a, b) in enumerate(((lanes(keys, chip), kh), (lanes(vals, chip), vh), (bias, bh))):
        go(remote(a, block(b, m), kcs.at[7, p], kr.at[m, p], c_peer))
    for i in range(4):
        side_event(i, EARLY)
    for i in range(4):
        corner_event(i, EARLY)
    core_events(EARLY)
    for copy in homes:
        copy.wait()

    packed = dst[4][...].reshape(32 * 16, 128)
    gain = expand(packed, 0, own_rows)
    gain_out[...] = jnp.concatenate(
        [gain, expand(packed, own_rows, own_rows), jnp.zeros((6, width), F32)], axis=0
    )
    low = (normed * gain).astype(BF16)
    h_ref[...] = low
    for i, ref in enumerate((q_ref, k_ref, v_ref)):
        weight = dst[0][:, :, i * width : (i + 1) * width].reshape(width, width)
        ref[...] = jnp.dot(low, weight, preferred_element_type=F32).astype(BF16)

    others = [(chip + d) % 8 for d in range(1, 8)]
    peers = [{"dp": y, "mem": o * ranks + c} for o in others]
    for d, (o, peer) in enumerate(zip(others, peers)):
        go(remote(lanes(q_ref, o), qh.at[chip], qs.at[d], qr.at[chip], peer))
    mine = pltpu.make_async_copy(lanes(q_ref, chip), qh.at[chip], ko.at[0])
    mine.start()

    line_event(1, LATE)

    below = lax.broadcasted_iota(jnp.int32, (rows, rows), 1)
    ok = (below <= lax.broadcasted_iota(jnp.int32, (rows, rows), 0)) & (below < lens[0, 0])
    lane = lax.broadcasted_iota(jnp.int32, (rows, 128), 1)
    tops = jnp.zeros((rows, 128), F32)
    sums = jnp.zeros((rows, 128), F32)
    for i in range(HEADS):
        at = slice(i * WIDTH, (i + 1) * WIDTH)
        s = lax.dot_general(
            q_ref[:, at], k_ref[:, at], (((1,), (1,)), ((), ())), preferred_element_type=F32
        )
        s = jnp.where(ok, s * factor, neg_big)
        top = jnp.max(s, axis=1, keepdims=True)
        p = jnp.exp2(s - top)
        tops = jnp.where(lane == i, top, tops)
        sums = jnp.where(lane == i, jnp.sum(p, axis=1, keepdims=True), sums)
        loc[:, at] = jnp.dot(p.astype(BF16), v_ref[:, at], preferred_element_type=F32)
    st[0] = tops
    st[1] = sums

    line_event(2, LATE)
    line_event(3, LATE)
    side_event(0, LATE)
    side_event(1, LATE)

    for i, (zz, xx) in reversed(list(enumerate(plane))):
        other = zz * 4 + xx * 2 + c
        for p, b in enumerate((kh, vh, bh)):
            view = block(b, other)
            remote(view, view, ko.at[p], kr.at[other, p], c_peer).wait_recv()
            go(remote(view, view, kcs.at[i, p], kr.at[other, p], c_peer))
    for zz, xx in [(z, x)] + plane[::-1]:
        other = zz * 4 + xx * 2 + 1 - c
        for p, b in enumerate((kh, vh, bh)):
            remote(block(b, other), block(b, other), ko.at[p], kr.at[other, p], c_peer).wait_recv()
    mine.wait()
    for o in others:
        remote(qh.at[o], qh.at[o], ko.at[0], qr.at[o], c_peer).wait_recv()

    def attend(d, _):
        j = (chip + d) % 8
        start, stop, base, window = key_window(j, ranks, c, docs, sizes, total)
        q = qh[j]
        parts = 3
        chunk = window // parts

        def step(t, carry):
            top, tsum, acc = carry
            at = base + t * chunk
            s = lax.dot_general(
                q, rows_of(kh, at, chunk), (((1,), (1,)), ((), ())), preferred_element_type=F32
            )
            s = s * factor + window_bias(bh, at, chunk, start, stop)
            best = jnp.maximum(top, jnp.max(s, axis=1, keepdims=True))
            p = jnp.exp2(s - best)
            keep = jnp.exp2(top - best)
            tsum = tsum * keep + jnp.sum(p, axis=1, keepdims=True)
            acc = acc * keep + jnp.dot(p.astype(BF16), rows_of(vh, at, chunk), preferred_element_type=F32)
            return best, tsum, acc

        top, tsum, acc = lax.fori_loop(
            0,
            parts,
            step,
            (jnp.full((rows, 1), neg_big, F32), jnp.zeros((rows, 1), F32), jnp.zeros((rows, WIDTH), F32)),
        )
        oh[j] = (acc / tsum).astype(BF16)
        lh[j] = jnp.broadcast_to(top + jnp.log2(tsum), (rows, rows)).T[0:8]
        return 0

    def answer(d):
        j = (chip + d) % 8
        peer = {"dp": y, "mem": j * ranks + c}
        go(remote(oh.at[j], lanes(mo, chip), os_.at[d, 0], or_.at[chip, 0], peer))
        go(remote(lh.at[j], ml.at[chip], os_.at[d, 1], or_.at[chip, 1], peer))

    lax.fori_loop(1, 3, attend, 0)
    answer(1)
    answer(2)
    side_event(2, LATE)
    lax.fori_loop(3, 5, attend, 0)
    answer(3)
    answer(4)
    side_event(3, LATE)
    lax.fori_loop(5, 7, attend, 0)
    answer(5)
    answer(6)
    corner_event(0, LATE)
    lax.fori_loop(7, 9, attend, 0)
    answer(7)
    backs = [
        pltpu.make_async_copy(oh.at[chip], lanes(mo, chip), ko.at[0]),
        pltpu.make_async_copy(lh.at[chip], ml.at[chip], ko.at[1]),
    ]
    for copy in backs:
        copy.start()
    corner_event(1, LATE)
    for o in others:
        remote(lanes(mo, o), lanes(mo, o), ko.at[0], or_.at[o, 0], c_peer).wait_recv()
        remote(ml.at[o], ml.at[o], ko.at[1], or_.at[o, 1], c_peer).wait_recv()
    for copy in backs:
        copy.wait()

    head_row = lax.broadcasted_iota(jnp.int32, (8, rows), 0)
    gathered = jnp.zeros((8, rows), F32)
    for i in range(HEADS):
        gathered = jnp.where(head_row == i, ml[i], gathered)
    mem_lse = columns(gathered)
    tops, sums = st[0], st[1]
    known = lane < HEADS
    loc_lse = jnp.where(known, tops + jnp.log2(jnp.where(known, sums, 1.0)), 0.0)
    best = jnp.maximum(loc_lse, mem_lse)
    whole = best + jnp.log2(jnp.exp2(loc_lse - best) + jnp.exp2(mem_lse - best))
    tot[...] = whole
    loc_scale = jnp.exp2(tops - whole)
    mem_scale = jnp.exp2(mem_lse - whole)
    for i in range(HEADS):
        at = slice(i * WIDTH, (i + 1) * WIDTH)
        value = loc[:, at] * loc_scale[:, i : i + 1] + mo[:, at].astype(F32) * mem_scale[:, i : i + 1]
        att[:, at] = value
        o_low[:, at] = value.astype(BF16)
    corner_event(2, LATE)
    corner_event(3, LATE)
    core_events(LATE)
    weight = dst[1][...].reshape(width, width)
    first_out[...] = x_ref[...].astype(F32) + jnp.dot(o_low[...], weight, preferred_element_type=F32)
    for copy in pending:
        copy.wait_send()

    @pl.when(inner == 1)
    def _():
        for copy in inner_pending:
            copy.wait_send()


def front(docs, sizes, lens, tokens, pieces, keys, values, bias, own_rows):
    dma = pltpu.SemaphoreType.DMA
    rows, width = tokens.shape
    total = keys.shape[0] * 16
    shape = jax.ShapeDtypeStruct
    wide = shape((rows, width), BF16)
    outs = [
        shape((rows, width), F32),
        wide,
        shape((rows, width), F32),
        shape((rows, 128), F32),
        wide,
        wide,
        wide,
        wide,
        shape((8, rows, WIDTH), BF16),
        shape((8, width), F32),
    ]
    outs += [shape((32,) + a.shape, a.dtype) for a in pieces]
    outs += [shape((total, KEYS, WIDTH), BF16)] * 2 + [shape((total, 8, KEYS), F32)]
    spaces = [VM] * 10 + [VM, VM, ANY, ANY, VM] + [VM] * 3
    return pl.pallas_call(
        functools.partial(front_kernel, own_rows),
        out_shape=outs,
        in_specs=[SM] * 3 + [VM] * 9,
        out_specs=spaces,
        scratch_shapes=[
            pltpu.VMEM((8, rows, WIDTH), BF16),
            pltpu.VMEM((8, 8, rows), F32),
            pltpu.VMEM((rows, width), BF16),
            pltpu.VMEM((8, 8, rows), F32),
            pltpu.VMEM((rows, width), F32),
            pltpu.VMEM((2, rows, 128), F32),
            dma((5,)),
            dma((32, 5)),
            dma((5, 5)),
            dma((8, 5)),
            dma((8, 5)),
            dma((16, 5)),
            dma((3,)),
            dma((16, 3)),
            dma((7, 3)),
            dma((8, 3)),
            dma((7,)),
            dma((8,)),
            dma((8, 2)),
            dma((8, 2)),
        ],
        compiler_params=pltpu.CompilerParams(
            collective_id=0, has_side_effects=True, vmem_limit_bytes=48 << 20
        ),
        name="front",
    )(docs, sizes, lens, tokens, *pieces, keys, values, bias)


def swap_kernel(kinds, ranks, *refs):
    n = len(kinds)
    srcs, dsts, (own, send, recv) = refs[:n], refs[n : 2 * n], refs[2 * n :]
    m = lax.axis_index("mem")
    y = lax.axis_index("dp")
    count = lax.axis_size("mem") // ranks
    rank, me = m % ranks, m // ranks

    def at(kind, ref, i, outside):
        wide = (kind == "heads") == outside
        if wide and len(ref.shape) == 2:
            return ref.at[:, pl.ds(pl.multiple_of(i * WIDTH, WIDTH), WIDTH)]
        return ref.at[i]

    others = [(me + d) % count for d in range(1, count)]
    targets = [{"dp": y, "mem": o * ranks + rank} for o in others]
    greet(targets)
    copies = []
    for d, (o, target) in enumerate(zip(others, targets)):
        for p, kind in enumerate(kinds):
            copy = remote(
                at(kind, srcs[p], o, True), at(kind, dsts[p], me, False), send.at[d, p], recv.at[me, p], target
            )
            copy.start()
            copies.append(copy)
    mine = []
    for p, kind in enumerate(kinds):
        copy = pltpu.make_async_copy(at(kind, srcs[p], me, True), at(kind, dsts[p], me, False), own.at[p])
        copy.start()
        mine.append(copy)
    for o, target in zip(others, targets):
        for p, kind in enumerate(kinds):
            view = at(kind, dsts[p], o, False)
            remote(view, view, own.at[p], recv.at[o, p], target).wait_recv()
    for copy in mine:
        copy.wait()
    for copy in copies:
        copy.wait_send()


def swap(kinds, arrays, outs, ranks, ident):
    dma = pltpu.SemaphoreType.DMA
    count = lax.axis_size("mem") // ranks
    n = len(kinds)
    return pl.pallas_call(
        functools.partial(swap_kernel, kinds, ranks),
        out_shape=outs,
        in_specs=[VM] * n,
        out_specs=[VM] * n,
        scratch_shapes=[dma((n,)), dma((count - 1, n)), dma((count, n))],
        compiler_params=pltpu.CompilerParams(
            collective_id=ident, has_side_effects=True, vmem_limit_bytes=16 << 20
        ),
        name=f"swap{ident}",
    )(*arrays)


def key_span(j, ranks, docs, sizes, rank_ref):
    doc = docs[0, j * ranks + rank_ref[0]]
    start = jnp.int32(0)
    stop = jnp.int32(0)
    for i in range(sizes.shape[1]):
        size = sizes[0, i]
        start = start + jnp.where(i < doc, size, 0)
        stop = stop + jnp.where(i <= doc, size, 0)
    return start, stop


def forward_kernel(ranks, block, docs, sizes, rank_ref, q_ref, k_ref, v_ref, bias_ref, o_ref, lse_ref):
    j = pl.program_id(0)
    start, stop = key_span(j, ranks, docs, sizes, rank_ref)
    q = q_ref[0]
    factor = WIDTH ** (-0.5) * LOG2E

    def step(b, carry):
        top, total, acc = carry
        s = lax.dot_general(
            q, rows_of(k_ref, b * block, block), (((1,), (1,)), ((), ())), preferred_element_type=F32
        )
        s = s * factor + window_bias(bias_ref, b * block, block, start, stop)
        best = jnp.maximum(top, jnp.max(s, axis=1, keepdims=True))
        p = jnp.exp2(s - best)
        keep = jnp.exp2(top - best)
        total = total * keep + jnp.sum(p, axis=1, keepdims=True)
        acc = acc * keep + jnp.dot(
            p.astype(BF16), rows_of(v_ref, b * block, block), preferred_element_type=F32
        )
        return best, total, acc

    rows = q.shape[0]
    top, total, acc = lax.fori_loop(
        start // (block * KEYS),
        (stop + block * KEYS - 1) // (block * KEYS),
        step,
        (jnp.full((rows, 1), neg_big, F32), jnp.zeros((rows, 1), F32), jnp.zeros((rows, WIDTH), F32)),
    )
    o_ref[0] = (acc / total).astype(BF16)
    lse = jnp.broadcast_to(top + jnp.log2(total), (rows, rows))
    lse_ref[0] = lse.T[0:8]


def backward_kernel(
    ranks, block, docs, sizes, rank_ref, q_ref, do_ref, stat_ref, k_ref, v_ref, bias_ref, dq_ref
):
    j = pl.program_id(0)
    start, stop = key_span(j, ranks, docs, sizes, rank_ref)
    q, do = q_ref[0], do_ref[0]
    rows = q.shape[0]
    factor = WIDTH ** (-0.5) * LOG2E
    stat = stat_ref[0]
    lse = jnp.broadcast_to(stat[0:1], (rows, rows)).T[:, 0:1]
    delta = jnp.broadcast_to(stat[1:2], (rows, rows)).T[:, 0:1]

    def step(b, acc):
        keys = rows_of(k_ref, b * block, block)
        s = lax.dot_general(q, keys, (((1,), (1,)), ((), ())), preferred_element_type=F32)
        p = jnp.exp2(s * factor + (window_bias(bias_ref, b * block, block, start, stop) - lse))
        dp = lax.dot_general(do, rows_of(v_ref, b * block, block), (((1,), (1,)), ((), ())), preferred_element_type=F32)
        ds = (p * (dp - delta)).astype(BF16)
        return acc + jnp.dot(ds, keys, preferred_element_type=F32)

    acc = lax.fori_loop(
        start // (block * KEYS), (stop + block * KEYS - 1) // (block * KEYS), step, jnp.zeros((rows, WIDTH), F32)
    )
    dq_ref[0] = (acc * WIDTH ** (-0.5)).astype(BF16)


def memory_forward(ranks, docs, sizes, rank, q, kh, vh, bh):
    count, rows, _ = q.shape
    seg = pl.BlockSpec((1, rows, WIDTH), lambda j: (j, 0, 0))
    stat = pl.BlockSpec((1, 8, rows), lambda j: (j, 0, 0))
    block = 8
    return pl.pallas_call(
        functools.partial(forward_kernel, ranks, block),
        grid=(count,),
        out_shape=[
            jax.ShapeDtypeStruct((count, rows, WIDTH), BF16),
            jax.ShapeDtypeStruct((count, 8, rows), F32),
        ],
        in_specs=[SM, SM, SM, seg, VM, VM, VM],
        out_specs=[seg, stat],
        compiler_params=pltpu.CompilerParams(vmem_limit_bytes=48 << 20),
        name="memory_forward",
    )(docs, sizes, rank, q, kh, vh, bh)


def memory_backward(ranks, docs, sizes, rank, q, do, stats, kh, vh, bh):
    count, rows, _ = q.shape
    seg = pl.BlockSpec((1, rows, WIDTH), lambda j: (j, 0, 0))
    stat = pl.BlockSpec((1, 8, rows), lambda j: (j, 0, 0))
    block = 8
    return pl.pallas_call(
        functools.partial(backward_kernel, ranks, block),
        grid=(count,),
        out_shape=jax.ShapeDtypeStruct((count, rows, WIDTH), BF16),
        in_specs=[SM, SM, SM, seg, seg, stat, VM, VM, VM],
        out_specs=seg,
        compiler_params=pltpu.CompilerParams(vmem_limit_bytes=48 << 20),
        name="memory_backward",
    )(docs, sizes, rank, q, do, stats, kh, vh, bh)


def reduce_kernel(*refs):
    h, dqkv, o, da, h2, dgu, hid, og, small = refs[:9]
    outs = refs[9:14]
    grads = refs[14:19]
    cores = refs[19:24]
    firsts = refs[24:29]
    seconds = refs[29:34]
    lines = refs[34:39]
    ht, ot, h2t, hidt = refs[39:43]
    cs, cr, fs, fr, ss, sr, zs, zr = refs[43:]
    n = 5
    y, z, x, c = place()
    y_peer, x_peer, c_peer = device(1 - y, z, x, c), device(y, z, 1 - x, c), device(y, z, x, 1 - c)
    greet([y_peer, x_peer, c_peer] + [device(y, flip_z(z, d), x, c) for d in (1, 2, 3)])
    ht[...] = h[...].T
    ot[...] = o[...].T
    h2t[...] = h2[...].T
    hidt[...] = hid[...].T
    pending = []

    def start(copy):
        copy.start()
        pending.append(copy)

    left = (ht, ot, h2t, hidt)
    right = (dqkv, da, dgu, og)
    order = [(k, d) for d in (3, 2, 1, 0) for k in (1, 0)]

    def unit(k, d):
        return (1 - y if k else y), flip_z(z, d)

    def produce(i):
        k, d = order[i]
        yy, zz = unit(k, d)
        u = yy * 4 + zz
        for p in range(4):
            rows = 4 * grads[p].shape[2]
            block = left[p][pl.ds(pl.multiple_of(u * rows, 32), rows), :]
            width = grads[p].shape[3]
            tile = 1024 if width % 1024 == 0 else 1408
            for t in range(0, width, tile):
                part = jnp.dot(block, right[p][:, t : t + tile], preferred_element_type=F32)
                grads[p][i, :, :, t : t + tile] = part.astype(BF16).reshape(4, rows // 4, tile)
        for q in range(4):
            grads[4][i, q] = small[u * 4 + q]
        for p in range(n):
            for xx in range(2):
                start(remote(grads[p].at[i, xx * 2 + 1 - c], cores[p].at[i, xx], cs.at[i, xx, p], cr.at[i, xx, p], c_peer))

    def wait(dst, sem):
        remote(dst, dst, cs.at[0, 0, 0], sem, c_peer).wait_recv()

    def merge(own, other):
        own[...] = (own[...].astype(F32) + other[...].astype(F32)).astype(own.dtype)

    def after_core(i):
        k, d = order[i]
        for p in range(n):
            for xx in (1 - x, x):
                own = grads[p].at[i, xx * 2 + c]
                wait(cores[p].at[i, xx], cr.at[i, xx, p])
                merge(own, cores[p].at[i, xx])
            if FIRST_BACK[p] == "x":
                start(remote(grads[p].at[i, (1 - x) * 2 + c], firsts[p].at[i], fs.at[i, 0, p], fr.at[i, 0, p], x_peer))
            elif k == 1:
                for xx in range(2):
                    start(remote(grads[p].at[i, xx * 2 + c], firsts[p].at[(i + 1) // 2 * 2 // 2 + 4 * xx], fs.at[i, xx, p], fr.at[i // 2, xx, p], y_peer))

    def after_first(i):
        k, d = order[i]
        for p in range(n):
            own = grads[p].at[i, x * 2 + c]
            if FIRST_BACK[p] == "x":
                wait(firsts[p].at[i], fr.at[i, 0, p])
                merge(own, firsts[p].at[i])
                if k == 1:
                    start(remote(own, seconds[p].at[i // 2], ss.at[i // 2, p], sr.at[i // 2, p], y_peer))
            elif k == 0:
                for xx in range(2):
                    wait(firsts[p].at[i // 2 + 4 * xx], fr.at[i // 2, xx, p])
                    merge(grads[p].at[i, xx * 2 + c], firsts[p].at[i // 2 + 4 * xx])
                start(remote(grads[p].at[i, (1 - x) * 2 + c], seconds[p].at[i // 2], ss.at[i // 2, p], sr.at[i // 2, p], x_peer))

    def after_second(i):
        k, d = order[i]
        if k == 1:
            return
        for p in range(n):
            own = grads[p].at[i, x * 2 + c]
            wait(seconds[p].at[i // 2], sr.at[i // 2, p])
            merge(own, seconds[p].at[i // 2])
            if d:
                start(remote(own, lines[p].at[d - 1], zs.at[d - 1, p], zr.at[d - 1, p], device(y, flip_z(z, d), x, c)))

    for t in range(8 + 6):
        if t < 8:
            produce(t)
        if 0 <= t - 1 < 8:
            after_core(t - 1)
        if 0 <= t - 3 < 8:
            after_first(t - 3)
        if 0 <= t - 5 < 8:
            after_second(t - 5)
    for p in range(n):
        total = grads[p][7, x * 2 + c].astype(F32)
        for d in (1, 2, 3):
            wait(lines[p].at[d - 1], zr.at[d - 1, p])
            total = total + lines[p][d - 1].astype(F32)
        outs[p][...] = total
    for copy in pending:
        copy.wait_send()


FIRST_BACK = ("y", "y", "x", "y", "x")


def reduce_call(h, dqkv, o, da, h2, dgu, hid, og, small):
    dma = pltpu.SemaphoreType.DMA
    rows, width = h.shape
    down = hid.shape[1] // 32
    own = width // 32
    shapes = [
        ((own, dqkv.shape[1]), BF16),
        ((own, da.shape[1]), BF16),
        ((own, dgu.shape[1]), BF16),
        ((down, og.shape[1]), BF16),
        (small.shape[1:], F32),
    ]

    def buffers(lead):
        return [
            pltpu.VMEM((lead(p) if isinstance(lead(p), tuple) else (lead(p),)) + s, t)
            for p, (s, t) in enumerate(shapes)
        ]

    return pl.pallas_call(
        reduce_kernel,
        out_shape=[jax.ShapeDtypeStruct(s, F32) for s, _ in shapes],
        in_specs=[VM] * 9,
        out_specs=[VM] * 5,
        scratch_shapes=buffers(lambda p: (8, 4))
        + buffers(lambda p: (8, 2))
        + buffers(lambda p: 8)
        + buffers(lambda p: 4)
        + buffers(lambda p: 3)
        + [
            pltpu.VMEM((width, rows), BF16),
            pltpu.VMEM((width, rows), BF16),
            pltpu.VMEM((width, rows), BF16),
            pltpu.VMEM((hid.shape[1], rows), BF16),
            dma((8, 2, 5)),
            dma((8, 2, 5)),
            dma((8, 2, 5)),
            dma((8, 2, 5)),
            dma((4, 5)),
            dma((4, 5)),
            dma((3, 5)),
            dma((3, 5)),
        ],
        compiler_params=pltpu.CompilerParams(
            collective_id=5, has_side_effects=True, vmem_limit_bytes=VMEM_MAX
        ),
        name="reduce",
    )(h, dqkv, o, da, h2, dgu, hid, og, small)


def gather_plain(pieces, keys, values, bias, ranks):
    full = [lax.all_gather(a, ("dp", "mem"), axis=0, tiled=False) for a in pieces]

    def spread(a):
        blocks = a.reshape(a.shape[0], HEADS, WIDTH).transpose(1, 0, 2)
        return lax.all_to_all(jnp.repeat(blocks, ranks, axis=0), "mem", 0, 0, tiled=True)

    return full + [
        spread(keys).reshape(-1, KEYS, WIDTH),
        spread(values).reshape(-1, KEYS, WIDTH),
        lax.all_gather(bias, "mem", axis=0, tiled=True),
    ]


def to_heads_plain(x, ranks):
    rank = lax.axis_index("mem") % ranks
    blocks = x if x.ndim == 3 else x.reshape(x.shape[0], HEADS, WIDTH).transpose(1, 0, 2)
    wide = jnp.where((jnp.arange(ranks) == rank)[None, :, None, None], blocks[:, None], 0)
    wide = wide.reshape((-1,) + blocks.shape[1:])
    got = lax.all_to_all(wide, "mem", 0, 0, tiled=True)
    return lax.dynamic_index_in_dim(got.reshape((-1, ranks) + blocks.shape[1:]), rank, 1, keepdims=False)


def to_tokens_plain(x, ranks, wide_out):
    rank = lax.axis_index("mem") % ranks
    wide = jnp.where((jnp.arange(ranks) == rank)[None, :, None, None], x[:, None], 0)
    got = lax.all_to_all(wide.reshape((-1,) + x.shape[1:]), "mem", 0, 0, tiled=True)
    got = lax.dynamic_index_in_dim(got.reshape((-1, ranks) + x.shape[1:]), rank, 1, keepdims=False)
    return got.transpose(1, 0, 2).reshape(x.shape[1], -1) if wide_out else got


def reduce_plain(h, dqkv, o, da, h2, dgu, hid, og, small):
    outs = []
    for a, b in ((h, dqkv), (o, da), (h2, dgu), (hid, og)):
        full = jnp.dot(a.T, b, preferred_element_type=F32)
        outs.append(lax.psum_scatter(full, ("dp", "mem"), scatter_dimension=0, tiled=True))
    outs.append(lax.psum_scatter(small, ("dp", "mem"), scatter_dimension=0, tiled=False))
    return outs


def normalize(values):
    inverse = lax.rsqrt(jnp.mean(values * values, axis=-1, keepdims=True) + epsilon)
    return (values * inverse, inverse)


def norm_back(grad_scaled, normed, inverse, gain_full):
    gain_grad = jnp.sum(grad_scaled * normed, axis=0)
    grad_normed = grad_scaled * gain_full
    grad_values = inverse * (
        grad_normed - normed * jnp.mean(grad_normed * normed, axis=-1, keepdims=True)
    )
    return (gain_grad, grad_values)


def shards(
    tokens,
    gain_attn,
    w_query,
    w_key,
    w_value,
    w_out,
    gain_ffn,
    w_gate,
    w_up,
    w_down,
    mem_keys,
    mem_values,
    out_grad,
    key_mask,
    mem_sizes,
    seg_doc,
    seg_len,
):
    seg_rows, model_width = tokens.shape
    mem_count = lax.axis_size("mem")
    dp_count = lax.axis_size("dp")
    devices = mem_count * dp_count
    ranks = mem_count // HEADS
    direct = dp_count == 2 and mem_count == 16
    factor = WIDTH ** (-0.5)
    ff_width = w_gate.shape[1]
    own = gain_attn.shape[0]
    down_rows = w_down.shape[0]

    pieces = [
        jnp.concatenate([w_query, w_key, w_value], axis=1),
        w_out,
        jnp.concatenate([w_gate, w_up], axis=1),
        w_down,
        jnp.pad(jnp.concatenate([gain_attn, gain_ffn])[None], ((0, 15), (0, 128 - 2 * own))),
    ]
    bias = jnp.where(key_mask == 1, 0.0, neg_big).astype(F32).reshape(-1, 1, KEYS)
    bias = jnp.broadcast_to(bias, (bias.shape[0], 8, KEYS))
    rank = (lax.axis_index("mem") % ranks).reshape(1).astype(jnp.int32)
    seg_count = mem_count // ranks
    block_shape = jax.ShapeDtypeStruct((seg_count, seg_rows, WIDTH), BF16)
    stat_shape = jax.ShapeDtypeStruct((seg_count, 8, seg_rows), F32)
    wide_shape = jax.ShapeDtypeStruct((seg_rows, model_width), BF16)
    inputs = tokens.astype(F32)
    normed_one, inverse_one = normalize(inputs)
    positions = lax.iota(jnp.int32, seg_rows)
    local_ok = ((positions[None, :] <= positions[:, None]) & (positions[None, :] < seg_len[0, 0]))[
        None
    ]

    if direct:
        split = (-1, KEYS, model_width)
        done = front(
            seg_doc, mem_sizes, seg_len, tokens, pieces, mem_keys.reshape(split), mem_values.reshape(split), bias, own
        )
        first, attended_low, attended, whole, normed_low, queries, keys_local, values_local = done[:8]
        q_heads, gains, joined_w, out_full, gate_up, down_full, _, kh, vh, bh = done[8:]
        gain_one, gain_two = gains[0], gains[1]
        attended = attended.reshape(seg_rows, HEADS, WIDTH)
        log_total = whole[:, :HEADS].T / LOG2E
    else:
        gathered = gather_plain(pieces, mem_keys, mem_values, bias, ranks)
        joined_w, out_full, gate_up, down_full, gains, kh, vh, bh = gathered
        gain_one = gains[:, 0, :own].reshape(-1).astype(F32)
        gain_two = gains[:, 0, own : 2 * own].reshape(-1).astype(F32)
    joined_w = joined_w.reshape(model_width, -1)
    out_full = out_full.reshape(model_width, -1)
    gate_up = gate_up.reshape(model_width, -1)
    down_full = down_full.reshape(ff_width, -1)
    if not direct:
        normed_low = (normed_one * gain_one).astype(BF16)
        projected = jnp.dot(normed_low, joined_w, preferred_element_type=F32).astype(BF16)
        queries = projected[:, :model_width]
        keys_local = projected[:, model_width : 2 * model_width]
        values_local = projected[:, 2 * model_width :]
    query_heads = queries.reshape(seg_rows, HEADS, WIDTH)
    key_heads = keys_local.reshape(seg_rows, HEADS, WIDTH)
    value_heads = values_local.reshape(seg_rows, HEADS, WIDTH)
    local_scores = (
        jnp.einsum("ihd,jhd->hij", query_heads, key_heads, preferred_element_type=F32) * factor
    )
    local_masked = jnp.where(local_ok, local_scores, neg_big)
    if not direct:
        q_heads = to_heads_plain(queries, ranks)
        o_mem, lse_mem = memory_forward(ranks, seg_doc, mem_sizes, rank, q_heads, kh, vh, bh)
        mem_o = to_tokens_plain(o_mem, ranks, True).reshape(seg_rows, HEADS, WIDTH).astype(F32)
        mem_lse = to_tokens_plain(lse_mem, ranks, False)[:, 0, :] / LOG2E
        local_top = jnp.max(local_masked, axis=2)
        local_total = jnp.sum(
            jnp.where(local_ok, jnp.exp(local_masked - local_top[:, :, None]), 0.0), axis=2
        )
        local_lse = local_top + jnp.log(local_total)
        best = jnp.maximum(local_lse, mem_lse)
        log_total = best + jnp.log(jnp.exp(local_lse - best) + jnp.exp(mem_lse - best))
    local_probs = jnp.where(local_ok, jnp.exp(local_masked - log_total[:, :, None]), 0.0)
    local_low = local_probs.astype(BF16)
    if not direct:
        attended = (
            jnp.einsum("hij,jhd->ihd", local_low, value_heads, preferred_element_type=F32)
            + mem_o * jnp.exp(mem_lse - log_total).T[..., None]
        )
        attended_low = attended.reshape(seg_rows, model_width).astype(BF16)
        first = inputs + jnp.dot(attended_low, out_full, preferred_element_type=F32)

    normed_two, inverse_two = normalize(first)
    normed_two_low = (normed_two * gain_two).astype(BF16)
    gate_upward = jnp.dot(normed_two_low, gate_up, preferred_element_type=F32)
    gate, upward = gate_upward[:, :ff_width], gate_upward[:, ff_width:]
    sigmoid_gate = jax.nn.sigmoid(gate)
    activated = gate * sigmoid_gate
    hidden = (activated * upward).astype(BF16)
    output = (first + jnp.dot(hidden, down_full, preferred_element_type=F32)).astype(BF16)
    grad_hidden = jnp.dot(out_grad, down_full.T, preferred_element_type=F32)
    grad_gate_up = jnp.concatenate(
        [
            (grad_hidden * upward * sigmoid_gate * (1.0 + gate * (1.0 - sigmoid_gate))).astype(BF16),
            (grad_hidden * activated).astype(BF16),
        ],
        axis=1,
    )
    grad_normed_two = jnp.dot(grad_gate_up, gate_up.T, preferred_element_type=F32)
    grad_gain_two, grad_first_norm = norm_back(grad_normed_two, normed_two, inverse_two, gain_two)
    grad_first = out_grad.astype(F32) + grad_first_norm

    grad_branch = grad_first.astype(BF16)
    grad_attended = jnp.dot(grad_branch, out_full.T, preferred_element_type=F32).astype(BF16)
    grad_att_heads = grad_attended.reshape(seg_rows, HEADS, WIDTH)
    delta = jnp.sum(grad_att_heads.astype(F32) * attended, axis=-1).T
    stats = jnp.pad(jnp.stack([log_total * LOG2E, delta], axis=1), ((0, 0), (0, 6), (0, 0)))
    if direct:
        do_heads, stat_heads = swap(
            ("heads", "heads"), (grad_attended, stats), (block_shape, stat_shape), ranks, 3
        )
    else:
        do_heads = to_heads_plain(grad_attended, ranks)
        stat_heads = to_heads_plain(stats, ranks)
    dq_heads = memory_backward(
        ranks, seg_doc, mem_sizes, rank, q_heads, do_heads, stat_heads, kh, vh, bh
    )
    if direct:
        (grad_query_memory,) = swap(("tokens",), (dq_heads,), (wide_shape,), ranks, 4)
    else:
        grad_query_memory = to_tokens_plain(dq_heads, ranks, True)

    grad_value_heads = jnp.einsum(
        "hij,ihd->jhd", local_low, grad_att_heads, preferred_element_type=F32
    )
    grad_local_probs = jnp.einsum(
        "ihd,jhd->hij", grad_att_heads, value_heads, preferred_element_type=F32
    )
    grad_local_scores = (local_probs * (grad_local_probs - delta[:, :, None])).astype(BF16)
    grad_query_heads = (
        jnp.einsum("hij,jhd->ihd", grad_local_scores, key_heads, preferred_element_type=F32)
        * factor
    )
    grad_key_heads = (
        jnp.einsum("hij,ihd->jhd", grad_local_scores, query_heads, preferred_element_type=F32)
        * factor
    )
    grad_queries = grad_query_heads.reshape(seg_rows, model_width) + grad_query_memory.astype(F32)
    grad_joined = jnp.concatenate(
        [
            grad_queries,
            grad_key_heads.reshape(seg_rows, model_width),
            grad_value_heads.reshape(seg_rows, model_width),
        ],
        axis=1,
    ).astype(BF16)
    grad_normed_one = jnp.dot(grad_joined, joined_w.T, preferred_element_type=F32)
    grad_gain_one, grad_input_norm = norm_back(grad_normed_one, normed_one, inverse_one, gain_one)
    input_grad = (grad_first + grad_input_norm).astype(BF16)

    small = jnp.stack([grad_gain_one.reshape(devices, own), grad_gain_two.reshape(devices, own)], axis=1)
    small = jnp.pad(small, ((0, 0), (0, 6), (0, 128 - own)))
    reducer = reduce_call if direct else reduce_plain
    attn_sums, out_sums, ffn_sums, down_sums, small_sums = reducer(
        normed_low, grad_joined, attended_low, grad_branch, normed_two_low, grad_gate_up, hidden, out_grad, small
    )
    return (
        output,
        input_grad,
        small_sums[0, :own],
        attn_sums[:, :model_width],
        attn_sums[:, model_width : 2 * model_width],
        attn_sums[:, 2 * model_width : 3 * model_width],
        out_sums,
        small_sums[1, :own],
        ffn_sums[:, :ff_width],
        ffn_sums[:, ff_width:],
        down_sums,
    )


def solution(mesh):
    rows = P(("dp", "mem"), None)
    vector = P(("dp", "mem"))
    in_specs = (
        (rows, vector) + (rows,) * 4 + (vector,) + (rows,) * 6
        + (P("dp", "mem"), P("dp", None), P("dp", None), P("dp", "mem"))
    )
    out_specs = (rows, rows, vector) + (rows,) * 4 + (vector,) + (rows,) * 3
    return jax.shard_map(shards, mesh=mesh, in_specs=in_specs, out_specs=out_specs, check_vma=False)
```

```python
import functools
import math

import jax
import jax.numpy as jnp
from jax import lax
from jax.experimental import pallas as pl
from jax.experimental.pallas import tpu as pltpu
from jax.sharding import PartitionSpec as P

HEADS = 8
WIDTH = 128
KEYS = 128
epsilon = 1e-05
neg_big = -1e30
LOG2E = 1.4426950408889634
VMEM_MAX = 67043328
MESH = pl.DeviceIdType.MESH
F32 = jnp.float32
BF16 = jnp.bfloat16

ANY = pl.BlockSpec(memory_space=pl.ANY)
VM = pl.BlockSpec(memory_space=pltpu.VMEM)
SM = pl.BlockSpec(memory_space=pltpu.SMEM)


def place():
    m = lax.axis_index("mem")
    return lax.axis_index("dp"), m // 4, (m // 2) % 2, m % 2


def device(y, z, x, c):
    return {"dp": y, "mem": z * 4 + x * 2 + c}


def flip_z(z, d):
    return (z, z + 1 - 2 * (z % 2), (z + 2) % 4, 3 - z)[d]


def greet(targets):
    barrier = pltpu.get_barrier_semaphore()
    for target in targets:
        pl.semaphore_signal(barrier, inc=1, device_id=target, device_id_type=MESH)
    pl.semaphore_wait(barrier, len(targets))


def remote(src, dst, send, recv, target):
    return pltpu.make_async_remote_copy(
        src_ref=src, dst_ref=dst, send_sem=send, recv_sem=recv, device_id=target, device_id_type=MESH
    )


Y_FIRST = (False, True, False, True, False)
EARLY, LATE = (0, 4), (1, 2, 3)


def line_of(z):
    inner = ((z + 1) // 2) % 2
    near = flip_z(z, 1)
    second = 3 - (inner * z + (1 - inner) * near)
    third = 3 - (inner * near + (1 - inner) * z)
    return inner, (z, near, second, third)


def expand(packed, first, count):
    rows, lanes = packed.shape
    width = rows // 16 * count
    lane = lax.broadcasted_iota(jnp.int32, (lanes, width), 0)
    column = lax.broadcasted_iota(jnp.int32, (lanes, width), 1)
    pick = (lane == first + column % count).astype(BF16)
    wide = jnp.dot(packed, pick, preferred_element_type=F32)
    shard = lax.broadcasted_iota(jnp.int32, (rows, width), 0) // 16
    column = lax.broadcasted_iota(jnp.int32, (rows, width), 1) // count
    return jnp.sum(jnp.where(shard == column, wide, 0.0), axis=0, keepdims=True)


def rows_of(ref, block, count):
    return jnp.concatenate([ref[block + i] for i in range(count)], axis=0)


def window_bias(ref, block, count, start, stop):
    size = ref.shape[2]
    parts = []
    for i in range(count):
        spots = (block + i) * size + lax.broadcasted_iota(jnp.int32, (8, size), 1)
        inside = (spots >= start) & (spots < stop)
        parts.append(jnp.where(inside, ref[block + i], neg_big))
    return jnp.concatenate(parts, axis=1)[0:1]


def key_window(j, ranks, rank, docs, sizes, blocks):
    window = blocks // 2 + 1
    doc = docs[0, j * ranks + rank]
    start = 0
    stop = 0
    for i in range(sizes.shape[1]):
        size = sizes[0, i]
        start = start + size * (i < doc).astype(jnp.int32)
        stop = stop + size * (i <= doc).astype(jnp.int32)
    base = lax.min(lax.div(start, jnp.int32(KEYS)), jnp.int32(blocks - window))
    return start, stop, base, window


def columns(block):
    rows = block.shape[1]
    return jnp.concatenate([block, jnp.zeros((rows - 8, rows), F32)], axis=0).T


def front_kernel(own_rows, *refs):
    docs, sizes, lens = refs[:3]
    x_ref = refs[3]
    src = refs[4:9]
    keys, vals, bias = refs[9:12]
    first_out, o_low, att, tot, h_ref, q_ref, k_ref, v_ref, qh, gain_out = refs[12:22]
    dst = refs[22:27]
    kh, vh, bh = refs[27:30]
    oh, lh, mo, ml, loc, st = refs[30:36]
    own_sem, rs, zs, ys, xs, cs, ko, kr, ks, kcs, qs, qr, os_, or_ = refs[36:]
    y, z, x, c = place()
    m = z * 4 + x * 2 + c
    ranks = 2
    chip = z * 2 + x
    rows = x_ref.shape[0]
    width = x_ref.shape[1]
    total = kh.shape[0]
    per = keys.shape[0]
    factor = WIDTH ** (-0.5) * LOG2E
    inner, line = line_of(z)
    y_peer, x_peer, c_peer = device(1 - y, z, x, c), device(y, z, 1 - x, c), device(y, z, x, 1 - c)
    near, across = device(y, flip_z(z, 1), x, c), device(y, 3 - z, x, c)
    plane = [
        (flip_z(z, dz), x if dx == 0 else 1 - x) for dz in (3, 2, 1, 0) for dx in (1, 0) if dz or dx
    ]
    pending = []
    inner_pending = []

    def shard(yy, zz, xx, cc):
        return yy * 16 + zz * 4 + xx * 2 + cc

    def slot(p, s):
        return dst[p].at[s]

    me = shard(y, z, x, c)

    def go(copy):
        copy.start()
        pending.append(copy)

    def push(p, s, target, sem, source=None):
        go(remote(slot(p, s) if source is None else source, slot(p, s), sem, rs.at[s, p], target))

    def push_inner(jobs):
        copies = [
            remote(slot(p, s) if source is None else source, slot(p, s), sem, rs.at[s, p], target)
            for p, s, target, sem, source in jobs
        ]
        inner_pending.extend(copies)

        @pl.when(inner == 1)
        def _():
            for copy in copies:
                copy.start()

    def arrived(p, s):
        remote(slot(p, s), slot(p, s), own_sem.at[p], rs.at[s, p], c_peer).wait_recv()

    def own_sends(group):
        push_inner([(p, me, across, zs.at[0, p], src[p]) for p in group])
        for p in group:
            push(p, me, near, zs.at[1, p], src[p])
        for p in group:
            push(p, me, y_peer, ys.at[0, p], src[p])
            push(p, me, x_peer, xs.at[0, p], src[p])
            push(p, me, c_peer, cs.at[0, p], src[p])

    def line_event(i, group):
        s = shard(y, line[i], x, c)
        for p in group:
            arrived(p, s)
        if i == 1:
            push_inner([(p, s, across, zs.at[2, p], None) for p in group])
        else:
            push_inner([(p, s, near, zs.at[i + 1, p], None) for p in group])
        for p in group:
            push(p, s, y_peer, ys.at[i, p])
            push(p, s, x_peer, xs.at[i, p])
            push(p, s, c_peer, cs.at[i, p])

    def side_event(i, group):
        for p in group:
            s = shard(1 - y, line[i], x, c)
            arrived(p, s)
            if Y_FIRST[p]:
                push(p, s, x_peer, xs.at[4 + i, p])
            push(p, s, c_peer, cs.at[4 + i, p])
        for p in group:
            s = shard(y, line[i], 1 - x, c)
            arrived(p, s)
            if not Y_FIRST[p]:
                push(p, s, y_peer, ys.at[4 + i, p])
            push(p, s, c_peer, cs.at[8 + i, p])

    def corner_event(i, group):
        s = shard(1 - y, line[i], 1 - x, c)
        for p in group:
            arrived(p, s)
            push(p, s, c_peer, cs.at[12 + i, p])

    def core_events(group):
        for yy in (y, 1 - y):
            for zz in line:
                for xx in (x, 1 - x):
                    for p in group:
                        arrived(p, shard(yy, zz, xx, 1 - c))

    def block(ref, i):
        return ref.at[pl.ds(i * per, per)]

    def lanes(ref, i):
        at = pl.ds(pl.multiple_of(i * WIDTH, WIDTH), WIDTH)
        return ref.at[:, at] if len(ref.shape) == 2 else ref.at[:, :, at]

    greet([device(y, a, b, c) for a, b in plane] + [y_peer, c_peer])
    own_sends(EARLY)
    own_sends(LATE)
    homes = []
    for p in range(5):
        homes.append(pltpu.make_async_copy(src[p], slot(p, me), own_sem.at[p]))
    for p, (a, b) in enumerate(((lanes(keys, chip), kh), (lanes(vals, chip), vh), (bias, bh))):
        homes.append(pltpu.make_async_copy(a, block(b, m), ko.at[p]))
    for copy in homes:
        copy.start()

    inputs = x_ref[...].astype(F32)
    normed = inputs * lax.rsqrt(jnp.mean(inputs * inputs, axis=-1, keepdims=True) + epsilon)

    line_event(1, EARLY)
    side_event(0, EARLY)
    line_event(1, LATE)
    for i, (zz, xx) in enumerate(plane):
        head = zz * 2 + xx
        for p, (a, b) in enumerate(((lanes(keys, head), kh), (lanes(vals, head), vh), (bias, bh))):
            go(remote(a, block(b, m), ks.at[i, p], kr.at[m, p], device(y, zz, xx, c)))
    for p, (a, b) in enumerate(((lanes(keys, chip), kh), (lanes(vals, chip), vh), (bias, bh))):
        go(remote(a, block(b, m), kcs.at[7, p], kr.at[m, p], c_peer))
    side_event(0, LATE)
    line_event(2, EARLY)
    side_event(1, EARLY)
    line_event(3, EARLY)
    line_event(2, LATE)
    side_event(2, EARLY)
    side_event(1, LATE)
    side_event(3, EARLY)
    line_event(3, LATE)
    for i in range(4):
        corner_event(i, EARLY)
    core_events(EARLY)
    for copy in homes:
        copy.wait()

    packed = dst[4][...].reshape(32 * 16, 128)
    gain = expand(packed, 0, own_rows)
    gain_out[...] = jnp.concatenate(
        [gain, expand(packed, own_rows, own_rows), jnp.zeros((6, width), F32)], axis=0
    )
    low = (normed * gain).astype(BF16)
    h_ref[...] = low
    for i, ref in enumerate((q_ref, k_ref, v_ref)):
        weight = dst[0][:, :, i * width : (i + 1) * width].reshape(width, width)
        ref[...] = jnp.dot(low, weight, preferred_element_type=F32).astype(BF16)

    others = [(chip + d) % 8 for d in range(1, 8)]
    peers = [{"dp": y, "mem": o * ranks + c} for o in others]
    for d, (o, peer) in enumerate(zip(others, peers)):
        go(remote(lanes(q_ref, o), qh.at[chip], qs.at[d], qr.at[chip], peer))
    mine = pltpu.make_async_copy(lanes(q_ref, chip), qh.at[chip], ko.at[0])
    mine.start()

    below = lax.broadcasted_iota(jnp.int32, (rows, rows), 1)
    ok = (below <= lax.broadcasted_iota(jnp.int32, (rows, rows), 0)) & (below < lens[0, 0])
    lane = lax.broadcasted_iota(jnp.int32, (rows, 128), 1)
    tops = jnp.zeros((rows, 128), F32)
    sums = jnp.zeros((rows, 128), F32)
    for i in range(HEADS):
        at = slice(i * WIDTH, (i + 1) * WIDTH)
        s = lax.dot_general(
            q_ref[:, at], k_ref[:, at], (((1,), (1,)), ((), ())), preferred_element_type=F32
        )
        s = jnp.where(ok, s * factor, neg_big)
        top = jnp.max(s, axis=1, keepdims=True)
        p = jnp.exp2(s - top)
        tops = jnp.where(lane == i, top, tops)
        sums = jnp.where(lane == i, jnp.sum(p, axis=1, keepdims=True), sums)
        loc[:, at] = jnp.dot(p.astype(BF16), v_ref[:, at], preferred_element_type=F32)
    st[0] = tops
    st[1] = sums
    side_event(2, LATE)

    for i, (zz, xx) in reversed(list(enumerate(plane))):
        other = zz * 4 + xx * 2 + c
        for p, b in enumerate((kh, vh, bh)):
            view = block(b, other)
            remote(view, view, ko.at[p], kr.at[other, p], c_peer).wait_recv()
            go(remote(view, view, kcs.at[i, p], kr.at[other, p], c_peer))
    for zz, xx in [(z, x)] + plane[::-1]:
        other = zz * 4 + xx * 2 + 1 - c
        for p, b in enumerate((kh, vh, bh)):
            remote(block(b, other), block(b, other), ko.at[p], kr.at[other, p], c_peer).wait_recv()
    mine.wait()
    for o in others:
        remote(qh.at[o], qh.at[o], ko.at[0], qr.at[o], c_peer).wait_recv()

    def attend(d, _):
        j = (chip + d) % 8
        start, stop, base, window = key_window(j, ranks, c, docs, sizes, total)
        q = qh[j]
        parts = 3
        chunk = window // parts

        def step(t, carry):
            top, tsum, acc = carry
            at = base + t * chunk
            s = lax.dot_general(
                q, rows_of(kh, at, chunk), (((1,), (1,)), ((), ())), preferred_element_type=F32
            )
            s = s * factor + window_bias(bh, at, chunk, start, stop)
            best = jnp.maximum(top, jnp.max(s, axis=1, keepdims=True))
            p = jnp.exp2(s - best)
            keep = jnp.exp2(top - best)
            tsum = tsum * keep + jnp.sum(p, axis=1, keepdims=True)
            acc = acc * keep + jnp.dot(p.astype(BF16), rows_of(vh, at, chunk), preferred_element_type=F32)
            return best, tsum, acc

        top, tsum, acc = lax.fori_loop(
            0,
            parts,
            step,
            (jnp.full((rows, 1), neg_big, F32), jnp.zeros((rows, 1), F32), jnp.zeros((rows, WIDTH), F32)),
        )
        oh[j] = (acc / tsum).astype(BF16)
        lh[j] = jnp.broadcast_to(top + jnp.log2(tsum), (rows, rows)).T[0:8]
        return 0

    def answer(d):
        j = (chip + d) % 8
        peer = {"dp": y, "mem": j * ranks + c}
        go(remote(oh.at[j], lanes(mo, chip), os_.at[d, 0], or_.at[chip, 0], peer))
        go(remote(lh.at[j], ml.at[chip], os_.at[d, 1], or_.at[chip, 1], peer))

    lax.fori_loop(1, 3, attend, 0)
    answer(1)
    answer(2)
    side_event(3, LATE)
    lax.fori_loop(3, 5, attend, 0)
    answer(3)
    answer(4)
    lax.fori_loop(5, 7, attend, 0)
    answer(5)
    answer(6)
    corner_event(0, LATE)
    lax.fori_loop(7, 9, attend, 0)
    answer(7)
    backs = [
        pltpu.make_async_copy(oh.at[chip], lanes(mo, chip), ko.at[0]),
        pltpu.make_async_copy(lh.at[chip], ml.at[chip], ko.at[1]),
    ]
    for copy in backs:
        copy.start()
    corner_event(1, LATE)
    for o in others:
        remote(lanes(mo, o), lanes(mo, o), ko.at[0], or_.at[o, 0], c_peer).wait_recv()
        remote(ml.at[o], ml.at[o], ko.at[1], or_.at[o, 1], c_peer).wait_recv()
    for copy in backs:
        copy.wait()

    head_row = lax.broadcasted_iota(jnp.int32, (8, rows), 0)
    gathered = jnp.zeros((8, rows), F32)
    for i in range(HEADS):
        gathered = jnp.where(head_row == i, ml[i], gathered)
    mem_lse = columns(gathered)
    tops, sums = st[0], st[1]
    known = lane < HEADS
    loc_lse = jnp.where(known, tops + jnp.log2(jnp.where(known, sums, 1.0)), 0.0)
    best = jnp.maximum(loc_lse, mem_lse)
    whole = best + jnp.log2(jnp.exp2(loc_lse - best) + jnp.exp2(mem_lse - best))
    tot[...] = whole
    loc_scale = jnp.exp2(tops - whole)
    mem_scale = jnp.exp2(mem_lse - whole)
    for i in range(HEADS):
        at = slice(i * WIDTH, (i + 1) * WIDTH)
        value = loc[:, at] * loc_scale[:, i : i + 1] + mo[:, at].astype(F32) * mem_scale[:, i : i + 1]
        att[:, at] = value
        o_low[:, at] = value.astype(BF16)
    corner_event(2, LATE)
    corner_event(3, LATE)
    core_events(LATE)
    weight = dst[1][...].reshape(width, width)
    first_out[...] = x_ref[...].astype(F32) + jnp.dot(o_low[...], weight, preferred_element_type=F32)
    for copy in pending:
        copy.wait_send()

    @pl.when(inner == 1)
    def _():
        for copy in inner_pending:
            copy.wait_send()


def front(docs, sizes, lens, tokens, pieces, keys, values, bias, own_rows):
    dma = pltpu.SemaphoreType.DMA
    rows, width = tokens.shape
    total = keys.shape[0] * 16
    shape = jax.ShapeDtypeStruct
    wide = shape((rows, width), BF16)
    outs = [
        shape((rows, width), F32),
        wide,
        shape((rows, width), F32),
        shape((rows, 128), F32),
        wide,
        wide,
        wide,
        wide,
        shape((8, rows, WIDTH), BF16),
        shape((8, width), F32),
    ]
    outs += [shape((32,) + a.shape, a.dtype) for a in pieces]
    outs += [shape((total, KEYS, WIDTH), BF16)] * 2 + [shape((total, 8, KEYS), F32)]
    spaces = [VM] * 10 + [VM, VM, ANY, ANY, VM] + [VM] * 3
    return pl.pallas_call(
        functools.partial(front_kernel, own_rows),
        out_shape=outs,
        in_specs=[SM] * 3 + [VM] * 9,
        out_specs=spaces,
        scratch_shapes=[
            pltpu.VMEM((8, rows, WIDTH), BF16),
            pltpu.VMEM((8, 8, rows), F32),
            pltpu.VMEM((rows, width), BF16),
            pltpu.VMEM((8, 8, rows), F32),
            pltpu.VMEM((rows, width), F32),
            pltpu.VMEM((2, rows, 128), F32),
            dma((5,)),
            dma((32, 5)),
            dma((5, 5)),
            dma((8, 5)),
            dma((8, 5)),
            dma((16, 5)),
            dma((3,)),
            dma((16, 3)),
            dma((7, 3)),
            dma((8, 3)),
            dma((7,)),
            dma((8,)),
            dma((8, 2)),
            dma((8, 2)),
        ],
        compiler_params=pltpu.CompilerParams(
            collective_id=0, has_side_effects=True, vmem_limit_bytes=48 << 20
        ),
        name="front",
    )(docs, sizes, lens, tokens, *pieces, keys, values, bias)


def swap_kernel(kinds, ranks, *refs):
    n = len(kinds)
    srcs, dsts, (own, send, recv) = refs[:n], refs[n : 2 * n], refs[2 * n :]
    m = lax.axis_index("mem")
    y = lax.axis_index("dp")
    count = lax.axis_size("mem") // ranks
    rank, me = m % ranks, m // ranks

    def at(kind, ref, i, outside):
        wide = (kind == "heads") == outside
        if wide and len(ref.shape) == 2:
            return ref.at[:, pl.ds(pl.multiple_of(i * WIDTH, WIDTH), WIDTH)]
        return ref.at[i]

    others = [(me + d) % count for d in range(1, count)]
    targets = [{"dp": y, "mem": o * ranks + rank} for o in others]
    greet(targets)
    copies = []
    for d, (o, target) in enumerate(zip(others, targets)):
        for p, kind in enumerate(kinds):
            copy = remote(
                at(kind, srcs[p], o, True), at(kind, dsts[p], me, False), send.at[d, p], recv.at[me, p], target
            )
            copy.start()
            copies.append(copy)
    mine = []
    for p, kind in enumerate(kinds):
        copy = pltpu.make_async_copy(at(kind, srcs[p], me, True), at(kind, dsts[p], me, False), own.at[p])
        copy.start()
        mine.append(copy)
    for o, target in zip(others, targets):
        for p, kind in enumerate(kinds):
            view = at(kind, dsts[p], o, False)
            remote(view, view, own.at[p], recv.at[o, p], target).wait_recv()
    for copy in mine:
        copy.wait()
    for copy in copies:
        copy.wait_send()


def swap(kinds, arrays, outs, ranks, ident):
    dma = pltpu.SemaphoreType.DMA
    count = lax.axis_size("mem") // ranks
    n = len(kinds)
    return pl.pallas_call(
        functools.partial(swap_kernel, kinds, ranks),
        out_shape=outs,
        in_specs=[VM] * n,
        out_specs=[VM] * n,
        scratch_shapes=[dma((n,)), dma((count - 1, n)), dma((count, n))],
        compiler_params=pltpu.CompilerParams(
            collective_id=ident, has_side_effects=True, vmem_limit_bytes=16 << 20
        ),
        name=f"swap{ident}",
    )(*arrays)


def key_span(j, ranks, docs, sizes, rank_ref):
    doc = docs[0, j * ranks + rank_ref[0]]
    start = jnp.int32(0)
    stop = jnp.int32(0)
    for i in range(sizes.shape[1]):
        size = sizes[0, i]
        start = start + jnp.where(i < doc, size, 0)
        stop = stop + jnp.where(i <= doc, size, 0)
    return start, stop


def forward_kernel(ranks, block, docs, sizes, rank_ref, q_ref, k_ref, v_ref, bias_ref, o_ref, lse_ref):
    j = pl.program_id(0)
    start, stop = key_span(j, ranks, docs, sizes, rank_ref)
    q = q_ref[0]
    factor = WIDTH ** (-0.5) * LOG2E

    def step(b, carry):
        top, total, acc = carry
        s = lax.dot_general(
            q, rows_of(k_ref, b * block, block), (((1,), (1,)), ((), ())), preferred_element_type=F32
        )
        s = s * factor + window_bias(bias_ref, b * block, block, start, stop)
        best = jnp.maximum(top, jnp.max(s, axis=1, keepdims=True))
        p = jnp.exp2(s - best)
        keep = jnp.exp2(top - best)
        total = total * keep + jnp.sum(p, axis=1, keepdims=True)
        acc = acc * keep + jnp.dot(
            p.astype(BF16), rows_of(v_ref, b * block, block), preferred_element_type=F32
        )
        return best, total, acc

    rows = q.shape[0]
    top, total, acc = lax.fori_loop(
        start // (block * KEYS),
        (stop + block * KEYS - 1) // (block * KEYS),
        step,
        (jnp.full((rows, 1), neg_big, F32), jnp.zeros((rows, 1), F32), jnp.zeros((rows, WIDTH), F32)),
    )
    o_ref[0] = (acc / total).astype(BF16)
    lse = jnp.broadcast_to(top + jnp.log2(total), (rows, rows))
    lse_ref[0] = lse.T[0:8]


def backward_kernel(
    ranks, block, docs, sizes, rank_ref, q_ref, do_ref, stat_ref, k_ref, v_ref, bias_ref, dq_ref
):
    j = pl.program_id(0)
    start, stop = key_span(j, ranks, docs, sizes, rank_ref)
    q, do = q_ref[0], do_ref[0]
    rows = q.shape[0]
    factor = WIDTH ** (-0.5) * LOG2E
    stat = stat_ref[0]
    lse = jnp.broadcast_to(stat[0:1], (rows, rows)).T[:, 0:1]
    delta = jnp.broadcast_to(stat[1:2], (rows, rows)).T[:, 0:1]

    def step(b, acc):
        keys = rows_of(k_ref, b * block, block)
        s = lax.dot_general(q, keys, (((1,), (1,)), ((), ())), preferred_element_type=F32)
        p = jnp.exp2(s * factor + (window_bias(bias_ref, b * block, block, start, stop) - lse))
        dp = lax.dot_general(do, rows_of(v_ref, b * block, block), (((1,), (1,)), ((), ())), preferred_element_type=F32)
        ds = (p * (dp - delta)).astype(BF16)
        return acc + jnp.dot(ds, keys, preferred_element_type=F32)

    acc = lax.fori_loop(
        start // (block * KEYS), (stop + block * KEYS - 1) // (block * KEYS), step, jnp.zeros((rows, WIDTH), F32)
    )
    dq_ref[0] = (acc * WIDTH ** (-0.5)).astype(BF16)


def memory_forward(ranks, docs, sizes, rank, q, kh, vh, bh):
    count, rows, _ = q.shape
    seg = pl.BlockSpec((1, rows, WIDTH), lambda j: (j, 0, 0))
    stat = pl.BlockSpec((1, 8, rows), lambda j: (j, 0, 0))
    block = 8
    return pl.pallas_call(
        functools.partial(forward_kernel, ranks, block),
        grid=(count,),
        out_shape=[
            jax.ShapeDtypeStruct((count, rows, WIDTH), BF16),
            jax.ShapeDtypeStruct((count, 8, rows), F32),
        ],
        in_specs=[SM, SM, SM, seg, VM, VM, VM],
        out_specs=[seg, stat],
        compiler_params=pltpu.CompilerParams(vmem_limit_bytes=48 << 20),
        name="memory_forward",
    )(docs, sizes, rank, q, kh, vh, bh)


def memory_backward(ranks, docs, sizes, rank, q, do, stats, kh, vh, bh):
    count, rows, _ = q.shape
    seg = pl.BlockSpec((1, rows, WIDTH), lambda j: (j, 0, 0))
    stat = pl.BlockSpec((1, 8, rows), lambda j: (j, 0, 0))
    block = 8
    return pl.pallas_call(
        functools.partial(backward_kernel, ranks, block),
        grid=(count,),
        out_shape=jax.ShapeDtypeStruct((count, rows, WIDTH), BF16),
        in_specs=[SM, SM, SM, seg, seg, stat, VM, VM, VM],
        out_specs=seg,
        compiler_params=pltpu.CompilerParams(vmem_limit_bytes=48 << 20),
        name="memory_backward",
    )(docs, sizes, rank, q, do, stats, kh, vh, bh)


def reduce_kernel(*refs):
    h, dqkv, o, da, h2, dgu, hid, og, small = refs[:9]
    outs = refs[9:14]
    grads = refs[14:19]
    cores = refs[19:24]
    firsts = refs[24:29]
    seconds = refs[29:34]
    lines = refs[34:39]
    ht, ot, h2t, hidt = refs[39:43]
    cs, cr, fs, fr, ss, sr, zs, zr = refs[43:]
    n = 5
    y, z, x, c = place()
    y_peer, x_peer, c_peer = device(1 - y, z, x, c), device(y, z, 1 - x, c), device(y, z, x, 1 - c)
    greet([y_peer, x_peer, c_peer] + [device(y, flip_z(z, d), x, c) for d in (1, 2, 3)])
    ht[...] = h[...].T
    ot[...] = o[...].T
    h2t[...] = h2[...].T
    hidt[...] = hid[...].T
    pending = []

    def start(copy):
        copy.start()
        pending.append(copy)

    left = (ht, ot, h2t, hidt)
    right = (dqkv, da, dgu, og)
    order = [(k, d) for d in (3, 2, 1, 0) for k in (1, 0)]

    def unit(k, d):
        return (1 - y if k else y), flip_z(z, d)

    def produce(i):
        k, d = order[i]
        yy, zz = unit(k, d)
        u = yy * 4 + zz
        for p in range(4):
            rows = 4 * grads[p].shape[2]
            block = left[p][pl.ds(pl.multiple_of(u * rows, 32), rows), :]
            width = grads[p].shape[3]
            tile = 1024 if width % 1024 == 0 else 1408
            for t in range(0, width, tile):
                part = jnp.dot(block, right[p][:, t : t + tile], preferred_element_type=F32)
                grads[p][i, :, :, t : t + tile] = part.astype(BF16).reshape(4, rows // 4, tile)
        for q in range(4):
            grads[4][i, q] = small[u * 4 + q]
        for p in range(n):
            for xx in range(2):
                start(remote(grads[p].at[i, xx * 2 + 1 - c], cores[p].at[i, xx], cs.at[i, xx, p], cr.at[i, xx, p], c_peer))

    def wait(dst, sem):
        remote(dst, dst, cs.at[0, 0, 0], sem, c_peer).wait_recv()

    def merge(own, other):
        own[...] = (own[...].astype(F32) + other[...].astype(F32)).astype(own.dtype)

    def after_core(i):
        k, d = order[i]
        for p in range(n):
            for xx in (1 - x, x):
                own = grads[p].at[i, xx * 2 + c]
                wait(cores[p].at[i, xx], cr.at[i, xx, p])
                merge(own, cores[p].at[i, xx])
            if FIRST_BACK[p] == "x":
                start(remote(grads[p].at[i, (1 - x) * 2 + c], firsts[p].at[i], fs.at[i, 0, p], fr.at[i, 0, p], x_peer))
            elif k == 1:
                for xx in range(2):
                    start(remote(grads[p].at[i, xx * 2 + c], firsts[p].at[(i + 1) // 2 * 2 // 2 + 4 * xx], fs.at[i, xx, p], fr.at[i // 2, xx, p], y_peer))

    def after_first(i):
        k, d = order[i]
        for p in range(n):
            own = grads[p].at[i, x * 2 + c]
            if FIRST_BACK[p] == "x":
                wait(firsts[p].at[i], fr.at[i, 0, p])
                merge(own, firsts[p].at[i])
                if k == 1:
                    start(remote(own, seconds[p].at[i // 2], ss.at[i // 2, p], sr.at[i // 2, p], y_peer))
            elif k == 0:
                for xx in range(2):
                    wait(firsts[p].at[i // 2 + 4 * xx], fr.at[i // 2, xx, p])
                    merge(grads[p].at[i, xx * 2 + c], firsts[p].at[i // 2 + 4 * xx])
                start(remote(grads[p].at[i, (1 - x) * 2 + c], seconds[p].at[i // 2], ss.at[i // 2, p], sr.at[i // 2, p], x_peer))

    def after_second(i):
        k, d = order[i]
        if k == 1:
            return
        for p in range(n):
            own = grads[p].at[i, x * 2 + c]
            wait(seconds[p].at[i // 2], sr.at[i // 2, p])
            merge(own, seconds[p].at[i // 2])
            if d:
                start(remote(own, lines[p].at[d - 1], zs.at[d - 1, p], zr.at[d - 1, p], device(y, flip_z(z, d), x, c)))

    for t in range(8 + 6):
        if t < 8:
            produce(t)
        if 0 <= t - 1 < 8:
            after_core(t - 1)
        if 0 <= t - 3 < 8:
            after_first(t - 3)
        if 0 <= t - 5 < 8:
            after_second(t - 5)
    for p in range(n):
        total = grads[p][7, x * 2 + c].astype(F32)
        for d in (1, 2, 3):
            wait(lines[p].at[d - 1], zr.at[d - 1, p])
            total = total + lines[p][d - 1].astype(F32)
        outs[p][...] = total
    for copy in pending:
        copy.wait_send()


FIRST_BACK = ("y", "y", "x", "y", "x")


def reduce_call(h, dqkv, o, da, h2, dgu, hid, og, small):
    dma = pltpu.SemaphoreType.DMA
    rows, width = h.shape
    down = hid.shape[1] // 32
    own = width // 32
    shapes = [
        ((own, dqkv.shape[1]), BF16),
        ((own, da.shape[1]), BF16),
        ((own, dgu.shape[1]), BF16),
        ((down, og.shape[1]), BF16),
        (small.shape[1:], F32),
    ]

    def buffers(lead):
        return [
            pltpu.VMEM((lead(p) if isinstance(lead(p), tuple) else (lead(p),)) + s, t)
            for p, (s, t) in enumerate(shapes)
        ]

    return pl.pallas_call(
        reduce_kernel,
        out_shape=[jax.ShapeDtypeStruct(s, F32) for s, _ in shapes],
        in_specs=[VM] * 9,
        out_specs=[VM] * 5,
        scratch_shapes=buffers(lambda p: (8, 4))
        + buffers(lambda p: (8, 2))
        + buffers(lambda p: 8)
        + buffers(lambda p: 4)
        + buffers(lambda p: 3)
        + [
            pltpu.VMEM((width, rows), BF16),
            pltpu.VMEM((width, rows), BF16),
            pltpu.VMEM((width, rows), BF16),
            pltpu.VMEM((hid.shape[1], rows), BF16),
            dma((8, 2, 5)),
            dma((8, 2, 5)),
            dma((8, 2, 5)),
            dma((8, 2, 5)),
            dma((4, 5)),
            dma((4, 5)),
            dma((3, 5)),
            dma((3, 5)),
        ],
        compiler_params=pltpu.CompilerParams(
            collective_id=5, has_side_effects=True, vmem_limit_bytes=VMEM_MAX
        ),
        name="reduce",
    )(h, dqkv, o, da, h2, dgu, hid, og, small)


def gather_plain(pieces, keys, values, bias, ranks):
    full = [lax.all_gather(a, ("dp", "mem"), axis=0, tiled=False) for a in pieces]

    def spread(a):
        blocks = a.reshape(a.shape[0], HEADS, WIDTH).transpose(1, 0, 2)
        return lax.all_to_all(jnp.repeat(blocks, ranks, axis=0), "mem", 0, 0, tiled=True)

    return full + [
        spread(keys).reshape(-1, KEYS, WIDTH),
        spread(values).reshape(-1, KEYS, WIDTH),
        lax.all_gather(bias, "mem", axis=0, tiled=True),
    ]


def to_heads_plain(x, ranks):
    rank = lax.axis_index("mem") % ranks
    blocks = x if x.ndim == 3 else x.reshape(x.shape[0], HEADS, WIDTH).transpose(1, 0, 2)
    wide = jnp.where((jnp.arange(ranks) == rank)[None, :, None, None], blocks[:, None], 0)
    wide = wide.reshape((-1,) + blocks.shape[1:])
    got = lax.all_to_all(wide, "mem", 0, 0, tiled=True)
    return lax.dynamic_index_in_dim(got.reshape((-1, ranks) + blocks.shape[1:]), rank, 1, keepdims=False)


def to_tokens_plain(x, ranks, wide_out):
    rank = lax.axis_index("mem") % ranks
    wide = jnp.where((jnp.arange(ranks) == rank)[None, :, None, None], x[:, None], 0)
    got = lax.all_to_all(wide.reshape((-1,) + x.shape[1:]), "mem", 0, 0, tiled=True)
    got = lax.dynamic_index_in_dim(got.reshape((-1, ranks) + x.shape[1:]), rank, 1, keepdims=False)
    return got.transpose(1, 0, 2).reshape(x.shape[1], -1) if wide_out else got


def reduce_plain(h, dqkv, o, da, h2, dgu, hid, og, small):
    outs = []
    for a, b in ((h, dqkv), (o, da), (h2, dgu), (hid, og)):
        full = jnp.dot(a.T, b, preferred_element_type=F32)
        outs.append(lax.psum_scatter(full, ("dp", "mem"), scatter_dimension=0, tiled=True))
    outs.append(lax.psum_scatter(small, ("dp", "mem"), scatter_dimension=0, tiled=False))
    return outs


def normalize(values):
    inverse = lax.rsqrt(jnp.mean(values * values, axis=-1, keepdims=True) + epsilon)
    return (values * inverse, inverse)


def norm_back(grad_scaled, normed, inverse, gain_full):
    gain_grad = jnp.sum(grad_scaled * normed, axis=0)
    grad_normed = grad_scaled * gain_full
    grad_values = inverse * (
        grad_normed - normed * jnp.mean(grad_normed * normed, axis=-1, keepdims=True)
    )
    return (gain_grad, grad_values)


def shards(
    tokens,
    gain_attn,
    w_query,
    w_key,
    w_value,
    w_out,
    gain_ffn,
    w_gate,
    w_up,
    w_down,
    mem_keys,
    mem_values,
    out_grad,
    key_mask,
    mem_sizes,
    seg_doc,
    seg_len,
):
    seg_rows, model_width = tokens.shape
    mem_count = lax.axis_size("mem")
    dp_count = lax.axis_size("dp")
    devices = mem_count * dp_count
    ranks = mem_count // HEADS
    direct = dp_count == 2 and mem_count == 16
    factor = WIDTH ** (-0.5)
    ff_width = w_gate.shape[1]
    own = gain_attn.shape[0]
    down_rows = w_down.shape[0]

    pieces = [
        jnp.concatenate([w_query, w_key, w_value], axis=1),
        w_out,
        jnp.concatenate([w_gate, w_up], axis=1),
        w_down,
        jnp.pad(jnp.concatenate([gain_attn, gain_ffn])[None], ((0, 15), (0, 128 - 2 * own))),
    ]
    bias = jnp.where(key_mask == 1, 0.0, neg_big).astype(F32).reshape(-1, 1, KEYS)
    bias = jnp.broadcast_to(bias, (bias.shape[0], 8, KEYS))
    rank = (lax.axis_index("mem") % ranks).reshape(1).astype(jnp.int32)
    seg_count = mem_count // ranks
    block_shape = jax.ShapeDtypeStruct((seg_count, seg_rows, WIDTH), BF16)
    stat_shape = jax.ShapeDtypeStruct((seg_count, 8, seg_rows), F32)
    wide_shape = jax.ShapeDtypeStruct((seg_rows, model_width), BF16)
    inputs = tokens.astype(F32)
    normed_one, inverse_one = normalize(inputs)
    positions = lax.iota(jnp.int32, seg_rows)
    local_ok = ((positions[None, :] <= positions[:, None]) & (positions[None, :] < seg_len[0, 0]))[
        None
    ]

    if direct:
        split = (-1, KEYS, model_width)
        done = front(
            seg_doc, mem_sizes, seg_len, tokens, pieces, mem_keys.reshape(split), mem_values.reshape(split), bias, own
        )
        first, attended_low, attended, whole, normed_low, queries, keys_local, values_local = done[:8]
        q_heads, gains, joined_w, out_full, gate_up, down_full, _, kh, vh, bh = done[8:]
        gain_one, gain_two = gains[0], gains[1]
        attended = attended.reshape(seg_rows, HEADS, WIDTH)
        log_total = whole[:, :HEADS].T / LOG2E
    else:
        gathered = gather_plain(pieces, mem_keys, mem_values, bias, ranks)
        joined_w, out_full, gate_up, down_full, gains, kh, vh, bh = gathered
        gain_one = gains[:, 0, :own].reshape(-1).astype(F32)
        gain_two = gains[:, 0, own : 2 * own].reshape(-1).astype(F32)
    joined_w = joined_w.reshape(model_width, -1)
    out_full = out_full.reshape(model_width, -1)
    gate_up = gate_up.reshape(model_width, -1)
    down_full = down_full.reshape(ff_width, -1)
    if not direct:
        normed_low = (normed_one * gain_one).astype(BF16)
        projected = jnp.dot(normed_low, joined_w, preferred_element_type=F32).astype(BF16)
        queries = projected[:, :model_width]
        keys_local = projected[:, model_width : 2 * model_width]
        values_local = projected[:, 2 * model_width :]
    query_heads = queries.reshape(seg_rows, HEADS, WIDTH)
    key_heads = keys_local.reshape(seg_rows, HEADS, WIDTH)
    value_heads = values_local.reshape(seg_rows, HEADS, WIDTH)
    local_scores = (
        jnp.einsum("ihd,jhd->hij", query_heads, key_heads, preferred_element_type=F32) * factor
    )
    local_masked = jnp.where(local_ok, local_scores, neg_big)
    if not direct:
        q_heads = to_heads_plain(queries, ranks)
        o_mem, lse_mem = memory_forward(ranks, seg_doc, mem_sizes, rank, q_heads, kh, vh, bh)
        mem_o = to_tokens_plain(o_mem, ranks, True).reshape(seg_rows, HEADS, WIDTH).astype(F32)
        mem_lse = to_tokens_plain(lse_mem, ranks, False)[:, 0, :] / LOG2E
        local_top = jnp.max(local_masked, axis=2)
        local_total = jnp.sum(
            jnp.where(local_ok, jnp.exp(local_masked - local_top[:, :, None]), 0.0), axis=2
        )
        local_lse = local_top + jnp.log(local_total)
        best = jnp.maximum(local_lse, mem_lse)
        log_total = best + jnp.log(jnp.exp(local_lse - best) + jnp.exp(mem_lse - best))
    local_probs = jnp.where(local_ok, jnp.exp(local_masked - log_total[:, :, None]), 0.0)
    local_low = local_probs.astype(BF16)
    if not direct:
        attended = (
            jnp.einsum("hij,jhd->ihd", local_low, value_heads, preferred_element_type=F32)
            + mem_o * jnp.exp(mem_lse - log_total).T[..., None]
        )
        attended_low = attended.reshape(seg_rows, model_width).astype(BF16)
        first = inputs + jnp.dot(attended_low, out_full, preferred_element_type=F32)

    normed_two, inverse_two = normalize(first)
    normed_two_low = (normed_two * gain_two).astype(BF16)
    gate_upward = jnp.dot(normed_two_low, gate_up, preferred_element_type=F32)
    gate, upward = gate_upward[:, :ff_width], gate_upward[:, ff_width:]
    sigmoid_gate = jax.nn.sigmoid(gate)
    activated = gate * sigmoid_gate
    hidden = (activated * upward).astype(BF16)
    output = (first + jnp.dot(hidden, down_full, preferred_element_type=F32)).astype(BF16)
    grad_hidden = jnp.dot(out_grad, down_full.T, preferred_element_type=F32)
    grad_gate_up = jnp.concatenate(
        [
            (grad_hidden * upward * sigmoid_gate * (1.0 + gate * (1.0 - sigmoid_gate))).astype(BF16),
            (grad_hidden * activated).astype(BF16),
        ],
        axis=1,
    )
    grad_normed_two = jnp.dot(grad_gate_up, gate_up.T, preferred_element_type=F32)
    grad_gain_two, grad_first_norm = norm_back(grad_normed_two, normed_two, inverse_two, gain_two)
    grad_first = out_grad.astype(F32) + grad_first_norm

    grad_branch = grad_first.astype(BF16)
    grad_attended = jnp.dot(grad_branch, out_full.T, preferred_element_type=F32).astype(BF16)
    grad_att_heads = grad_attended.reshape(seg_rows, HEADS, WIDTH)
    delta = jnp.sum(grad_att_heads.astype(F32) * attended, axis=-1).T
    stats = jnp.pad(jnp.stack([log_total * LOG2E, delta], axis=1), ((0, 0), (0, 6), (0, 0)))
    if direct:
        do_heads, stat_heads = swap(
            ("heads", "heads"), (grad_attended, stats), (block_shape, stat_shape), ranks, 3
        )
    else:
        do_heads = to_heads_plain(grad_attended, ranks)
        stat_heads = to_heads_plain(stats, ranks)
    dq_heads = memory_backward(
        ranks, seg_doc, mem_sizes, rank, q_heads, do_heads, stat_heads, kh, vh, bh
    )
    if direct:
        (grad_query_memory,) = swap(("tokens",), (dq_heads,), (wide_shape,), ranks, 4)
    else:
        grad_query_memory = to_tokens_plain(dq_heads, ranks, True)

    grad_value_heads = jnp.einsum(
        "hij,ihd->jhd", local_low, grad_att_heads, preferred_element_type=F32
    )
    grad_local_probs = jnp.einsum(
        "ihd,jhd->hij", grad_att_heads, value_heads, preferred_element_type=F32
    )
    grad_local_scores = (local_probs * (grad_local_probs - delta[:, :, None])).astype(BF16)
    grad_query_heads = (
        jnp.einsum("hij,jhd->ihd", grad_local_scores, key_heads, preferred_element_type=F32)
        * factor
    )
    grad_key_heads = (
        jnp.einsum("hij,ihd->jhd", grad_local_scores, query_heads, preferred_element_type=F32)
        * factor
    )
    grad_queries = grad_query_heads.reshape(seg_rows, model_width) + grad_query_memory.astype(F32)
    grad_joined = jnp.concatenate(
        [
            grad_queries,
            grad_key_heads.reshape(seg_rows, model_width),
            grad_value_heads.reshape(seg_rows, model_width),
        ],
        axis=1,
    ).astype(BF16)
    grad_normed_one = jnp.dot(grad_joined, joined_w.T, preferred_element_type=F32)
    grad_gain_one, grad_input_norm = norm_back(grad_normed_one, normed_one, inverse_one, gain_one)
    input_grad = (grad_first + grad_input_norm).astype(BF16)

    small = jnp.stack([grad_gain_one.reshape(devices, own), grad_gain_two.reshape(devices, own)], axis=1)
    small = jnp.pad(small, ((0, 0), (0, 6), (0, 128 - own)))
    reducer = reduce_call if direct else reduce_plain
    attn_sums, out_sums, ffn_sums, down_sums, small_sums = reducer(
        normed_low, grad_joined, attended_low, grad_branch, normed_two_low, grad_gate_up, hidden, out_grad, small
    )
    return (
        output,
        input_grad,
        small_sums[0, :own],
        attn_sums[:, :model_width],
        attn_sums[:, model_width : 2 * model_width],
        attn_sums[:, 2 * model_width : 3 * model_width],
        out_sums,
        small_sums[1, :own],
        ffn_sums[:, :ff_width],
        ffn_sums[:, ff_width:],
        down_sums,
    )


def solution(mesh):
    rows = P(("dp", "mem"), None)
    vector = P(("dp", "mem"))
    in_specs = (
        (rows, vector) + (rows,) * 4 + (vector,) + (rows,) * 6
        + (P("dp", "mem"), P("dp", None), P("dp", None), P("dp", "mem"))
    )
    out_specs = (rows, rows, vector) + (rows,) * 4 + (vector,) + (rows,) * 3
    return jax.shard_map(shards, mesh=mesh, in_specs=in_specs, out_specs=out_specs, check_vma=False)
```

```python
import functools
import math

import jax
import jax.numpy as jnp
from jax import lax
from jax.experimental import pallas as pl
from jax.experimental.pallas import tpu as pltpu
from jax.sharding import PartitionSpec as P

HEADS = 8
WIDTH = 128
KEYS = 128
epsilon = 1e-05
neg_big = -1e30
LOG2E = 1.4426950408889634
VMEM_MAX = 67043328
MESH = pl.DeviceIdType.MESH
F32 = jnp.float32
BF16 = jnp.bfloat16

ANY = pl.BlockSpec(memory_space=pl.ANY)
VM = pl.BlockSpec(memory_space=pltpu.VMEM)
SM = pl.BlockSpec(memory_space=pltpu.SMEM)


def place():
    m = lax.axis_index("mem")
    return lax.axis_index("dp"), m // 4, (m // 2) % 2, m % 2


def device(y, z, x, c):
    return {"dp": y, "mem": z * 4 + x * 2 + c}


def flip_z(z, d):
    return (z, z + 1 - 2 * (z % 2), (z + 2) % 4, 3 - z)[d]


def greet(targets):
    barrier = pltpu.get_barrier_semaphore()
    for target in targets:
        pl.semaphore_signal(barrier, inc=1, device_id=target, device_id_type=MESH)
    pl.semaphore_wait(barrier, len(targets))


def remote(src, dst, send, recv, target):
    return pltpu.make_async_remote_copy(
        src_ref=src, dst_ref=dst, send_sem=send, recv_sem=recv, device_id=target, device_id_type=MESH
    )


Y_FIRST = (False, True, False, True, False)
EARLY, LATE = (0, 4), (1, 2, 3)


def line_of(z):
    inner = ((z + 1) // 2) % 2
    near = flip_z(z, 1)
    second = 3 - (inner * z + (1 - inner) * near)
    third = 3 - (inner * near + (1 - inner) * z)
    return inner, (z, near, second, third)


def expand(packed, first, count):
    rows, lanes = packed.shape
    width = rows // 16 * count
    lane = lax.broadcasted_iota(jnp.int32, (lanes, width), 0)
    column = lax.broadcasted_iota(jnp.int32, (lanes, width), 1)
    pick = (lane == first + column % count).astype(BF16)
    wide = jnp.dot(packed, pick, preferred_element_type=F32)
    shard = lax.broadcasted_iota(jnp.int32, (rows, width), 0) // 16
    column = lax.broadcasted_iota(jnp.int32, (rows, width), 1) // count
    return jnp.sum(jnp.where(shard == column, wide, 0.0), axis=0, keepdims=True)


def rows_of(ref, block, count):
    return jnp.concatenate([ref[block + i] for i in range(count)], axis=0)


def window_bias(ref, block, count, start, stop):
    size = ref.shape[2]
    parts = []
    for i in range(count):
        spots = (block + i) * size + lax.broadcasted_iota(jnp.int32, (8, size), 1)
        inside = (spots >= start) & (spots < stop)
        parts.append(jnp.where(inside, ref[block + i], neg_big))
    return jnp.concatenate(parts, axis=1)[0:1]


def key_window(j, ranks, rank, docs, sizes, blocks):
    window = blocks // 2 + 1
    doc = docs[0, j * ranks + rank]
    start = 0
    stop = 0
    for i in range(sizes.shape[1]):
        size = sizes[0, i]
        start = start + size * (i < doc).astype(jnp.int32)
        stop = stop + size * (i <= doc).astype(jnp.int32)
    base = lax.min(lax.div(start, jnp.int32(KEYS)), jnp.int32(blocks - window))
    return start, stop, base, window


def columns(block):
    rows = block.shape[1]
    return jnp.concatenate([block, jnp.zeros((rows - 8, rows), F32)], axis=0).T


def front_kernel(own_rows, *refs):
    docs, sizes, lens = refs[:3]
    x_ref = refs[3]
    src = refs[4:9]
    keys, vals, bias = refs[9:12]
    first_out, o_low, att, tot, h_ref, q_ref, k_ref, v_ref, qh, gain_out = refs[12:22]
    dst = refs[22:27]
    kh, vh, bh = refs[27:30]
    oh, lh, mo, ml, loc, st = refs[30:36]
    own_sem, rs, zs, ys, xs, cs, ko, kr, ks, kcs, qs, qr, os_, or_ = refs[36:]
    y, z, x, c = place()
    m = z * 4 + x * 2 + c
    ranks = 2
    chip = z * 2 + x
    rows = x_ref.shape[0]
    width = x_ref.shape[1]
    total = kh.shape[0]
    per = keys.shape[0]
    factor = WIDTH ** (-0.5) * LOG2E
    inner, line = line_of(z)
    y_peer, x_peer, c_peer = device(1 - y, z, x, c), device(y, z, 1 - x, c), device(y, z, x, 1 - c)
    near, across = device(y, flip_z(z, 1), x, c), device(y, 3 - z, x, c)
    plane = [
        (flip_z(z, dz), x if dx == 0 else 1 - x) for dz in (3, 2, 1, 0) for dx in (1, 0) if dz or dx
    ]
    pending = []
    inner_pending = []

    def shard(yy, zz, xx, cc):
        return yy * 16 + zz * 4 + xx * 2 + cc

    def slot(p, s):
        return dst[p].at[s]

    me = shard(y, z, x, c)

    def go(copy):
        copy.start()
        pending.append(copy)

    def push(p, s, target, sem, source=None):
        go(remote(slot(p, s) if source is None else source, slot(p, s), sem, rs.at[s, p], target))

    def push_inner(jobs):
        copies = [
            remote(slot(p, s) if source is None else source, slot(p, s), sem, rs.at[s, p], target)
            for p, s, target, sem, source in jobs
        ]
        inner_pending.extend(copies)

        @pl.when(inner == 1)
        def _():
            for copy in copies:
                copy.start()

    def arrived(p, s):
        remote(slot(p, s), slot(p, s), own_sem.at[p], rs.at[s, p], c_peer).wait_recv()

    def own_sends(group):
        push_inner([(p, me, across, zs.at[0, p], src[p]) for p in group])
        for p in group:
            push(p, me, near, zs.at[1, p], src[p])
        for p in group:
            push(p, me, y_peer, ys.at[0, p], src[p])
            push(p, me, x_peer, xs.at[0, p], src[p])
            push(p, me, c_peer, cs.at[0, p], src[p])

    def line_event(i, group):
        s = shard(y, line[i], x, c)
        for p in group:
            arrived(p, s)
        if i == 1:
            push_inner([(p, s, across, zs.at[2, p], None) for p in group])
        else:
            push_inner([(p, s, near, zs.at[i + 1, p], None) for p in group])
        for p in group:
            push(p, s, y_peer, ys.at[i, p])
            push(p, s, x_peer, xs.at[i, p])
            push(p, s, c_peer, cs.at[i, p])

    def side_event(i, group):
        for p in group:
            s = shard(1 - y, line[i], x, c)
            arrived(p, s)
            if Y_FIRST[p]:
                push(p, s, x_peer, xs.at[4 + i, p])
            push(p, s, c_peer, cs.at[4 + i, p])
        for p in group:
            s = shard(y, line[i], 1 - x, c)
            arrived(p, s)
            if not Y_FIRST[p]:
                push(p, s, y_peer, ys.at[4 + i, p])
            push(p, s, c_peer, cs.at[8 + i, p])

    def corner_event(i, group):
        s = shard(1 - y, line[i], 1 - x, c)
        for p in group:
            arrived(p, s)
            push(p, s, c_peer, cs.at[12 + i, p])

    def core_events(group):
        for yy in (y, 1 - y):
            for zz in line:
                for xx in (x, 1 - x):
                    for p in group:
                        arrived(p, shard(yy, zz, xx, 1 - c))

    def block(ref, i):
        return ref.at[pl.ds(i * per, per)]

    def lanes(ref, i):
        at = pl.ds(pl.multiple_of(i * WIDTH, WIDTH), WIDTH)
        return ref.at[:, at] if len(ref.shape) == 2 else ref.at[:, :, at]

    greet([device(y, a, b, c) for a, b in plane] + [y_peer, c_peer])
    own_sends(EARLY)
    own_sends(LATE)
    homes = []
    for p in range(5):
        homes.append(pltpu.make_async_copy(src[p], slot(p, me), own_sem.at[p]))
    for p, (a, b) in enumerate(((lanes(keys, chip), kh), (lanes(vals, chip), vh), (bias, bh))):
        homes.append(pltpu.make_async_copy(a, block(b, m), ko.at[p]))
    for copy in homes:
        copy.start()

    inputs = x_ref[...].astype(F32)
    normed = inputs * lax.rsqrt(jnp.mean(inputs * inputs, axis=-1, keepdims=True) + epsilon)

    line_event(1, EARLY)
    side_event(0, EARLY)
    line_event(1, LATE)
    for i, (zz, xx) in enumerate(plane):
        head = zz * 2 + xx
        for p, (a, b) in enumerate(((lanes(keys, head), kh), (lanes(vals, head), vh), (bias, bh))):
            go(remote(a, block(b, m), ks.at[i, p], kr.at[m, p], device(y, zz, xx, c)))
    for p, (a, b) in enumerate(((lanes(keys, chip), kh), (lanes(vals, chip), vh), (bias, bh))):
        go(remote(a, block(b, m), kcs.at[7, p], kr.at[m, p], c_peer))
    side_event(0, LATE)
    line_event(2, EARLY)
    side_event(1, EARLY)
    line_event(3, EARLY)
    line_event(2, LATE)
    side_event(2, EARLY)
    side_event(1, LATE)
    side_event(3, EARLY)
    line_event(3, LATE)
    for i in range(4):
        corner_event(i, EARLY)
    core_events(EARLY)
    for copy in homes:
        copy.wait()

    packed = dst[4][...].reshape(32 * 16, 128)
    gain = expand(packed, 0, own_rows)
    gain_out[...] = jnp.concatenate(
        [gain, expand(packed, own_rows, own_rows), jnp.zeros((6, width), F32)], axis=0
    )
    low = (normed * gain).astype(BF16)
    h_ref[...] = low
    for i, ref in enumerate((q_ref, k_ref, v_ref)):
        weight = dst[0][:, :, i * width : (i + 1) * width].reshape(width, width)
        ref[...] = jnp.dot(low, weight, preferred_element_type=F32).astype(BF16)

    others = [(chip + d) % 8 for d in range(1, 8)]
    peers = [{"dp": y, "mem": o * ranks + c} for o in others]
    for d, (o, peer) in enumerate(zip(others, peers)):
        go(remote(lanes(q_ref, o), qh.at[chip], qs.at[d], qr.at[chip], peer))
    mine = pltpu.make_async_copy(lanes(q_ref, chip), qh.at[chip], ko.at[0])
    mine.start()

    below = lax.broadcasted_iota(jnp.int32, (rows, rows), 1)
    ok = (below <= lax.broadcasted_iota(jnp.int32, (rows, rows), 0)) & (below < lens[0, 0])
    lane = lax.broadcasted_iota(jnp.int32, (rows, 128), 1)
    tops = jnp.zeros((rows, 128), F32)
    sums = jnp.zeros((rows, 128), F32)
    for i in range(HEADS):
        at = slice(i * WIDTH, (i + 1) * WIDTH)
        s = lax.dot_general(
            q_ref[:, at], k_ref[:, at], (((1,), (1,)), ((), ())), preferred_element_type=F32
        )
        s = jnp.where(ok, s * factor, neg_big)
        top = jnp.max(s, axis=1, keepdims=True)
        p = jnp.exp2(s - top)
        tops = jnp.where(lane == i, top, tops)
        sums = jnp.where(lane == i, jnp.sum(p, axis=1, keepdims=True), sums)
        loc[:, at] = jnp.dot(p.astype(BF16), v_ref[:, at], preferred_element_type=F32)
    st[0] = tops
    st[1] = sums
    side_event(2, LATE)

    for i, (zz, xx) in reversed(list(enumerate(plane))):
        other = zz * 4 + xx * 2 + c
        for p, b in enumerate((kh, vh, bh)):
            view = block(b, other)
            remote(view, view, ko.at[p], kr.at[other, p], c_peer).wait_recv()
            go(remote(view, view, kcs.at[i, p], kr.at[other, p], c_peer))
    for zz, xx in [(z, x)] + plane[::-1]:
        other = zz * 4 + xx * 2 + 1 - c
        for p, b in enumerate((kh, vh, bh)):
            remote(block(b, other), block(b, other), ko.at[p], kr.at[other, p], c_peer).wait_recv()
    mine.wait()
    for o in others:
        remote(qh.at[o], qh.at[o], ko.at[0], qr.at[o], c_peer).wait_recv()

    def attend(d, _):
        j = (chip + d) % 8
        start, stop, base, window = key_window(j, ranks, c, docs, sizes, total)
        q = qh[j]
        parts = 3
        chunk = window // parts

        def step(t, carry):
            top, tsum, acc = carry
            at = base + t * chunk
            s = lax.dot_general(
                q, rows_of(kh, at, chunk), (((1,), (1,)), ((), ())), preferred_element_type=F32
            )
            s = s * factor + window_bias(bh, at, chunk, start, stop)
            best = jnp.maximum(top, jnp.max(s, axis=1, keepdims=True))
            p = jnp.exp2(s - best)
            keep = jnp.exp2(top - best)
            tsum = tsum * keep + jnp.sum(p, axis=1, keepdims=True)
            acc = acc * keep + jnp.dot(p.astype(BF16), rows_of(vh, at, chunk), preferred_element_type=F32)
            return best, tsum, acc

        top, tsum, acc = lax.fori_loop(
            0,
            parts,
            step,
            (jnp.full((rows, 1), neg_big, F32), jnp.zeros((rows, 1), F32), jnp.zeros((rows, WIDTH), F32)),
        )
        oh[j] = (acc / tsum).astype(BF16)
        lh[j] = jnp.broadcast_to(top + jnp.log2(tsum), (rows, rows)).T[0:8]
        return 0

    def answer(d):
        j = (chip + d) % 8
        peer = {"dp": y, "mem": j * ranks + c}
        go(remote(oh.at[j], lanes(mo, chip), os_.at[d, 0], or_.at[chip, 0], peer))
        go(remote(lh.at[j], ml.at[chip], os_.at[d, 1], or_.at[chip, 1], peer))

    lax.fori_loop(1, 3, attend, 0)
    answer(1)
    answer(2)
    side_event(3, LATE)
    lax.fori_loop(3, 5, attend, 0)
    answer(3)
    answer(4)
    lax.fori_loop(5, 7, attend, 0)
    answer(5)
    answer(6)
    corner_event(0, LATE)
    lax.fori_loop(7, 9, attend, 0)
    answer(7)
    backs = [
        pltpu.make_async_copy(oh.at[chip], lanes(mo, chip), ko.at[0]),
        pltpu.make_async_copy(lh.at[chip], ml.at[chip], ko.at[1]),
    ]
    for copy in backs:
        copy.start()
    corner_event(1, LATE)
    for o in others:
        remote(lanes(mo, o), lanes(mo, o), ko.at[0], or_.at[o, 0], c_peer).wait_recv()
        remote(ml.at[o], ml.at[o], ko.at[1], or_.at[o, 1], c_peer).wait_recv()
    for copy in backs:
        copy.wait()

    head_row = lax.broadcasted_iota(jnp.int32, (8, rows), 0)
    gathered = jnp.zeros((8, rows), F32)
    for i in range(HEADS):
        gathered = jnp.where(head_row == i, ml[i], gathered)
    mem_lse = columns(gathered)
    tops, sums = st[0], st[1]
    known = lane < HEADS
    loc_lse = jnp.where(known, tops + jnp.log2(jnp.where(known, sums, 1.0)), 0.0)
    best = jnp.maximum(loc_lse, mem_lse)
    whole = best + jnp.log2(jnp.exp2(loc_lse - best) + jnp.exp2(mem_lse - best))
    tot[...] = whole
    loc_scale = jnp.exp2(tops - whole)
    mem_scale = jnp.exp2(mem_lse - whole)
    for i in range(HEADS):
        at = slice(i * WIDTH, (i + 1) * WIDTH)
        value = loc[:, at] * loc_scale[:, i : i + 1] + mo[:, at].astype(F32) * mem_scale[:, i : i + 1]
        att[:, at] = value
        o_low[:, at] = value.astype(BF16)
    corner_event(2, LATE)
    corner_event(3, LATE)
    core_events(LATE)
    weight = dst[1][...].reshape(width, width)
    first_out[...] = x_ref[...].astype(F32) + jnp.dot(o_low[...], weight, preferred_element_type=F32)
    for copy in pending:
        copy.wait_send()

    @pl.when(inner == 1)
    def _():
        for copy in inner_pending:
            copy.wait_send()


def front(docs, sizes, lens, tokens, pieces, keys, values, bias, own_rows):
    dma = pltpu.SemaphoreType.DMA
    rows, width = tokens.shape
    total = keys.shape[0] * 16
    shape = jax.ShapeDtypeStruct
    wide = shape((rows, width), BF16)
    outs = [
        shape((rows, width), F32),
        wide,
        shape((rows, width), F32),
        shape((rows, 128), F32),
        wide,
        wide,
        wide,
        wide,
        shape((8, rows, WIDTH), BF16),
        shape((8, width), F32),
    ]
    outs += [shape((32,) + a.shape, a.dtype) for a in pieces]
    outs += [shape((total, KEYS, WIDTH), BF16)] * 2 + [shape((total, 8, KEYS), F32)]
    spaces = [VM] * 10 + [VM, VM, ANY, ANY, VM] + [VM] * 3
    return pl.pallas_call(
        functools.partial(front_kernel, own_rows),
        out_shape=outs,
        in_specs=[SM] * 3 + [VM] * 9,
        out_specs=spaces,
        scratch_shapes=[
            pltpu.VMEM((8, rows, WIDTH), BF16),
            pltpu.VMEM((8, 8, rows), F32),
            pltpu.VMEM((rows, width), BF16),
            pltpu.VMEM((8, 8, rows), F32),
            pltpu.VMEM((rows, width), F32),
            pltpu.VMEM((2, rows, 128), F32),
            dma((5,)),
            dma((32, 5)),
            dma((5, 5)),
            dma((8, 5)),
            dma((8, 5)),
            dma((16, 5)),
            dma((3,)),
            dma((16, 3)),
            dma((7, 3)),
            dma((8, 3)),
            dma((7,)),
            dma((8,)),
            dma((8, 2)),
            dma((8, 2)),
        ],
        compiler_params=pltpu.CompilerParams(
            collective_id=0, has_side_effects=True, vmem_limit_bytes=48 << 20
        ),
        name="front",
    )(docs, sizes, lens, tokens, *pieces, keys, values, bias)


def key_span(j, ranks, docs, sizes, rank_ref):
    doc = docs[0, j * ranks + rank_ref[0]]
    start = jnp.int32(0)
    stop = jnp.int32(0)
    for i in range(sizes.shape[1]):
        size = sizes[0, i]
        start = start + jnp.where(i < doc, size, 0)
        stop = stop + jnp.where(i <= doc, size, 0)
    return start, stop


def forward_kernel(ranks, block, docs, sizes, rank_ref, q_ref, k_ref, v_ref, bias_ref, o_ref, lse_ref):
    j = pl.program_id(0)
    start, stop = key_span(j, ranks, docs, sizes, rank_ref)
    q = q_ref[0]
    factor = WIDTH ** (-0.5) * LOG2E

    def step(b, carry):
        top, total, acc = carry
        s = lax.dot_general(
            q, rows_of(k_ref, b * block, block), (((1,), (1,)), ((), ())), preferred_element_type=F32
        )
        s = s * factor + window_bias(bias_ref, b * block, block, start, stop)
        best = jnp.maximum(top, jnp.max(s, axis=1, keepdims=True))
        p = jnp.exp2(s - best)
        keep = jnp.exp2(top - best)
        total = total * keep + jnp.sum(p, axis=1, keepdims=True)
        acc = acc * keep + jnp.dot(
            p.astype(BF16), rows_of(v_ref, b * block, block), preferred_element_type=F32
        )
        return best, total, acc

    rows = q.shape[0]
    top, total, acc = lax.fori_loop(
        start // (block * KEYS),
        (stop + block * KEYS - 1) // (block * KEYS),
        step,
        (jnp.full((rows, 1), neg_big, F32), jnp.zeros((rows, 1), F32), jnp.zeros((rows, WIDTH), F32)),
    )
    o_ref[0] = (acc / total).astype(BF16)
    lse = jnp.broadcast_to(top + jnp.log2(total), (rows, rows))
    lse_ref[0] = lse.T[0:8]


def backward_kernel(
    ranks, block, docs, sizes, rank_ref, q_ref, do_ref, stat_ref, k_ref, v_ref, bias_ref, dq_ref
):
    j = pl.program_id(0)
    start, stop = key_span(j, ranks, docs, sizes, rank_ref)
    q, do = q_ref[0], do_ref[0]
    rows = q.shape[0]
    factor = WIDTH ** (-0.5) * LOG2E
    stat = stat_ref[0]
    lse = jnp.broadcast_to(stat[0:1], (rows, rows)).T[:, 0:1]
    delta = jnp.broadcast_to(stat[1:2], (rows, rows)).T[:, 0:1]

    def step(b, acc):
        keys = rows_of(k_ref, b * block, block)
        s = lax.dot_general(q, keys, (((1,), (1,)), ((), ())), preferred_element_type=F32)
        p = jnp.exp2(s * factor + (window_bias(bias_ref, b * block, block, start, stop) - lse))
        dp = lax.dot_general(do, rows_of(v_ref, b * block, block), (((1,), (1,)), ((), ())), preferred_element_type=F32)
        ds = (p * (dp - delta)).astype(BF16)
        return acc + jnp.dot(ds, keys, preferred_element_type=F32)

    acc = lax.fori_loop(
        start // (block * KEYS), (stop + block * KEYS - 1) // (block * KEYS), step, jnp.zeros((rows, WIDTH), F32)
    )
    dq_ref[0] = (acc * WIDTH ** (-0.5)).astype(BF16)


def memory_forward(ranks, docs, sizes, rank, q, kh, vh, bh):
    count, rows, _ = q.shape
    seg = pl.BlockSpec((1, rows, WIDTH), lambda j: (j, 0, 0))
    stat = pl.BlockSpec((1, 8, rows), lambda j: (j, 0, 0))
    block = 8
    return pl.pallas_call(
        functools.partial(forward_kernel, ranks, block),
        grid=(count,),
        out_shape=[
            jax.ShapeDtypeStruct((count, rows, WIDTH), BF16),
            jax.ShapeDtypeStruct((count, 8, rows), F32),
        ],
        in_specs=[SM, SM, SM, seg, VM, VM, VM],
        out_specs=[seg, stat],
        compiler_params=pltpu.CompilerParams(vmem_limit_bytes=48 << 20),
        name="memory_forward",
    )(docs, sizes, rank, q, kh, vh, bh)


def memory_backward(ranks, docs, sizes, rank, q, do, stats, kh, vh, bh):
    count, rows, _ = q.shape
    seg = pl.BlockSpec((1, rows, WIDTH), lambda j: (j, 0, 0))
    stat = pl.BlockSpec((1, 8, rows), lambda j: (j, 0, 0))
    block = 8
    return pl.pallas_call(
        functools.partial(backward_kernel, ranks, block),
        grid=(count,),
        out_shape=jax.ShapeDtypeStruct((count, rows, WIDTH), BF16),
        in_specs=[SM, SM, SM, seg, seg, stat, VM, VM, VM],
        out_specs=seg,
        compiler_params=pltpu.CompilerParams(vmem_limit_bytes=48 << 20),
        name="memory_backward",
    )(docs, sizes, rank, q, do, stats, kh, vh, bh)


FIRST_BACK = ("y", "y", "x", "y", "x")
DEPTH = 3


def contract(row, first, lanes):
    width = row.shape[1]
    count = width // 32
    shard = lax.broadcasted_iota(jnp.int32, (32, width), 0)
    column = lax.broadcasted_iota(jnp.int32, (32, width), 1)
    masked = jnp.where(column // count == shard, jnp.broadcast_to(row, (32, width)), 0.0)
    feature = lax.broadcasted_iota(jnp.int32, (width, lanes), 0)
    lane = lax.broadcasted_iota(jnp.int32, (width, lanes), 1)
    pick = (lane == first + feature % count).astype(F32)
    return jnp.dot(masked, pick, preferred_element_type=F32, precision=lax.Precision.HIGHEST)


def tiles_of(width):
    for count in (4, 3, 2, 1):
        if width % (count * 128) == 0 and width // count >= 512:
            return count, width // count
    return 1, width


def back_kernel(*refs):
    docs, sizes, lens = refs[:3]
    x_ref, gains, dy, gain_two_row, tot, att = refs[3:9]
    h, o, da, h2, dgu, hid, og, do = refs[9:17]
    q_ref, k_ref, v_ref, qh, kh, vh, bh = refs[17:24]
    weights = refs[24]
    g_q, g_k, g_v, g_o, g_gate, g_up, g_down, g_small, input_grad = refs[25:34]
    stage, cores, firsts, seconds, lines = (refs[34 + 5 * i : 39 + 5 * i] for i in range(5))
    ht, ot, h2t, hidt, dqkv, dql, small, sst, doh, sth, dqo, dqm, wbuf = refs[59:72]
    cs, cr, fs, fr, ss, sr, zs, zr, own, dsend, drecv, qsend, qrecv, wsem = refs[72:]
    y, z, x, c = place()
    ranks = 2
    chip = z * 2 + x
    rows, width = x_ref.shape
    factor = WIDTH ** (-0.5) * LOG2E
    y_peer, x_peer, c_peer = device(1 - y, z, x, c), device(y, z, 1 - x, c), device(y, z, x, 1 - c)
    others = [(chip + d) % 8 for d in range(1, 8)]
    peers = [{"dp": y, "mem": p * ranks + c} for p in others]
    pending = []

    def go(copy):
        copy.start()
        pending.append(copy)

    def wait(dst, sem):
        remote(dst, dst, own.at[0], sem, c_peer).wait_recv()

    def lanes(ref, i):
        return ref.at[:, pl.ds(pl.multiple_of(i * WIDTH, WIDTH), WIDTH)]

    greet(peers + [y_peer, c_peer])

    for d, (p, peer) in enumerate(zip(others, peers)):
        go(remote(lanes(do, p), doh.at[chip], dsend.at[d, 0], drecv.at[chip, 0], peer))
    lane = lax.broadcasted_iota(jnp.int32, (rows, 128), 1)
    deltas = jnp.zeros((rows, 128), F32)
    for i in range(HEADS):
        at = slice(i * WIDTH, (i + 1) * WIDTH)
        part = jnp.sum(do[:, at].astype(F32) * att[:, at], axis=1, keepdims=True)
        deltas = jnp.where(lane == i, part, deltas)
    tot_rows, delta_rows = tot[...].T, deltas.T
    head_row = lax.broadcasted_iota(jnp.int32, (8, rows), 0)
    for i in range(HEADS):
        sst[i] = jnp.where(head_row == 0, tot_rows[i : i + 1], delta_rows[i : i + 1])
    ht[...] = h[...].T
    ot[...] = o[...].T
    h2t[...] = h2[...].T
    hidt[...] = hid[...].T
    for d, (p, peer) in enumerate(zip(others, peers)):
        go(remote(sst.at[p], sth.at[chip], dsend.at[d, 1], drecv.at[chip, 1], peer))
    homes = [
        pltpu.make_async_copy(lanes(do, chip), doh.at[chip], own.at[1]),
        pltpu.make_async_copy(sst.at[chip], sth.at[chip], own.at[2]),
    ]
    for copy in homes:
        copy.start()

    left = (ht, ot, h2t, hidt)
    right = (dqkv, da, dgu, og)
    order = [(k, d) for d in (3, 2, 1, 0) for k in (1, 0)]

    def produce(i, group):
        k, d = order[i]
        u = (1 - y if k else y) * 4 + flip_z(z, d)
        for p in group:
            room = stage[p].at[i % DEPTH]
            if p == 4:
                for n in range(4):
                    room[n] = small[u * 4 + n]
            else:
                size = 4 * stage[p].shape[2]
                block = left[p][pl.ds(pl.multiple_of(u * size, 32), size), :]
                count, tile = tiles_of(stage[p].shape[3])

                def some(t, _):
                    at = pl.ds(pl.multiple_of(t * tile, 128), tile)
                    part = jnp.dot(block, right[p][:, at], preferred_element_type=F32)
                    room[:, :, at] = part.astype(BF16).reshape(4, size // 4, tile)
                    return 0

                lax.fori_loop(0, count, some, 0)
            for xx in range(2):
                core_copy(i, p, xx).start()

    def core_copy(i, p, xx):
        return remote(
            stage[p].at[i % DEPTH, xx * 2 + 1 - c], cores[p].at[i, xx], cs.at[i, xx, p], cr.at[i, xx, p], c_peer
        )

    def merge(into, other):
        count, tile = tiles_of(into.shape[1])

        def some(t, _):
            at = pl.ds(pl.multiple_of(t * tile, 128), tile)
            into[:, at] = (into[:, at].astype(F32) + other[:, at].astype(F32)).astype(into.dtype)
            return 0

        lax.fori_loop(0, count, some, 0)

    def after_core(i, group):
        k, d = order[i]
        for p in group:
            for xx in (1 - x, x):
                into = cores[p].at[i, xx]
                wait(into, cr.at[i, xx, p])
                merge(into, stage[p].at[i % DEPTH, xx * 2 + c])
            if FIRST_BACK[p] == "x":
                go(remote(cores[p].at[i, 1 - x], firsts[p].at[i], fs.at[i, 0, p], fr.at[i, 0, p], x_peer))
            elif k == 1:
                t = i // 2
                for xx in range(2):
                    go(remote(cores[p].at[i, xx], firsts[p].at[t + 4 * xx], fs.at[i, xx, p], fr.at[t, xx, p], y_peer))
            for xx in range(2):
                core_copy(i, p, xx).wait_send()

    def after_first(i, group):
        k, d = order[i]
        t = i // 2
        for p in group:
            mine = cores[p].at[i, x]
            if FIRST_BACK[p] == "x":
                wait(firsts[p].at[i], fr.at[i, 0, p])
                merge(mine, firsts[p].at[i])
                if k == 1:
                    go(remote(mine, seconds[p].at[t], ss.at[t, p], sr.at[t, p], y_peer))
            elif k == 0:
                for xx in (1 - x, x):
                    room = firsts[p].at[t + 4 * xx]
                    wait(room, fr.at[t, xx, p])
                    merge(cores[p].at[i, xx], room)
                go(remote(cores[p].at[i, 1 - x], seconds[p].at[t], ss.at[t, p], sr.at[t, p], x_peer))

    def after_second(i, group):
        k, d = order[i]
        t = i // 2
        for p in group:
            mine = cores[p].at[i, x]
            wait(seconds[p].at[t], sr.at[t, p])
            merge(mine, seconds[p].at[t])
            if d:
                go(
                    remote(
                        mine, lines[p].at[d - 1], zs.at[d - 1, p], zr.at[d - 1, p], device(y, flip_z(z, d), x, c)
                    )
                )

    def finish(group):
        for p in group:
            for d in (1, 2, 3):
                wait(lines[p].at[d - 1], zr.at[d - 1, p])
            outs = ((g_q, g_k, g_v), (g_o,), (g_gate, g_up), (g_down,), (g_small,))[p]
            span = cores[p].shape[3] // len(outs)
            for i, out in enumerate(outs):
                at = slice(i * span, (i + 1) * span)
                total = cores[p][7, x, :, at].astype(F32)
                for d in range(3):
                    total = total + lines[p][d, :, at].astype(F32)
                out[...] = total

    def attend(d, _):
        j = (chip + d) % 8
        start, stop, base, window = key_window(j, ranks, c, docs, sizes, kh.shape[0])
        q, dout, stat = qh[j], doh[j], sth[j]
        lse = jnp.broadcast_to(stat[0:1], (rows, rows)).T[:, 0:1]
        delta = jnp.broadcast_to(stat[1:2], (rows, rows)).T[:, 0:1]
        parts = 3
        chunk = window // parts

        def step(t, acc):
            at = base + t * chunk
            keys = rows_of(kh, at, chunk)
            s = lax.dot_general(q, keys, (((1,), (1,)), ((), ())), preferred_element_type=F32)
            p = jnp.exp2(s * factor + (window_bias(bh, at, chunk, start, stop) - lse))
            dp = lax.dot_general(
                dout, rows_of(vh, at, chunk), (((1,), (1,)), ((), ())), preferred_element_type=F32
            )
            ds = (p * (dp - delta)).astype(BF16)
            return acc + jnp.dot(ds, keys, preferred_element_type=F32)

        acc = lax.fori_loop(0, parts, step, jnp.zeros((rows, WIDTH), F32))
        dqo[j] = (acc * WIDTH ** (-0.5)).astype(BF16)
        return 0

    def answer(d):
        j = (chip + d) % 8
        go(remote(dqo.at[j], lanes(dqm, chip), qsend.at[d - 1], qrecv.at[chip], {"dp": y, "mem": j * ranks + c}))

    def load_weight(i):
        copy = pltpu.make_async_copy(weights.at[:, :, i * width : (i + 1) * width], wbuf.at[i % 2], wsem.at[i % 2])
        copy.start()
        return copy

    ffn, att_group = (2, 3, 1), (0, 4)
    produce(0, ffn)
    produce(1, ffn)
    after_core(0, ffn)
    produce(2, ffn)
    after_core(1, ffn)
    produce(3, ffn)
    after_core(2, ffn)

    below = lax.broadcasted_iota(jnp.int32, (rows, rows), 1)
    ok = (below <= lax.broadcasted_iota(jnp.int32, (rows, rows), 0)) & (below < lens[0, 0])
    for i in range(HEADS):
        at = slice(i * WIDTH, (i + 1) * WIDTH)
        q, k, v, dout = q_ref[:, at], k_ref[:, at], v_ref[:, at], do[:, at]
        s = lax.dot_general(q, k, (((1,), (1,)), ((), ())), preferred_element_type=F32)
        p = jnp.where(ok, jnp.exp2(s * factor - tot[:, i : i + 1]), 0.0)
        dp = lax.dot_general(dout, v, (((1,), (1,)), ((), ())), preferred_element_type=F32)
        ds = (p * (dp - deltas[:, i : i + 1])).astype(BF16)
        dql[:, at] = jnp.dot(ds, k, preferred_element_type=F32) * WIDTH ** (-0.5)
        dk = lax.dot_general(ds, q, (((0,), (0,)), ((), ())), preferred_element_type=F32) * WIDTH ** (-0.5)
        dv = lax.dot_general(p.astype(BF16), dout, (((0,), (0,)), ((), ())), preferred_element_type=F32)
        dqkv[:, width + i * WIDTH : width + (i + 1) * WIDTH] = dk.astype(BF16)
        dqkv[:, 2 * width + i * WIDTH : 2 * width + (i + 1) * WIDTH] = dv.astype(BF16)

    for copy in homes:
        copy.wait()
    for p in others:
        wait(doh.at[p], drecv.at[p, 0])
        wait(sth.at[p], drecv.at[p, 1])
    lax.fori_loop(1, 3, attend, 0)
    answer(1)
    answer(2)
    after_first(0, ffn)
    after_core(3, ffn)
    produce(4, ffn)
    lax.fori_loop(3, 5, attend, 0)
    answer(3)
    answer(4)
    after_first(1, ffn)
    after_core(4, ffn)
    produce(5, ffn)
    lax.fori_loop(5, 7, attend, 0)
    answer(5)
    answer(6)
    after_first(2, ffn)
    after_core(5, ffn)
    produce(6, ffn)
    lax.fori_loop(7, 9, attend, 0)
    answer(7)
    back = pltpu.make_async_copy(dqo.at[chip], lanes(dqm, chip), own.at[1])
    back.start()
    loads = [load_weight(0), load_weight(1)]
    after_first(3, ffn)
    after_second(1, ffn)
    after_core(6, ffn)
    produce(7, ffn)
    for p in others:
        wait(lanes(dqm, p), qrecv.at[p])
    back.wait()
    dqkv[:, :width] = (dql[...] + dqm[...].astype(F32)).astype(BF16)

    dh = jnp.zeros((rows, width), F32)
    for i in range(3):
        loads[i].wait()
        weight = wbuf[i % 2].reshape(width, width)
        dh = dh + lax.dot_general(
            dqkv[:, i * width : (i + 1) * width], weight, (((1,), (1,)), ((), ())), preferred_element_type=F32
        )
        if i == 0:
            loads.append(load_weight(2))
    inputs = x_ref[...].astype(F32)
    inverse = lax.rsqrt(jnp.mean(inputs * inputs, axis=-1, keepdims=True) + epsilon)
    normed = inputs * inverse
    pulled = contract(jnp.sum(dh * normed, axis=0, keepdims=True), 0, 128)
    pulled = pulled + contract(gain_two_row[...], width // 32, 128)
    small[...] = jnp.broadcast_to(pulled[:, None, :], small.shape)
    dn = dh * gains[0:1]
    input_grad[...] = (
        dy[...] + inverse * (dn - normed * jnp.mean(dn * normed, axis=-1, keepdims=True))
    ).astype(BF16)

    produce(0, att_group)
    produce(1, att_group)
    after_core(0, att_group)
    produce(2, att_group)
    after_core(1, att_group)
    after_core(7, ffn)
    after_first(4, ffn)
    produce(3, att_group)
    after_core(2, att_group)
    produce(4, att_group)
    after_core(3, att_group)
    after_first(5, ffn)
    after_second(3, ffn)
    produce(5, att_group)
    after_core(4, att_group)
    after_first(0, att_group)
    after_first(1, att_group)
    produce(6, att_group)
    after_core(5, att_group)
    after_first(6, ffn)
    after_first(2, att_group)
    after_first(3, att_group)
    produce(7, att_group)
    after_core(6, att_group)
    after_core(7, att_group)
    after_second(1, att_group)
    after_first(7, ffn)
    after_second(5, ffn)
    after_first(4, att_group)
    after_first(5, att_group)
    after_second(3, att_group)
    after_first(6, att_group)
    after_first(7, att_group)
    after_second(5, att_group)
    after_second(7, ffn)
    after_second(7, att_group)
    finish(ffn)
    finish(att_group)
    for copy in pending:
        copy.wait_send()


def back(scalars, f32_args, bf16_args, heads_args, weights):
    dma = pltpu.SemaphoreType.DMA
    x = f32_args[0]
    h, o, da, h2, dgu, hid, og, do = bf16_args
    rows, width = x.shape
    own = width // 32
    down = hid.shape[1] // 32
    shapes = [
        ((own, 3 * width), BF16),
        ((own, width), BF16),
        ((own, dgu.shape[1]), BF16),
        ((down, width), BF16),
        ((8, 128), F32),
    ]

    def buffers(*lead):
        return [pltpu.VMEM(lead + s, t) for s, t in shapes]

    shape = jax.ShapeDtypeStruct
    outs = [shape((own, width), F32)] * 4 + [shape((own, hid.shape[1]), F32)] * 2
    outs += [shape((down, width), F32), shape((8, 128), F32), shape((rows, width), BF16)]
    return pl.pallas_call(
        back_kernel,
        out_shape=outs,
        in_specs=[SM] * 3 + [VM] * 21 + [ANY],
        out_specs=[VM] * 9,
        scratch_shapes=buffers(DEPTH, 4)
        + buffers(8, 2)
        + buffers(8)
        + buffers(4)
        + buffers(3)
        + [
            pltpu.VMEM((width, rows), BF16),
            pltpu.VMEM((width, rows), BF16),
            pltpu.VMEM((width, rows), BF16),
            pltpu.VMEM((hid.shape[1], rows), BF16),
            pltpu.VMEM((rows, 3 * width), BF16),
            pltpu.VMEM((rows, width), F32),
            pltpu.VMEM((32, 8, 128), F32),
            pltpu.VMEM((8, 8, rows), F32),
            pltpu.VMEM((8, rows, WIDTH), BF16),
            pltpu.VMEM((8, 8, rows), F32),
            pltpu.VMEM((8, rows, WIDTH), BF16),
            pltpu.VMEM((rows, width), BF16),
            pltpu.VMEM((2, 32, own, width), BF16),
            dma((8, 2, 5)),
            dma((8, 2, 5)),
            dma((8, 2, 5)),
            dma((8, 2, 5)),
            dma((4, 5)),
            dma((4, 5)),
            dma((3, 5)),
            dma((3, 5)),
            dma((3,)),
            dma((7, 2)),
            dma((8, 2)),
            dma((7,)),
            dma((8,)),
            dma((2,)),
        ],
        compiler_params=pltpu.CompilerParams(
            collective_id=1, has_side_effects=True, vmem_limit_bytes=VMEM_MAX
        ),
        name="back",
    )(*scalars, *f32_args, *bf16_args, *heads_args, weights)


def gather_plain(pieces, keys, values, bias, ranks):
    full = [lax.all_gather(a, ("dp", "mem"), axis=0, tiled=False) for a in pieces]

    def spread(a):
        blocks = a.reshape(a.shape[0], HEADS, WIDTH).transpose(1, 0, 2)
        return lax.all_to_all(jnp.repeat(blocks, ranks, axis=0), "mem", 0, 0, tiled=True)

    return full + [
        spread(keys).reshape(-1, KEYS, WIDTH),
        spread(values).reshape(-1, KEYS, WIDTH),
        lax.all_gather(bias, "mem", axis=0, tiled=True),
    ]


def to_heads_plain(x, ranks):
    rank = lax.axis_index("mem") % ranks
    blocks = x if x.ndim == 3 else x.reshape(x.shape[0], HEADS, WIDTH).transpose(1, 0, 2)
    wide = jnp.where((jnp.arange(ranks) == rank)[None, :, None, None], blocks[:, None], 0)
    wide = wide.reshape((-1,) + blocks.shape[1:])
    got = lax.all_to_all(wide, "mem", 0, 0, tiled=True)
    return lax.dynamic_index_in_dim(got.reshape((-1, ranks) + blocks.shape[1:]), rank, 1, keepdims=False)


def to_tokens_plain(x, ranks, wide_out):
    rank = lax.axis_index("mem") % ranks
    wide = jnp.where((jnp.arange(ranks) == rank)[None, :, None, None], x[:, None], 0)
    got = lax.all_to_all(wide.reshape((-1,) + x.shape[1:]), "mem", 0, 0, tiled=True)
    got = lax.dynamic_index_in_dim(got.reshape((-1, ranks) + x.shape[1:]), rank, 1, keepdims=False)
    return got.transpose(1, 0, 2).reshape(x.shape[1], -1) if wide_out else got


def reduce_plain(h, dqkv, o, da, h2, dgu, hid, og, small):
    outs = []
    for a, b in ((h, dqkv), (o, da), (h2, dgu), (hid, og)):
        full = jnp.dot(a.T, b, preferred_element_type=F32)
        outs.append(lax.psum_scatter(full, ("dp", "mem"), scatter_dimension=0, tiled=True))
    outs.append(lax.psum_scatter(small, ("dp", "mem"), scatter_dimension=0, tiled=False))
    return outs


def normalize(values):
    inverse = lax.rsqrt(jnp.mean(values * values, axis=-1, keepdims=True) + epsilon)
    return (values * inverse, inverse)


def norm_back(grad_scaled, normed, inverse, gain_full):
    gain_grad = jnp.sum(grad_scaled * normed, axis=0)
    grad_normed = grad_scaled * gain_full
    grad_values = inverse * (
        grad_normed - normed * jnp.mean(grad_normed * normed, axis=-1, keepdims=True)
    )
    return (gain_grad, grad_values)


def shards(
    tokens,
    gain_attn,
    w_query,
    w_key,
    w_value,
    w_out,
    gain_ffn,
    w_gate,
    w_up,
    w_down,
    mem_keys,
    mem_values,
    out_grad,
    key_mask,
    mem_sizes,
    seg_doc,
    seg_len,
):
    seg_rows, model_width = tokens.shape
    mem_count = lax.axis_size("mem")
    dp_count = lax.axis_size("dp")
    devices = mem_count * dp_count
    ranks = mem_count // HEADS
    direct = dp_count == 2 and mem_count == 16
    factor = WIDTH ** (-0.5)
    ff_width = w_gate.shape[1]
    own = gain_attn.shape[0]
    down_rows = w_down.shape[0]

    pieces = [
        jnp.concatenate([w_query, w_key, w_value], axis=1),
        w_out,
        jnp.concatenate([w_gate, w_up], axis=1),
        w_down,
        jnp.pad(jnp.concatenate([gain_attn, gain_ffn])[None], ((0, 15), (0, 128 - 2 * own))),
    ]
    bias = jnp.where(key_mask == 1, 0.0, neg_big).astype(F32).reshape(-1, 1, KEYS)
    bias = jnp.broadcast_to(bias, (bias.shape[0], 8, KEYS))
    rank = (lax.axis_index("mem") % ranks).reshape(1).astype(jnp.int32)
    inputs = tokens.astype(F32)
    normed_one, inverse_one = normalize(inputs)
    if direct:
        split = (-1, KEYS, model_width)
        done = front(
            seg_doc, mem_sizes, seg_len, tokens, pieces, mem_keys.reshape(split), mem_values.reshape(split), bias, own
        )
        first, attended_low, attended, whole, normed_low, queries, keys_local, values_local = done[:8]
        q_heads, gains, joined_w, out_full, gate_up, down_full, _, kh, vh, bh = done[8:]
        gain_one, gain_two = gains[0], gains[1]
    else:
        gathered = gather_plain(pieces, mem_keys, mem_values, bias, ranks)
        joined_w, out_full, gate_up, down_full, gains, kh, vh, bh = gathered
        gain_one = gains[:, 0, :own].reshape(-1).astype(F32)
        gain_two = gains[:, 0, own : 2 * own].reshape(-1).astype(F32)
    joined_w = joined_w.reshape(model_width, -1)
    out_full = out_full.reshape(model_width, -1)
    gate_up = gate_up.reshape(model_width, -1)
    down_full = down_full.reshape(ff_width, -1)
    if not direct:
        normed_low = (normed_one * gain_one).astype(BF16)
        projected = jnp.dot(normed_low, joined_w, preferred_element_type=F32).astype(BF16)
        queries = projected[:, :model_width]
        keys_local = projected[:, model_width : 2 * model_width]
        values_local = projected[:, 2 * model_width :]
    if not direct:
        query_heads = queries.reshape(seg_rows, HEADS, WIDTH)
        key_heads = keys_local.reshape(seg_rows, HEADS, WIDTH)
        value_heads = values_local.reshape(seg_rows, HEADS, WIDTH)
        positions = lax.iota(jnp.int32, seg_rows)
        local_ok = (positions[None, :] <= positions[:, None]) & (positions[None, :] < seg_len[0, 0])
        local_ok = local_ok[None]
        local_scores = (
            jnp.einsum("ihd,jhd->hij", query_heads, key_heads, preferred_element_type=F32) * factor
        )
        local_masked = jnp.where(local_ok, local_scores, neg_big)
        q_heads = to_heads_plain(queries, ranks)
        o_mem, lse_mem = memory_forward(ranks, seg_doc, mem_sizes, rank, q_heads, kh, vh, bh)
        mem_o = to_tokens_plain(o_mem, ranks, True).reshape(seg_rows, HEADS, WIDTH).astype(F32)
        mem_lse = to_tokens_plain(lse_mem, ranks, False)[:, 0, :] / LOG2E
        local_top = jnp.max(local_masked, axis=2)
        local_total = jnp.sum(
            jnp.where(local_ok, jnp.exp(local_masked - local_top[:, :, None]), 0.0), axis=2
        )
        local_lse = local_top + jnp.log(local_total)
        best = jnp.maximum(local_lse, mem_lse)
        log_total = best + jnp.log(jnp.exp(local_lse - best) + jnp.exp(mem_lse - best))
        local_probs = jnp.where(local_ok, jnp.exp(local_masked - log_total[:, :, None]), 0.0)
        local_low = local_probs.astype(BF16)
        attended = (
            jnp.einsum("hij,jhd->ihd", local_low, value_heads, preferred_element_type=F32)
            + mem_o * jnp.exp(mem_lse - log_total).T[..., None]
        )
        attended_low = attended.reshape(seg_rows, model_width).astype(BF16)
        first = inputs + jnp.dot(attended_low, out_full, preferred_element_type=F32)

    normed_two, inverse_two = normalize(first)
    normed_two_low = (normed_two * gain_two).astype(BF16)
    gate_upward = jnp.dot(normed_two_low, gate_up, preferred_element_type=F32)
    gate, upward = gate_upward[:, :ff_width], gate_upward[:, ff_width:]
    sigmoid_gate = jax.nn.sigmoid(gate)
    activated = gate * sigmoid_gate
    hidden = (activated * upward).astype(BF16)
    output = (first + jnp.dot(hidden, down_full, preferred_element_type=F32)).astype(BF16)
    grad_hidden = jnp.dot(out_grad, down_full.T, preferred_element_type=F32)
    grad_gate_up = jnp.concatenate(
        [
            (grad_hidden * upward * sigmoid_gate * (1.0 + gate * (1.0 - sigmoid_gate))).astype(BF16),
            (grad_hidden * activated).astype(BF16),
        ],
        axis=1,
    )
    grad_normed_two = jnp.dot(grad_gate_up, gate_up.T, preferred_element_type=F32)
    grad_gain_two, grad_first_norm = norm_back(grad_normed_two, normed_two, inverse_two, gain_two)
    grad_first = out_grad.astype(F32) + grad_first_norm

    grad_branch = grad_first.astype(BF16)
    grad_attended = jnp.dot(grad_branch, out_full.T, preferred_element_type=F32).astype(BF16)
    if direct:
        g_q, g_k, g_v, g_o, g_gate, g_up, g_down, g_small, input_grad = back(
            (seg_doc, mem_sizes, seg_len),
            (tokens, gains, grad_first, grad_gain_two[None], whole, attended),
            (normed_low, attended_low, grad_branch, normed_two_low, grad_gate_up, hidden, out_grad, grad_attended),
            (queries, keys_local, values_local, q_heads, kh, vh, bh),
            done[10],
        )
        return (
            output,
            input_grad,
            g_small[0, :own],
            g_q,
            g_k,
            g_v,
            g_o,
            g_small[0, own : 2 * own],
            g_gate,
            g_up,
            g_down,
        )
    grad_att_heads = grad_attended.reshape(seg_rows, HEADS, WIDTH)
    delta = jnp.sum(grad_att_heads.astype(F32) * attended, axis=-1).T
    stats = jnp.pad(jnp.stack([log_total * LOG2E, delta], axis=1), ((0, 0), (0, 6), (0, 0)))
    do_heads = to_heads_plain(grad_attended, ranks)
    stat_heads = to_heads_plain(stats, ranks)
    dq_heads = memory_backward(
        ranks, seg_doc, mem_sizes, rank, q_heads, do_heads, stat_heads, kh, vh, bh
    )
    grad_query_memory = to_tokens_plain(dq_heads, ranks, True)

    grad_value_heads = jnp.einsum(
        "hij,ihd->jhd", local_low, grad_att_heads, preferred_element_type=F32
    )
    grad_local_probs = jnp.einsum(
        "ihd,jhd->hij", grad_att_heads, value_heads, preferred_element_type=F32
    )
    grad_local_scores = (local_probs * (grad_local_probs - delta[:, :, None])).astype(BF16)
    grad_query_heads = (
        jnp.einsum("hij,jhd->ihd", grad_local_scores, key_heads, preferred_element_type=F32)
        * factor
    )
    grad_key_heads = (
        jnp.einsum("hij,ihd->jhd", grad_local_scores, query_heads, preferred_element_type=F32)
        * factor
    )
    grad_queries = grad_query_heads.reshape(seg_rows, model_width) + grad_query_memory.astype(F32)
    grad_joined = jnp.concatenate(
        [
            grad_queries,
            grad_key_heads.reshape(seg_rows, model_width),
            grad_value_heads.reshape(seg_rows, model_width),
        ],
        axis=1,
    ).astype(BF16)
    grad_normed_one = jnp.dot(grad_joined, joined_w.T, preferred_element_type=F32)
    grad_gain_one, grad_input_norm = norm_back(grad_normed_one, normed_one, inverse_one, gain_one)
    input_grad = (grad_first + grad_input_norm).astype(BF16)

    small = jnp.stack([grad_gain_one.reshape(devices, own), grad_gain_two.reshape(devices, own)], axis=1)
    small = jnp.pad(small, ((0, 0), (0, 6), (0, 128 - own)))
    attn_sums, out_sums, ffn_sums, down_sums, small_sums = reduce_plain(
        normed_low, grad_joined, attended_low, grad_branch, normed_two_low, grad_gate_up, hidden, out_grad, small
    )
    return (
        output,
        input_grad,
        small_sums[0, :own],
        attn_sums[:, :model_width],
        attn_sums[:, model_width : 2 * model_width],
        attn_sums[:, 2 * model_width : 3 * model_width],
        out_sums,
        small_sums[1, :own],
        ffn_sums[:, :ff_width],
        ffn_sums[:, ff_width:],
        down_sums,
    )


def solution(mesh):
    rows = P(("dp", "mem"), None)
    vector = P(("dp", "mem"))
    in_specs = (
        (rows, vector) + (rows,) * 4 + (vector,) + (rows,) * 6
        + (P("dp", "mem"), P("dp", None), P("dp", None), P("dp", "mem"))
    )
    out_specs = (rows, rows, vector) + (rows,) * 4 + (vector,) + (rows,) * 3
    return jax.shard_map(shards, mesh=mesh, in_specs=in_specs, out_specs=out_specs, check_vma=False)
```

```python
import functools
import math

import jax
import jax.numpy as jnp
from jax import lax
from jax.experimental import pallas as pl
from jax.experimental.pallas import tpu as pltpu
from jax.sharding import PartitionSpec as P

HEADS = 8
WIDTH = 128
KEYS = 128
epsilon = 1e-05
neg_big = -1e30
LOG2E = 1.4426950408889634
VMEM_MAX = 67043328
MESH = pl.DeviceIdType.MESH
F32 = jnp.float32
BF16 = jnp.bfloat16

ANY = pl.BlockSpec(memory_space=pl.ANY)
VM = pl.BlockSpec(memory_space=pltpu.VMEM)
SM = pl.BlockSpec(memory_space=pltpu.SMEM)


def place():
    m = lax.axis_index("mem")
    return lax.axis_index("dp"), m // 4, (m // 2) % 2, m % 2


def device(y, z, x, c):
    return {"dp": y, "mem": z * 4 + x * 2 + c}


def flip_z(z, d):
    return (z, z + 1 - 2 * (z % 2), (z + 2) % 4, 3 - z)[d]


def greet(targets):
    barrier = pltpu.get_barrier_semaphore()
    for target in targets:
        pl.semaphore_signal(barrier, inc=1, device_id=target, device_id_type=MESH)
    pl.semaphore_wait(barrier, len(targets))


def remote(src, dst, send, recv, target):
    return pltpu.make_async_remote_copy(
        src_ref=src, dst_ref=dst, send_sem=send, recv_sem=recv, device_id=target, device_id_type=MESH
    )


EARLY, LATE = (0, 4), (1, 3, 2, 5)
CROSS = (0, 1, 4)


def line_of(z):
    inner = ((z + 1) // 2) % 2
    near = flip_z(z, 1)
    second = 3 - (inner * z + (1 - inner) * near)
    third = 3 - (inner * near + (1 - inner) * z)
    return inner, (z, near, second, third)


def expand(packed, first, count):
    rows, lanes = packed.shape
    width = rows // 16 * count
    lane = lax.broadcasted_iota(jnp.int32, (lanes, width), 0)
    column = lax.broadcasted_iota(jnp.int32, (lanes, width), 1)
    pick = (lane == first + column % count).astype(BF16)
    wide = jnp.dot(packed, pick, preferred_element_type=F32)
    shard = lax.broadcasted_iota(jnp.int32, (rows, width), 0) // 16
    column = lax.broadcasted_iota(jnp.int32, (rows, width), 1) // count
    return jnp.sum(jnp.where(shard == column, wide, 0.0), axis=0, keepdims=True)


def rows_of(ref, block, count):
    return jnp.concatenate([ref[block + i] for i in range(count)], axis=0)


def window_bias(ref, block, count, start, stop):
    size = ref.shape[2]
    parts = []
    for i in range(count):
        spots = (block + i) * size + lax.broadcasted_iota(jnp.int32, (8, size), 1)
        inside = (spots >= start) & (spots < stop)
        parts.append(jnp.where(inside, ref[block + i], neg_big))
    return jnp.concatenate(parts, axis=1)[0:1]


def key_window(j, ranks, rank, docs, sizes, blocks):
    window = blocks // 2 + 1
    doc = docs[0, j * ranks + rank]
    start = 0
    stop = 0
    for i in range(sizes.shape[1]):
        size = sizes[0, i]
        start = start + size * (i < doc).astype(jnp.int32)
        stop = stop + size * (i <= doc).astype(jnp.int32)
    base = lax.min(lax.div(start, jnp.int32(KEYS)), jnp.int32(blocks - window))
    return start, stop, base, window


def columns(block):
    rows = block.shape[1]
    return jnp.concatenate([block, jnp.zeros((rows - 8, rows), F32)], axis=0).T


def front_kernel(own_rows, *refs):
    docs, sizes, lens = refs[:3]
    x_ref, og = refs[3:5]
    src = refs[5:10]
    keys, vals, bias = refs[10:13]
    first_out, o_low, att, tot, h_ref, q_ref, k_ref, v_ref, qh, gain_out, h2c, ogc = refs[13:25]
    dst = refs[25:30]
    kh, vh, bh = refs[30:33]
    oh, lh, mo, ml, loc, st = refs[33:39]
    own_sem, rs, sends, ko, kr, ks, kcs, qs, qr, os_, or_, pair = refs[39:]
    y, z, x, c = place()
    m = z * 4 + x * 2 + c
    ranks = 2
    chip = z * 2 + x
    rows = x_ref.shape[0]
    width = x_ref.shape[1]
    total = kh.shape[0]
    per = keys.shape[0]
    factor = WIDTH ** (-0.5) * LOG2E
    inner, line = line_of(z)
    y_peer, x_peer, c_peer = device(1 - y, z, x, c), device(y, z, 1 - x, c), device(y, z, x, 1 - c)
    near, across = device(y, flip_z(z, 1), x, c), device(y, 3 - z, x, c)
    plane = [
        (flip_z(z, dz), x if dx == 0 else 1 - x) for dz in (3, 2, 1, 0) for dx in (1, 0) if dz or dx
    ]
    pending = []
    inner_pending = []
    used = [0]

    def next_sem():
        used[0] += 1
        return sends.at[used[0] - 1]

    def go(copy):
        copy.start()
        pending.append(copy)

    def spot(p, zz, xx, cc, far=False):
        n = zz * 4 + xx * 2 + cc
        if p == 3:
            return dst[3].at[n], rs.at[n, 3]
        n = n + 16 * (1 - y if far or p == 5 else y)
        p = 2 if p == 5 else p
        return dst[p].at[n], rs.at[n, p]

    def push(place, target, source=None):
        view, sem = place
        go(remote(view if source is None else source, view, next_sem(), sem, target))

    def push_inner(jobs, target):
        copies = [
            remote(view if source is None else source, view, next_sem(), sem, target)
            for (view, sem), source in jobs
        ]
        inner_pending.extend(copies)

        @pl.when(inner == 1)
        def _():
            for copy in copies:
                copy.start()

    def arrived(place):
        view, sem = place
        remote(view, view, own_sem.at[0], sem, c_peer).wait_recv()

    def own_sends(group):
        jobs = []
        for p in group:
            source = None if p == 5 else src[2].at[y] if p == 2 else src[p]
            jobs.append((spot(p, z, x, c), source, p))
        push_inner([job[:2] for job in jobs], across)
        for view, source, p in jobs:
            push(view, near, source)
        for view, source, p in jobs:
            if p in CROSS:
                push(view, y_peer, source)
            push(view, x_peer, source)
            push(view, c_peer, source)

    def mirror():
        arrived(spot(5, z, x, c))
        own_sends((5,))

    def line_event(i, group):
        views = [(spot(p, line[i], x, c), p) for p in group]
        for view, p in views:
            arrived(view)
        push_inner([(view, None) for view, p in views], across if i == 1 else near)
        for view, p in views:
            if p in CROSS:
                push(view, y_peer)
            push(view, x_peer)
            push(view, c_peer)

    def x_event(i, group):
        for p in group:
            view = spot(p, line[i], 1 - x, c)
            arrived(view)
            if p in CROSS:
                push(view, y_peer)
            push(view, c_peer)

    def y_event(i, group):
        for p in group:
            view = spot(p, line[i], x, c, True)
            arrived(view)
            push(view, c_peer)

    def corner_event(i, group):
        for p in group:
            view = spot(p, line[i], 1 - x, c, True)
            arrived(view)
            push(view, c_peer)

    def core_events(group):
        for p in group:
            for far in (False, True) if p in CROSS else (False,):
                for zz in line:
                    for xx in (x, 1 - x):
                        arrived(spot(p, zz, xx, 1 - c, far))

    def block(ref, i):
        return ref.at[pl.ds(i * per, per)]

    def lanes(ref, i):
        at = pl.ds(pl.multiple_of(i * WIDTH, WIDTH), WIDTH)
        return ref.at[:, at] if len(ref.shape) == 2 else ref.at[:, :, at]

    memory = []
    for i, (zz, xx) in enumerate(plane):
        head = zz * 2 + xx
        for p, (a, b) in enumerate(((lanes(keys, head), kh), (lanes(vals, head), vh), (bias, bh))):
            memory.append(remote(a, block(b, m), ks.at[i, p], kr.at[m, p], device(y, zz, xx, c)))

    greet([device(y, a, b, c) for a, b in plane] + [y_peer, c_peer])
    own_sends(EARLY)
    push(spot(2, z, x, c), y_peer, src[2].at[1 - y])
    go(remote(og, ogc.at[1], pair.at[0], pair.at[1], y_peer))
    homes = [
        pltpu.make_async_copy(src[2].at[y] if p == 2 else src[p], spot(p, z, x, c)[0], own_sem.at[p])
        for p in range(5)
    ]
    for p, (a, b) in enumerate(((lanes(keys, chip), kh), (lanes(vals, chip), vh), (bias, bh))):
        homes.append(pltpu.make_async_copy(a, block(b, m), ko.at[p]))
    homes.append(pltpu.make_async_copy(og, ogc.at[0], own_sem.at[5]))
    for copy in homes:
        copy.start()

    @pl.when(inner == 0)
    def _():
        for copy in memory:
            copy.start()

    inputs = x_ref[...].astype(F32)
    normed = inputs * lax.rsqrt(jnp.mean(inputs * inputs, axis=-1, keepdims=True) + epsilon)

    line_event(1, EARLY)
    y_event(0, EARLY)
    line_event(2, EARLY)
    line_event(3, EARLY)

    @pl.when(inner == 1)
    def _():
        for copy in memory:
            copy.start()

    for p, (a, b) in enumerate(((lanes(keys, chip), kh), (lanes(vals, chip), vh), (bias, bh))):
        go(remote(a, block(b, m), kcs.at[7, p], kr.at[m, p], c_peer))
    own_sends((1, 3, 2))
    mirror()
    x_event(0, EARLY)
    for i in (1, 2, 3):
        y_event(i, EARLY)
    for i in (1, 2, 3):
        x_event(i, EARLY)
    for i in range(4):
        corner_event(i, EARLY)
    core_events(EARLY)
    for copy in homes:
        copy.wait()

    packed = dst[4][...].reshape(32 * 16, 128)
    gain = expand(packed, 0, own_rows)
    gain_out[...] = jnp.concatenate(
        [gain, expand(packed, own_rows, own_rows), jnp.zeros((6, width), F32)], axis=0
    )
    low = (normed * gain).astype(BF16)
    h_ref[...] = low
    for i, ref in enumerate((q_ref, k_ref, v_ref)):
        weight = dst[0][:, :, i * width : (i + 1) * width].reshape(width, width)
        ref[...] = jnp.dot(low, weight, preferred_element_type=F32).astype(BF16)

    others = [(chip + d) % 8 for d in range(1, 8)]
    peers = [{"dp": y, "mem": o * ranks + c} for o in others]
    for d, (o, peer) in enumerate(zip(others, peers)):
        go(remote(lanes(q_ref, o), qh.at[chip], qs.at[d], qr.at[chip], peer))
    mine = pltpu.make_async_copy(lanes(q_ref, chip), qh.at[chip], ko.at[0])
    mine.start()

    below = lax.broadcasted_iota(jnp.int32, (rows, rows), 1)
    ok = (below <= lax.broadcasted_iota(jnp.int32, (rows, rows), 0)) & (below < lens[0, 0])
    lane = lax.broadcasted_iota(jnp.int32, (rows, 128), 1)
    tops = jnp.zeros((rows, 128), F32)
    sums = jnp.zeros((rows, 128), F32)
    for i in range(HEADS):
        at = slice(i * WIDTH, (i + 1) * WIDTH)
        s = lax.dot_general(
            q_ref[:, at], k_ref[:, at], (((1,), (1,)), ((), ())), preferred_element_type=F32
        )
        s = jnp.where(ok, s * factor, neg_big)
        top = jnp.max(s, axis=1, keepdims=True)
        p = jnp.exp2(s - top)
        tops = jnp.where(lane == i, top, tops)
        sums = jnp.where(lane == i, jnp.sum(p, axis=1, keepdims=True), sums)
        loc[:, at] = jnp.dot(p.astype(BF16), v_ref[:, at], preferred_element_type=F32)
    st[0] = tops
    st[1] = sums
    y_event(0, (1,))
    line_event(1, LATE)
    x_event(0, LATE)

    for i, (zz, xx) in reversed(list(enumerate(plane))):
        other = zz * 4 + xx * 2 + c
        for p, b in enumerate((kh, vh, bh)):
            view = block(b, other)
            remote(view, view, ko.at[p], kr.at[other, p], c_peer).wait_recv()
            go(remote(view, view, kcs.at[i, p], kr.at[other, p], c_peer))
    for zz, xx in [(z, x)] + plane[::-1]:
        other = zz * 4 + xx * 2 + 1 - c
        for p, b in enumerate((kh, vh, bh)):
            remote(block(b, other), block(b, other), ko.at[p], kr.at[other, p], c_peer).wait_recv()
    mine.wait()
    for o in others:
        remote(qh.at[o], qh.at[o], ko.at[0], qr.at[o], c_peer).wait_recv()

    def attend(d, _):
        j = (chip + d) % 8
        start, stop, base, window = key_window(j, ranks, c, docs, sizes, total)
        q = qh[j]
        parts = 3
        chunk = window // parts

        def step(t, carry):
            top, tsum, acc = carry
            at = base + t * chunk
            s = lax.dot_general(
                q, rows_of(kh, at, chunk), (((1,), (1,)), ((), ())), preferred_element_type=F32
            )
            s = s * factor + window_bias(bh, at, chunk, start, stop)
            best = jnp.maximum(top, jnp.max(s, axis=1, keepdims=True))
            p = jnp.exp2(s - best)
            keep = jnp.exp2(top - best)
            tsum = tsum * keep + jnp.sum(p, axis=1, keepdims=True)
            acc = acc * keep + jnp.dot(p.astype(BF16), rows_of(vh, at, chunk), preferred_element_type=F32)
            return best, tsum, acc

        top, tsum, acc = lax.fori_loop(
            0,
            parts,
            step,
            (jnp.full((rows, 1), neg_big, F32), jnp.zeros((rows, 1), F32), jnp.zeros((rows, WIDTH), F32)),
        )
        oh[j] = (acc / tsum).astype(BF16)
        lh[j] = jnp.broadcast_to(top + jnp.log2(tsum), (rows, rows)).T[0:8]
        return 0

    def answer(d):
        j = (chip + d) % 8
        peer = {"dp": y, "mem": j * ranks + c}
        go(remote(oh.at[j], lanes(mo, chip), os_.at[d, 0], or_.at[chip, 0], peer))
        go(remote(lh.at[j], ml.at[chip], os_.at[d, 1], or_.at[chip, 1], peer))

    lax.fori_loop(1, 3, attend, 0)
    answer(1)
    answer(2)
    line_event(2, LATE)
    lax.fori_loop(3, 5, attend, 0)
    answer(3)
    answer(4)
    x_event(1, LATE)
    line_event(3, LATE)
    lax.fori_loop(5, 7, attend, 0)
    answer(5)
    answer(6)
    x_event(2, LATE)
    lax.fori_loop(7, 9, attend, 0)
    answer(7)
    backs = [
        pltpu.make_async_copy(oh.at[chip], lanes(mo, chip), ko.at[0]),
        pltpu.make_async_copy(lh.at[chip], ml.at[chip], ko.at[1]),
    ]
    for copy in backs:
        copy.start()
    for i in (1, 2, 3):
        y_event(i, (1,))
    x_event(3, LATE)
    for i in range(4):
        corner_event(i, (1,))
    for o in others:
        remote(lanes(mo, o), lanes(mo, o), ko.at[0], or_.at[o, 0], c_peer).wait_recv()
        remote(ml.at[o], ml.at[o], ko.at[1], or_.at[o, 1], c_peer).wait_recv()
    for copy in backs:
        copy.wait()

    head_row = lax.broadcasted_iota(jnp.int32, (8, rows), 0)
    gathered = jnp.zeros((8, rows), F32)
    for i in range(HEADS):
        gathered = jnp.where(head_row == i, ml[i], gathered)
    mem_lse = columns(gathered)
    tops, sums = st[0], st[1]
    known = lane < HEADS
    loc_lse = jnp.where(known, tops + jnp.log2(jnp.where(known, sums, 1.0)), 0.0)
    best = jnp.maximum(loc_lse, mem_lse)
    whole = best + jnp.log2(jnp.exp2(loc_lse - best) + jnp.exp2(mem_lse - best))
    tot[...] = whole
    loc_scale = jnp.exp2(tops - whole)
    mem_scale = jnp.exp2(mem_lse - whole)
    for i in range(HEADS):
        at = slice(i * WIDTH, (i + 1) * WIDTH)
        value = loc[:, at] * loc_scale[:, i : i + 1] + mo[:, at].astype(F32) * mem_scale[:, i : i + 1]
        att[:, at] = value
        o_low[:, at] = value.astype(BF16)
    core_events((1,))
    weight = dst[1][...].reshape(width, width)
    first = x_ref[...].astype(F32) + jnp.dot(o_low[...], weight, preferred_element_type=F32)
    first_out[...] = first
    normed_two = first * lax.rsqrt(jnp.mean(first * first, axis=-1, keepdims=True) + epsilon)
    h2c[0] = (normed_two * gain_out[1:2]).astype(BF16)
    go(remote(h2c.at[0], h2c.at[1], pair.at[2], pair.at[3], y_peer))
    core_events((3, 2, 5))
    remote(ogc.at[1], ogc.at[1], pair.at[0], pair.at[1], y_peer).wait_recv()
    remote(h2c.at[1], h2c.at[1], pair.at[2], pair.at[3], y_peer).wait_recv()
    for copy in memory:
        copy.wait_send()
    for copy in pending:
        copy.wait_send()

    @pl.when(inner == 1)
    def _():
        for copy in inner_pending:
            copy.wait_send()


def front(docs, sizes, lens, tokens, out_grad, pieces, keys, values, bias, own_rows):
    dma = pltpu.SemaphoreType.DMA
    rows, width = tokens.shape
    total = keys.shape[0] * 16
    shape = jax.ShapeDtypeStruct
    wide = shape((rows, width), BF16)
    outs = [
        shape((rows, width), F32),
        wide,
        shape((rows, width), F32),
        shape((rows, 128), F32),
        wide,
        wide,
        wide,
        wide,
        shape((8, rows, WIDTH), BF16),
        shape((8, width), F32),
        shape((2, rows, width), BF16),
        shape((2, rows, width), BF16),
    ]
    counts = (32, 32, 32, 16, 32)
    outs += [shape((n,) + a.shape[-2:], a.dtype) for n, a in zip(counts, pieces)]
    outs += [shape((total, KEYS, WIDTH), BF16)] * 2 + [shape((total, 8, KEYS), F32)]
    spaces = [VM] * 12 + [VM, VM, ANY, ANY, VM] + [VM] * 3
    return pl.pallas_call(
        functools.partial(front_kernel, own_rows),
        out_shape=outs,
        in_specs=[SM] * 3 + [VM] * 10,
        out_specs=spaces,
        scratch_shapes=[
            pltpu.VMEM((8, rows, WIDTH), BF16),
            pltpu.VMEM((8, 8, rows), F32),
            pltpu.VMEM((rows, width), BF16),
            pltpu.VMEM((8, 8, rows), F32),
            pltpu.VMEM((rows, width), F32),
            pltpu.VMEM((2, rows, 128), F32),
            dma((6,)),
            dma((32, 5)),
            dma((192,)),
            dma((3,)),
            dma((16, 3)),
            dma((7, 3)),
            dma((8, 3)),
            dma((7,)),
            dma((8,)),
            dma((8, 2)),
            dma((8, 2)),
            dma((4,)),
        ],
        compiler_params=pltpu.CompilerParams(
            collective_id=0, has_side_effects=True, vmem_limit_bytes=48 << 20
        ),
        name="front",
    )(docs, sizes, lens, tokens, out_grad, *pieces, keys, values, bias)


def key_span(j, ranks, docs, sizes, rank_ref):
    doc = docs[0, j * ranks + rank_ref[0]]
    start = jnp.int32(0)
    stop = jnp.int32(0)
    for i in range(sizes.shape[1]):
        size = sizes[0, i]
        start = start + jnp.where(i < doc, size, 0)
        stop = stop + jnp.where(i <= doc, size, 0)
    return start, stop


def forward_kernel(ranks, block, docs, sizes, rank_ref, q_ref, k_ref, v_ref, bias_ref, o_ref, lse_ref):
    j = pl.program_id(0)
    start, stop = key_span(j, ranks, docs, sizes, rank_ref)
    q = q_ref[0]
    factor = WIDTH ** (-0.5) * LOG2E

    def step(b, carry):
        top, total, acc = carry
        s = lax.dot_general(
            q, rows_of(k_ref, b * block, block), (((1,), (1,)), ((), ())), preferred_element_type=F32
        )
        s = s * factor + window_bias(bias_ref, b * block, block, start, stop)
        best = jnp.maximum(top, jnp.max(s, axis=1, keepdims=True))
        p = jnp.exp2(s - best)
        keep = jnp.exp2(top - best)
        total = total * keep + jnp.sum(p, axis=1, keepdims=True)
        acc = acc * keep + jnp.dot(
            p.astype(BF16), rows_of(v_ref, b * block, block), preferred_element_type=F32
        )
        return best, total, acc

    rows = q.shape[0]
    top, total, acc = lax.fori_loop(
        start // (block * KEYS),
        (stop + block * KEYS - 1) // (block * KEYS),
        step,
        (jnp.full((rows, 1), neg_big, F32), jnp.zeros((rows, 1), F32), jnp.zeros((rows, WIDTH), F32)),
    )
    o_ref[0] = (acc / total).astype(BF16)
    lse = jnp.broadcast_to(top + jnp.log2(total), (rows, rows))
    lse_ref[0] = lse.T[0:8]


def backward_kernel(
    ranks, block, docs, sizes, rank_ref, q_ref, do_ref, stat_ref, k_ref, v_ref, bias_ref, dq_ref
):
    j = pl.program_id(0)
    start, stop = key_span(j, ranks, docs, sizes, rank_ref)
    q, do = q_ref[0], do_ref[0]
    rows = q.shape[0]
    factor = WIDTH ** (-0.5) * LOG2E
    stat = stat_ref[0]
    lse = jnp.broadcast_to(stat[0:1], (rows, rows)).T[:, 0:1]
    delta = jnp.broadcast_to(stat[1:2], (rows, rows)).T[:, 0:1]

    def step(b, acc):
        keys = rows_of(k_ref, b * block, block)
        s = lax.dot_general(q, keys, (((1,), (1,)), ((), ())), preferred_element_type=F32)
        p = jnp.exp2(s * factor + (window_bias(bias_ref, b * block, block, start, stop) - lse))
        dp = lax.dot_general(do, rows_of(v_ref, b * block, block), (((1,), (1,)), ((), ())), preferred_element_type=F32)
        ds = (p * (dp - delta)).astype(BF16)
        return acc + jnp.dot(ds, keys, preferred_element_type=F32)

    acc = lax.fori_loop(
        start // (block * KEYS), (stop + block * KEYS - 1) // (block * KEYS), step, jnp.zeros((rows, WIDTH), F32)
    )
    dq_ref[0] = (acc * WIDTH ** (-0.5)).astype(BF16)


def memory_forward(ranks, docs, sizes, rank, q, kh, vh, bh):
    count, rows, _ = q.shape
    seg = pl.BlockSpec((1, rows, WIDTH), lambda j: (j, 0, 0))
    stat = pl.BlockSpec((1, 8, rows), lambda j: (j, 0, 0))
    block = 8
    return pl.pallas_call(
        functools.partial(forward_kernel, ranks, block),
        grid=(count,),
        out_shape=[
            jax.ShapeDtypeStruct((count, rows, WIDTH), BF16),
            jax.ShapeDtypeStruct((count, 8, rows), F32),
        ],
        in_specs=[SM, SM, SM, seg, VM, VM, VM],
        out_specs=[seg, stat],
        compiler_params=pltpu.CompilerParams(vmem_limit_bytes=48 << 20),
        name="memory_forward",
    )(docs, sizes, rank, q, kh, vh, bh)


def memory_backward(ranks, docs, sizes, rank, q, do, stats, kh, vh, bh):
    count, rows, _ = q.shape
    seg = pl.BlockSpec((1, rows, WIDTH), lambda j: (j, 0, 0))
    stat = pl.BlockSpec((1, 8, rows), lambda j: (j, 0, 0))
    block = 8
    return pl.pallas_call(
        functools.partial(backward_kernel, ranks, block),
        grid=(count,),
        out_shape=jax.ShapeDtypeStruct((count, rows, WIDTH), BF16),
        in_specs=[SM, SM, SM, seg, seg, stat, VM, VM, VM],
        out_specs=seg,
        compiler_params=pltpu.CompilerParams(vmem_limit_bytes=48 << 20),
        name="memory_backward",
    )(docs, sizes, rank, q, do, stats, kh, vh, bh)


DEPTH = 3


def contract(row, first, lanes):
    width = row.shape[1]
    count = width // 32
    shard = lax.broadcasted_iota(jnp.int32, (32, width), 0)
    column = lax.broadcasted_iota(jnp.int32, (32, width), 1)
    masked = jnp.where(column // count == shard, jnp.broadcast_to(row, (32, width)), 0.0)
    feature = lax.broadcasted_iota(jnp.int32, (width, lanes), 0)
    lane = lax.broadcasted_iota(jnp.int32, (width, lanes), 1)
    pick = (lane == first + feature % count).astype(F32)
    return jnp.dot(masked, pick, preferred_element_type=F32, precision=lax.Precision.HIGHEST)


def tiles_of(width):
    for count in (4, 3, 2, 1):
        if width % (count * 128) == 0 and width // count >= 512:
            return count, width // count
    return 1, width


def back_kernel(*refs):
    docs, sizes, lens = refs[:3]
    x_ref, gains, first, tot, att, dh_own, dh_far, out_own, out_far = refs[3:12]
    h, o, h2, dgu, hid, og = refs[12:18]
    q_ref, k_ref, v_ref, qh, kh, vh, bh = refs[18:25]
    w_in, w_out = refs[25:27]
    output, input_grad, g_q, g_k, g_v, g_o, g_gate, g_up, g_down, g_small = refs[27:37]
    stage, cores, firsts, seconds, lines = (refs[37 + 6 * i : 43 + 6 * i] for i in range(5))
    ht, ot, h2t, hidt, dqs, dkv, dql, das, dys, do, small, sst, doh, sth, dqo, dqm, wbuf = refs[67:84]
    dh_in, out_in, far_out, far_in = refs[84:88]
    cs, cr, fs, fr, ss, sr, zs, zr, own, dsend, drecv, qsend, qrecv, wsem, psend, precv = refs[88:]
    y, z, x, c = place()
    ranks = 2
    chip = z * 2 + x
    rows, width = x_ref.shape
    half = hid.shape[1]
    factor = WIDTH ** (-0.5) * LOG2E
    y_peer, x_peer, c_peer = device(1 - y, z, x, c), device(y, z, 1 - x, c), device(y, z, x, 1 - c)
    others = [(chip + d) % 8 for d in range(1, 8)]
    peers = [{"dp": y, "mem": p * ranks + c} for p in others]
    pending = []

    def go(copy):
        copy.start()
        pending.append(copy)

    def wait(dst, sem):
        remote(dst, dst, own.at[0], sem, c_peer).wait_recv()

    def lanes(ref, i):
        return ref.at[:, pl.ds(pl.multiple_of(i * WIDTH, WIDTH), WIDTH)]

    def load(source, i):
        copy = pltpu.make_async_copy(source, wbuf.at[i], wsem.at[i])
        copy.start()
        return copy

    def weight_part(i):
        return w_in.at[:, :, i * width : (i + 1) * width]

    greet(peers + [y_peer, c_peer])

    left = (ht, ht, ot, h2t, hidt)
    right = (dqs, dkv, das, dgu, og)
    order = [(k, d) for d in (3, 2, 1, 0) for k in (1, 0)]
    split = (3, 4)

    def used(i, group):
        return [p for p in group if p != 4 or order[i][0] == 0]

    def held(i, p):
        return i // 2 if p == 4 else i

    def produce(i, group):
        k, d = order[i]
        zz = flip_z(z, d)
        for p in used(i, group):
            u = zz if p == 4 else (1 - y if k else y) * 4 + zz
            room = stage[p].at[i % DEPTH]
            if p == 5:
                for n in range(4):
                    room[n] = small[u * 4 + n]
            else:
                size = 4 * stage[p].shape[2]
                block = left[p][pl.ds(pl.multiple_of(u * size, 32), size), :]
                count, tile = tiles_of(stage[p].shape[3])

                def some(t, _):
                    at = pl.ds(pl.multiple_of(t * tile, 128), tile)
                    part = jnp.dot(block, right[p][:, at], preferred_element_type=F32)
                    room[:, :, at] = part.astype(BF16).reshape(4, size // 4, tile)
                    return 0

                lax.fori_loop(0, count, some, 0)
            for xx in range(2):
                core_copy(i, p, xx).start()

    def core_copy(i, p, xx):
        return remote(
            stage[p].at[i % DEPTH, xx * 2 + 1 - c], cores[p].at[held(i, p), xx], cs.at[i, xx, p], cr.at[i, xx, p], c_peer
        )

    def merge(into, other):
        count, tile = tiles_of(into.shape[1])

        def some(t, _):
            at = pl.ds(pl.multiple_of(t * tile, 128), tile)
            into[:, at] = (into[:, at].astype(F32) + other[:, at].astype(F32)).astype(into.dtype)
            return 0

        lax.fori_loop(0, count, some, 0)

    def after_core(i, group):
        k, d = order[i]
        for p in used(i, group):
            for xx in (1 - x, x):
                into = cores[p].at[held(i, p), xx]
                wait(into, cr.at[i, xx, p])
                merge(into, stage[p].at[i % DEPTH, xx * 2 + c])
            if p in split:
                n = held(i, p)
                go(remote(cores[p].at[n, 1 - x], firsts[p].at[n], fs.at[i, 0, p], fr.at[i, 0, p], x_peer))
            elif k == 1:
                t = i // 2
                for xx in range(2):
                    go(remote(cores[p].at[i, xx], firsts[p].at[t + 4 * xx], fs.at[i, xx, p], fr.at[t, xx, p], y_peer))
            for xx in range(2):
                core_copy(i, p, xx).wait_send()

    def to_line(i, p):
        k, d = order[i]
        if d:
            n = d - 1 + 3 * k
            go(remote(cores[p].at[held(i, p), x], lines[p].at[n], zs.at[n, p], zr.at[n, p], device(y, flip_z(z, d), x, c)))

    def after_first(i, group):
        k, d = order[i]
        t = i // 2
        for p in used(i, group):
            if p in split:
                n = held(i, p)
                wait(firsts[p].at[n], fr.at[i, 0, p])
                merge(cores[p].at[n, x], firsts[p].at[n])
                to_line(i, p)
            elif k == 0:
                for xx in (1 - x, x):
                    room = firsts[p].at[t + 4 * xx]
                    wait(room, fr.at[t, xx, p])
                    merge(cores[p].at[i, xx], room)
                go(remote(cores[p].at[i, 1 - x], seconds[p].at[t], ss.at[t, p], sr.at[t, p], x_peer))

    def after_second(i, group):
        t = i // 2
        for p in group:
            wait(seconds[p].at[t], sr.at[t, p])
            merge(cores[p].at[i, x], seconds[p].at[t])
            to_line(i, p)

    def along(p, k, at):
        total = cores[p][held(7 - k, p), x, :, at].astype(F32)
        for d in range(3):
            total = total + lines[p][d + 3 * k, :, at].astype(F32)
        return total

    def line_wait(p, k):
        for d in range(3):
            wait(lines[p].at[d + 3 * k], zr.at[d + 3 * k, p])

    def finish(group):
        for p in group:
            line_wait(p, 0)
            outs = ((g_q,), (g_k, g_v), (g_o,), (), (g_down,), (g_small,))[p]
            for i, out in enumerate(outs):
                span = cores[p].shape[3] // len(outs)
                out[...] = along(p, 0, slice(i * span, (i + 1) * span))

    def attend(d, _):
        j = (chip + d) % 8
        start, stop, base, window = key_window(j, ranks, c, docs, sizes, kh.shape[0])
        q, dout, stat = qh[j], doh[j], sth[j]
        lse = jnp.broadcast_to(stat[0:1], (rows, rows)).T[:, 0:1]
        delta = jnp.broadcast_to(stat[1:2], (rows, rows)).T[:, 0:1]
        parts = 3
        chunk = window // parts

        def step(t, acc):
            at = base + t * chunk
            keys = rows_of(kh, at, chunk)
            s = lax.dot_general(q, keys, (((1,), (1,)), ((), ())), preferred_element_type=F32)
            p = jnp.exp2(s * factor + (window_bias(bh, at, chunk, start, stop) - lse))
            dp = lax.dot_general(
                dout, rows_of(vh, at, chunk), (((1,), (1,)), ((), ())), preferred_element_type=F32
            )
            ds = (p * (dp - delta)).astype(BF16)
            return acc + jnp.dot(ds, keys, preferred_element_type=F32)

        acc = lax.fori_loop(0, parts, step, jnp.zeros((rows, WIDTH), F32))
        dqo[j] = (acc * WIDTH ** (-0.5)).astype(BF16)
        return 0

    def answer(d):
        j = (chip + d) % 8
        go(remote(dqo.at[j], lanes(dqm, chip), qsend.at[d - 1], qrecv.at[chip], {"dp": y, "mem": j * ranks + c}))

    ffn, query, others_att, gain = (3, 4), (0,), (1, 2), (5,)
    go(remote(dh_far, dh_in, psend.at[0], precv.at[0], y_peer))
    go(remote(out_far, out_in, psend.at[1], precv.at[1], y_peer))
    load_out = load(w_out, 0)
    load_key = load(weight_part(1), 1)
    h2t[...] = h2[...].T
    produce(0, ffn)
    hidt[...] = hid[...].T
    produce(1, ffn)
    after_core(0, ffn)
    produce(2, ffn)
    after_core(1, ffn)

    wait(dh_in, precv.at[0])
    residual = first[...]
    inverse_two = lax.rsqrt(jnp.mean(residual * residual, axis=-1, keepdims=True) + epsilon)
    normed_two = residual * inverse_two
    dh2 = dh_own[...] + dh_in[...].astype(F32)
    pulled = contract(jnp.sum(dh2 * normed_two, axis=0, keepdims=True), width // 32, 128)
    small[...] = jnp.broadcast_to(pulled[:, None, :], small.shape)
    dn = dh2 * gains[1:2]
    dy = og[0:rows].astype(F32) + inverse_two * (
        dn - normed_two * jnp.mean(dn * normed_two, axis=-1, keepdims=True)
    )
    dys[...] = dy
    low = dy.astype(BF16)
    das[...] = low
    load_out.wait()
    do[...] = lax.dot_general(
        low, wbuf[0].reshape(width, width), (((1,), (1,)), ((), ())), preferred_element_type=F32
    ).astype(BF16)
    load_value = load(weight_part(2), 0)

    lane = lax.broadcasted_iota(jnp.int32, (rows, 128), 1)
    deltas = jnp.zeros((rows, 128), F32)
    for i in range(HEADS):
        at = slice(i * WIDTH, (i + 1) * WIDTH)
        part = jnp.sum(do[:, at].astype(F32) * att[:, at], axis=1, keepdims=True)
        deltas = jnp.where(lane == i, part, deltas)
    tot_rows, delta_rows = tot[...].T, deltas.T
    head_row = lax.broadcasted_iota(jnp.int32, (8, rows), 0)
    for i in range(HEADS):
        sst[i] = jnp.where(head_row == 0, tot_rows[i : i + 1], delta_rows[i : i + 1])
    for d, (p, peer) in enumerate(zip(others, peers)):
        go(remote(lanes(do, p), doh.at[chip], dsend.at[d, 0], drecv.at[chip, 0], peer))
        go(remote(sst.at[p], sth.at[chip], dsend.at[d, 1], drecv.at[chip, 1], peer))
    homes = [
        pltpu.make_async_copy(lanes(do, chip), doh.at[chip], own.at[1]),
        pltpu.make_async_copy(sst.at[chip], sth.at[chip], own.at[2]),
    ]
    for copy in homes:
        copy.start()
    ht[...] = h[...].T
    ot[...] = o[...].T
    produce(3, ffn)
    after_core(2, ffn)

    below = lax.broadcasted_iota(jnp.int32, (rows, rows), 1)
    ok = (below <= lax.broadcasted_iota(jnp.int32, (rows, rows), 0)) & (below < lens[0, 0])
    for i in range(HEADS):
        at = slice(i * WIDTH, (i + 1) * WIDTH)
        q, k, v, dout = q_ref[:, at], k_ref[:, at], v_ref[:, at], do[:, at]
        s = lax.dot_general(q, k, (((1,), (1,)), ((), ())), preferred_element_type=F32)
        p = jnp.where(ok, jnp.exp2(s * factor - tot[:, i : i + 1]), 0.0)
        dp = lax.dot_general(dout, v, (((1,), (1,)), ((), ())), preferred_element_type=F32)
        ds = (p * (dp - deltas[:, i : i + 1])).astype(BF16)
        dql[:, at] = jnp.dot(ds, k, preferred_element_type=F32) * WIDTH ** (-0.5)
        dk = lax.dot_general(ds, q, (((0,), (0,)), ((), ())), preferred_element_type=F32) * WIDTH ** (-0.5)
        dv = lax.dot_general(p.astype(BF16), dout, (((0,), (0,)), ((), ())), preferred_element_type=F32)
        dkv[:, at] = dk.astype(BF16)
        dkv[:, width + i * WIDTH : width + (i + 1) * WIDTH] = dv.astype(BF16)

    produce(0, others_att)
    produce(1, others_att)
    after_core(0, others_att)
    produce(2, others_att)
    after_core(1, others_att)
    after_core(2, others_att)
    for copy in homes:
        copy.wait()
    for p in others:
        wait(doh.at[p], drecv.at[p, 0])
        wait(sth.at[p], drecv.at[p, 1])
    lax.fori_loop(1, 3, attend, 0)
    answer(1)
    answer(2)
    after_first(0, ffn)
    after_core(3, ffn)
    produce(4, ffn)
    produce(3, others_att)
    produce(4, others_att)
    lax.fori_loop(3, 5, attend, 0)
    answer(3)
    answer(4)
    after_first(1, ffn)
    after_core(4, ffn)
    produce(5, ffn)
    after_core(3, others_att)
    after_core(4, others_att)
    after_first(1, others_att)
    lax.fori_loop(5, 7, attend, 0)
    answer(5)
    answer(6)
    after_first(2, ffn)
    after_core(5, ffn)
    produce(6, ffn)
    produce(5, others_att)
    produce(6, others_att)
    after_first(3, others_att)
    lax.fori_loop(7, 9, attend, 0)
    answer(7)
    back_copy = pltpu.make_async_copy(dqo.at[chip], lanes(dqm, chip), own.at[1])
    back_copy.start()
    after_first(3, ffn)
    after_core(6, ffn)
    produce(7, ffn)
    after_core(5, others_att)
    after_core(6, others_att)
    produce(7, others_att)
    after_second(1, others_att)
    after_core(7, ffn)
    wait(out_in, precv.at[1])
    output[...] = (residual + out_own[...] + out_in[...].astype(F32)).astype(BF16)
    load_key.wait()
    dh = lax.dot_general(
        dkv[:, :width], wbuf[1].reshape(width, width), (((1,), (1,)), ((), ())), preferred_element_type=F32
    )
    load_query = load(weight_part(0), 1)
    load_value.wait()
    dh = dh + lax.dot_general(
        dkv[:, width:], wbuf[0].reshape(width, width), (((1,), (1,)), ((), ())), preferred_element_type=F32
    )
    after_first(4, ffn)
    after_first(5, others_att)
    after_core(7, others_att)
    for p in others:
        wait(lanes(dqm, p), qrecv.at[p])
    back_copy.wait()
    dqs[...] = (dql[...] + dqm[...].astype(F32)).astype(BF16)
    produce(0, query)
    produce(1, query)
    after_core(0, query)
    produce(2, query)
    after_core(1, query)
    after_core(2, query)
    after_first(5, ffn)
    produce(3, query)
    produce(4, query)
    after_core(3, query)
    after_core(4, query)
    produce(5, query)
    produce(6, query)
    after_core(5, query)
    after_core(6, query)
    produce(7, query)
    after_core(7, query)
    after_second(3, others_att)
    after_first(7, others_att)

    load_query.wait()
    dh = dh + lax.dot_general(
        dqs[...], wbuf[1].reshape(width, width), (((1,), (1,)), ((), ())), preferred_element_type=F32
    )
    inputs = x_ref[...].astype(F32)
    inverse = lax.rsqrt(jnp.mean(inputs * inputs, axis=-1, keepdims=True) + epsilon)
    normed = inputs * inverse
    pulled = contract(jnp.sum(dh * normed, axis=0, keepdims=True), 0, 128)
    small[...] = small[...] + jnp.broadcast_to(pulled[:, None, :], small.shape)
    for i in range(8):
        produce(i, gain)
        if i:
            after_core(i - 1, gain)
    after_core(7, gain)
    after_first(6, ffn)
    after_first(1, query)
    after_first(7, ffn)
    after_first(3, query)
    for i in (1, 3, 5, 7):
        after_first(i, gain)
    dn = dh * gains[0:1]
    input_grad[...] = (
        dys[...] + inverse * (dn - normed * jnp.mean(dn * normed, axis=-1, keepdims=True))
    ).astype(BF16)
    after_second(5, others_att)
    after_first(5, query)
    after_second(1, query)
    after_first(7, query)
    after_second(7, others_att)
    after_second(3, query)
    for i in (1, 3, 5):
        after_second(i, gain)

    line_wait(3, 1)
    far_out[...] = along(3, 1, slice(0, 2 * half)).astype(BF16)
    go(remote(far_out, far_in, psend.at[2], precv.at[2], y_peer))
    after_second(5, query)
    after_second(7, query)
    after_second(7, gain)
    line_wait(3, 0)
    near_at = pl.ds(pl.multiple_of(y * half, 128), half)
    far_at = pl.ds(pl.multiple_of((1 - y) * half, 128), half)
    g_gate[:, near_at] = along(3, 0, slice(0, half))
    g_up[:, near_at] = along(3, 0, slice(half, 2 * half))
    finish((4, 1, 2))
    wait(far_in, precv.at[2])
    g_gate[:, far_at] = far_in[:, :half].astype(F32)
    g_up[:, far_at] = far_in[:, half:].astype(F32)
    finish((0, 5))
    for copy in pending:
        copy.wait_send()


def back(scalars, f32_args, bf16_args, heads_args, weights):
    dma = pltpu.SemaphoreType.DMA
    x = f32_args[0]
    h, o, h2, dgu, hid, og = bf16_args
    rows, width = x.shape
    half = hid.shape[1]
    own = width // 32
    down = half // 16
    shapes = [
        ((own, width), BF16),
        ((own, 2 * width), BF16),
        ((own, width), BF16),
        ((own, 2 * half), BF16),
        ((down, width), BF16),
        ((8, 128), F32),
    ]

    def buffers(*leads):
        return [pltpu.VMEM(lead + s, t) for lead, (s, t) in zip(leads, shapes)]

    none = (1,)

    shape = jax.ShapeDtypeStruct
    outs = [shape((rows, width), BF16)] * 2 + [shape((own, width), F32)] * 4
    outs += [shape((own, 2 * half), F32)] * 2 + [shape((down, width), F32), shape((8, 128), F32)]
    return pl.pallas_call(
        back_kernel,
        out_shape=outs,
        in_specs=[SM] * 3 + [VM] * 22 + [ANY] * 2,
        out_specs=[VM] * 10,
        scratch_shapes=buffers(*[(DEPTH, 4)] * 6)
        + buffers(*[(8, 2)] * 4, (4, 2), (8, 2))
        + buffers(*[(8,)] * 4, (4,), (8,))
        + buffers((4,), (4,), (4,), none, none, (4,))
        + buffers((3,), (3,), (3,), (6,), (3,), (3,))
        + [
            pltpu.VMEM((width, rows), BF16),
            pltpu.VMEM((width, rows), BF16),
            pltpu.VMEM((width, 2 * rows), BF16),
            pltpu.VMEM((half, 2 * rows), BF16),
            pltpu.VMEM((rows, width), BF16),
            pltpu.VMEM((rows, 2 * width), BF16),
            pltpu.VMEM((rows, width), F32),
            pltpu.VMEM((rows, width), BF16),
            pltpu.VMEM((rows, width), F32),
            pltpu.VMEM((rows, width), BF16),
            pltpu.VMEM((32, 8, 128), F32),
            pltpu.VMEM((8, 8, rows), F32),
            pltpu.VMEM((8, rows, WIDTH), BF16),
            pltpu.VMEM((8, 8, rows), F32),
            pltpu.VMEM((8, rows, WIDTH), BF16),
            pltpu.VMEM((rows, width), BF16),
            pltpu.VMEM((2, 32, own, width), BF16),
            pltpu.VMEM((rows, width), BF16),
            pltpu.VMEM((rows, width), BF16),
            pltpu.VMEM((own, 2 * half), BF16),
            pltpu.VMEM((own, 2 * half), BF16),
            dma((8, 2, 6)),
            dma((8, 2, 6)),
            dma((8, 2, 6)),
            dma((8, 2, 6)),
            dma((4, 6)),
            dma((4, 6)),
            dma((6, 6)),
            dma((6, 6)),
            dma((3,)),
            dma((7, 2)),
            dma((8, 2)),
            dma((7,)),
            dma((8,)),
            dma((2,)),
            dma((3,)),
            dma((3,)),
        ],
        compiler_params=pltpu.CompilerParams(
            collective_id=1, has_side_effects=True, vmem_limit_bytes=38 << 20
        ),
        name="back",
    )(*scalars, *f32_args, *bf16_args, *heads_args, *weights)


def settle_kernel(*refs):
    n = len(refs) // 2
    copies = [pltpu.make_async_copy(refs[i], refs[n + i], refs[2 * n].at[i]) for i in range(n)]
    for copy in copies:
        copy.start()
    for copy in copies:
        copy.wait()


def settle(arrays):
    return pl.pallas_call(
        settle_kernel,
        out_shape=[jax.ShapeDtypeStruct(a.shape, a.dtype) for a in arrays],
        in_specs=[VM] * len(arrays),
        out_specs=[ANY] * len(arrays),
        scratch_shapes=[pltpu.SemaphoreType.DMA((len(arrays),))],
        compiler_params=pltpu.CompilerParams(vmem_limit_bytes=8 << 20),
        name="settle",
    )(*arrays)


def gather_plain(pieces, keys, values, bias, ranks):
    full = [lax.all_gather(a, ("dp", "mem"), axis=0, tiled=False) for a in pieces]

    def spread(a):
        blocks = a.reshape(a.shape[0], HEADS, WIDTH).transpose(1, 0, 2)
        return lax.all_to_all(jnp.repeat(blocks, ranks, axis=0), "mem", 0, 0, tiled=True)

    return full + [
        spread(keys).reshape(-1, KEYS, WIDTH),
        spread(values).reshape(-1, KEYS, WIDTH),
        lax.all_gather(bias, "mem", axis=0, tiled=True),
    ]


def to_heads_plain(x, ranks):
    rank = lax.axis_index("mem") % ranks
    blocks = x if x.ndim == 3 else x.reshape(x.shape[0], HEADS, WIDTH).transpose(1, 0, 2)
    wide = jnp.where((jnp.arange(ranks) == rank)[None, :, None, None], blocks[:, None], 0)
    wide = wide.reshape((-1,) + blocks.shape[1:])
    got = lax.all_to_all(wide, "mem", 0, 0, tiled=True)
    return lax.dynamic_index_in_dim(got.reshape((-1, ranks) + blocks.shape[1:]), rank, 1, keepdims=False)


def to_tokens_plain(x, ranks, wide_out):
    rank = lax.axis_index("mem") % ranks
    wide = jnp.where((jnp.arange(ranks) == rank)[None, :, None, None], x[:, None], 0)
    got = lax.all_to_all(wide.reshape((-1,) + x.shape[1:]), "mem", 0, 0, tiled=True)
    got = lax.dynamic_index_in_dim(got.reshape((-1, ranks) + x.shape[1:]), rank, 1, keepdims=False)
    return got.transpose(1, 0, 2).reshape(x.shape[1], -1) if wide_out else got


def reduce_plain(h, dqkv, o, da, h2, dgu, hid, og, small):
    outs = []
    for a, b in ((h, dqkv), (o, da), (h2, dgu), (hid, og)):
        full = jnp.dot(a.T, b, preferred_element_type=F32)
        outs.append(lax.psum_scatter(full, ("dp", "mem"), scatter_dimension=0, tiled=True))
    outs.append(lax.psum_scatter(small, ("dp", "mem"), scatter_dimension=0, tiled=False))
    return outs


def normalize(values):
    inverse = lax.rsqrt(jnp.mean(values * values, axis=-1, keepdims=True) + epsilon)
    return (values * inverse, inverse)


def norm_back(grad_scaled, normed, inverse, gain_full):
    gain_grad = jnp.sum(grad_scaled * normed, axis=0)
    grad_normed = grad_scaled * gain_full
    grad_values = inverse * (
        grad_normed - normed * jnp.mean(grad_normed * normed, axis=-1, keepdims=True)
    )
    return (gain_grad, grad_values)


def feed_forward(normed_low, out_grad, gate_up, down):
    units = down.shape[0]
    both = jnp.dot(normed_low, gate_up, preferred_element_type=F32)
    gate, up = both[:, :units], both[:, units:]
    sigmoid_gate = jax.nn.sigmoid(gate)
    activated = gate * sigmoid_gate
    hidden = (activated * up).astype(BF16)
    grad_hidden = jnp.dot(out_grad, down.T, preferred_element_type=F32)
    grad_gate_up = jnp.concatenate(
        [
            (grad_hidden * up * sigmoid_gate * (1.0 + gate * (1.0 - sigmoid_gate))).astype(BF16),
            (grad_hidden * activated).astype(BF16),
        ],
        axis=1,
    )
    return hidden, grad_gate_up


def shards(
    tokens,
    gain_attn,
    w_query,
    w_key,
    w_value,
    w_out,
    gain_ffn,
    w_gate,
    w_up,
    w_down,
    mem_keys,
    mem_values,
    out_grad,
    key_mask,
    mem_sizes,
    seg_doc,
    seg_len,
):
    seg_rows, model_width = tokens.shape
    mem_count = lax.axis_size("mem")
    dp_count = lax.axis_size("dp")
    devices = mem_count * dp_count
    ranks = mem_count // HEADS
    direct = dp_count == 2 and mem_count == 16
    factor = WIDTH ** (-0.5)
    ff_width = w_gate.shape[1]
    own = gain_attn.shape[0]
    down_rows = w_down.shape[0]

    half = ff_width // 2
    if direct:
        joined = jnp.stack(
            [
                jnp.concatenate([w_gate[:, i * half : (i + 1) * half], w_up[:, i * half : (i + 1) * half]], axis=1)
                for i in range(2)
            ]
        )
    else:
        joined = jnp.concatenate([w_gate, w_up], axis=1)
    pieces = [
        jnp.concatenate([w_query, w_key, w_value], axis=1),
        w_out,
        joined,
        w_down,
        jnp.pad(jnp.concatenate([gain_attn, gain_ffn])[None], ((0, 15), (0, 128 - 2 * own))),
    ]
    bias = jnp.where(key_mask == 1, 0.0, neg_big).astype(F32).reshape(-1, 1, KEYS)
    bias = jnp.broadcast_to(bias, (bias.shape[0], 8, KEYS))
    rank = (lax.axis_index("mem") % ranks).reshape(1).astype(jnp.int32)
    if direct:
        split = (-1, KEYS, model_width)
        done = front(
            seg_doc,
            mem_sizes,
            seg_len,
            tokens,
            out_grad,
            pieces,
            mem_keys.reshape(split),
            mem_values.reshape(split),
            bias,
            own,
        )
        first, attended_low, attended, whole, normed_low, queries, keys_local, values_local = done[:8]
        q_heads, gains, pair_normed, pair_grad, joined_w, out_full, gate_up, down, _, kh, vh, bh = done[8:]
        pair_normed = pair_normed.reshape(2 * seg_rows, model_width)
        pair_grad = pair_grad.reshape(2 * seg_rows, model_width)
        gate_up = gate_up.reshape(model_width, 2 * half)
        down = down.reshape(half, model_width)
        hidden, grad_gate_up = feed_forward(pair_normed, pair_grad, gate_up, down)
        partial = jnp.dot(hidden, down, preferred_element_type=F32)
        grad_partial = jnp.dot(grad_gate_up, gate_up.T, preferred_element_type=F32)
        sums = back(
            (seg_doc, mem_sizes, seg_len),
            (
                tokens,
                gains,
                first,
                whole,
                attended,
                grad_partial[:seg_rows],
                grad_partial[seg_rows:].astype(BF16),
                partial[:seg_rows],
                partial[seg_rows:].astype(BF16),
            ),
            (normed_low, attended_low, pair_normed, grad_gate_up, hidden, pair_grad),
            (queries, keys_local, values_local, q_heads, kh, vh, bh),
            (joined_w, out_full),
        )
        small = sums[9]
        output, input_grad, g_q, g_k, g_v, g_o, g_gate, g_up, g_down = settle(sums[:9])
        return (
            output,
            input_grad,
            small[0, :own],
            g_q,
            g_k,
            g_v,
            g_o,
            small[0, own : 2 * own],
            g_gate,
            g_up,
            g_down,
        )

    inputs = tokens.astype(F32)
    normed_one, inverse_one = normalize(inputs)
    gathered = gather_plain(pieces, mem_keys, mem_values, bias, ranks)
    joined_w, out_full, gate_up, down_full, gains, kh, vh, bh = gathered
    gain_one = gains[:, 0, :own].reshape(-1).astype(F32)
    gain_two = gains[:, 0, own : 2 * own].reshape(-1).astype(F32)
    joined_w = joined_w.reshape(model_width, -1)
    out_full = out_full.reshape(model_width, -1)
    gate_up = gate_up.reshape(model_width, -1)
    down_full = down_full.reshape(ff_width, -1)
    normed_low = (normed_one * gain_one).astype(BF16)
    projected = jnp.dot(normed_low, joined_w, preferred_element_type=F32).astype(BF16)
    queries = projected[:, :model_width]
    keys_local = projected[:, model_width : 2 * model_width]
    values_local = projected[:, 2 * model_width :]
    query_heads = queries.reshape(seg_rows, HEADS, WIDTH)
    key_heads = keys_local.reshape(seg_rows, HEADS, WIDTH)
    value_heads = values_local.reshape(seg_rows, HEADS, WIDTH)
    positions = lax.iota(jnp.int32, seg_rows)
    local_ok = (positions[None, :] <= positions[:, None]) & (positions[None, :] < seg_len[0, 0])
    local_ok = local_ok[None]
    local_scores = (
        jnp.einsum("ihd,jhd->hij", query_heads, key_heads, preferred_element_type=F32) * factor
    )
    local_masked = jnp.where(local_ok, local_scores, neg_big)
    q_heads = to_heads_plain(queries, ranks)
    o_mem, lse_mem = memory_forward(ranks, seg_doc, mem_sizes, rank, q_heads, kh, vh, bh)
    mem_o = to_tokens_plain(o_mem, ranks, True).reshape(seg_rows, HEADS, WIDTH).astype(F32)
    mem_lse = to_tokens_plain(lse_mem, ranks, False)[:, 0, :] / LOG2E
    local_top = jnp.max(local_masked, axis=2)
    local_total = jnp.sum(
        jnp.where(local_ok, jnp.exp(local_masked - local_top[:, :, None]), 0.0), axis=2
    )
    local_lse = local_top + jnp.log(local_total)
    best = jnp.maximum(local_lse, mem_lse)
    log_total = best + jnp.log(jnp.exp(local_lse - best) + jnp.exp(mem_lse - best))
    local_probs = jnp.where(local_ok, jnp.exp(local_masked - log_total[:, :, None]), 0.0)
    local_low = local_probs.astype(BF16)
    attended = (
        jnp.einsum("hij,jhd->ihd", local_low, value_heads, preferred_element_type=F32)
        + mem_o * jnp.exp(mem_lse - log_total).T[..., None]
    )
    attended_low = attended.reshape(seg_rows, model_width).astype(BF16)
    first = inputs + jnp.dot(attended_low, out_full, preferred_element_type=F32)

    normed_two, inverse_two = normalize(first)
    normed_two_low = (normed_two * gain_two).astype(BF16)
    hidden, grad_gate_up = feed_forward(normed_two_low, out_grad, gate_up, down_full)
    output = (first + jnp.dot(hidden, down_full, preferred_element_type=F32)).astype(BF16)
    grad_normed_two = jnp.dot(grad_gate_up, gate_up.T, preferred_element_type=F32)
    grad_gain_two, grad_first_norm = norm_back(grad_normed_two, normed_two, inverse_two, gain_two)
    grad_first = out_grad.astype(F32) + grad_first_norm

    grad_branch = grad_first.astype(BF16)
    grad_attended = jnp.dot(grad_branch, out_full.T, preferred_element_type=F32).astype(BF16)
    grad_att_heads = grad_attended.reshape(seg_rows, HEADS, WIDTH)
    delta = jnp.sum(grad_att_heads.astype(F32) * attended, axis=-1).T
    stats = jnp.pad(jnp.stack([log_total * LOG2E, delta], axis=1), ((0, 0), (0, 6), (0, 0)))
    do_heads = to_heads_plain(grad_attended, ranks)
    stat_heads = to_heads_plain(stats, ranks)
    dq_heads = memory_backward(
        ranks, seg_doc, mem_sizes, rank, q_heads, do_heads, stat_heads, kh, vh, bh
    )
    grad_query_memory = to_tokens_plain(dq_heads, ranks, True)

    grad_value_heads = jnp.einsum(
        "hij,ihd->jhd", local_low, grad_att_heads, preferred_element_type=F32
    )
    grad_local_probs = jnp.einsum(
        "ihd,jhd->hij", grad_att_heads, value_heads, preferred_element_type=F32
    )
    grad_local_scores = (local_probs * (grad_local_probs - delta[:, :, None])).astype(BF16)
    grad_query_heads = (
        jnp.einsum("hij,jhd->ihd", grad_local_scores, key_heads, preferred_element_type=F32)
        * factor
    )
    grad_key_heads = (
        jnp.einsum("hij,ihd->jhd", grad_local_scores, query_heads, preferred_element_type=F32)
        * factor
    )
    grad_queries = grad_query_heads.reshape(seg_rows, model_width) + grad_query_memory.astype(F32)
    grad_joined = jnp.concatenate(
        [
            grad_queries,
            grad_key_heads.reshape(seg_rows, model_width),
            grad_value_heads.reshape(seg_rows, model_width),
        ],
        axis=1,
    ).astype(BF16)
    grad_normed_one = jnp.dot(grad_joined, joined_w.T, preferred_element_type=F32)
    grad_gain_one, grad_input_norm = norm_back(grad_normed_one, normed_one, inverse_one, gain_one)
    input_grad = (grad_first + grad_input_norm).astype(BF16)

    small = jnp.stack([grad_gain_one.reshape(devices, own), grad_gain_two.reshape(devices, own)], axis=1)
    small = jnp.pad(small, ((0, 0), (0, 6), (0, 128 - own)))
    attn_sums, out_sums, ffn_sums, down_sums, small_sums = reduce_plain(
        normed_low, grad_joined, attended_low, grad_branch, normed_two_low, grad_gate_up, hidden, out_grad, small
    )
    return (
        output,
        input_grad,
        small_sums[0, :own],
        attn_sums[:, :model_width],
        attn_sums[:, model_width : 2 * model_width],
        attn_sums[:, 2 * model_width : 3 * model_width],
        out_sums,
        small_sums[1, :own],
        ffn_sums[:, :ff_width],
        ffn_sums[:, ff_width:],
        down_sums,
    )


def solution(mesh):
    rows = P(("dp", "mem"), None)
    vector = P(("dp", "mem"))
    in_specs = (
        (rows, vector) + (rows,) * 4 + (vector,) + (rows,) * 6
        + (P("dp", "mem"), P("dp", None), P("dp", None), P("dp", "mem"))
    )
    out_specs = (rows, rows, vector) + (rows,) * 4 + (vector,) + (rows,) * 3
    return jax.shard_map(shards, mesh=mesh, in_specs=in_specs, out_specs=out_specs, check_vma=False)
```

```python
import functools
import math

import jax
import jax.numpy as jnp
from jax import lax
from jax.experimental import pallas as pl
from jax.experimental.pallas import tpu as pltpu
from jax.sharding import PartitionSpec as P

HEADS = 8
WIDTH = 128
KEYS = 128
epsilon = 1e-05
neg_big = -1e30
LOG2E = 1.4426950408889634
VMEM_MAX = 67043328
MESH = pl.DeviceIdType.MESH
F32 = jnp.float32
BF16 = jnp.bfloat16

ANY = pl.BlockSpec(memory_space=pl.ANY)
VM = pl.BlockSpec(memory_space=pltpu.VMEM)
SM = pl.BlockSpec(memory_space=pltpu.SMEM)


def place():
    m = lax.axis_index("mem")
    return lax.axis_index("dp"), m // 4, (m // 2) % 2, m % 2


def device(y, z, x, c):
    return {"dp": y, "mem": z * 4 + x * 2 + c}


def flip_z(z, d):
    return (z, z + 1 - 2 * (z % 2), (z + 2) % 4, 3 - z)[d]


def greet(targets):
    barrier = pltpu.get_barrier_semaphore()
    for target in targets:
        pl.semaphore_signal(barrier, inc=1, device_id=target, device_id_type=MESH)
    pl.semaphore_wait(barrier, len(targets))


def remote(src, dst, send, recv, target):
    return pltpu.make_async_remote_copy(
        src_ref=src, dst_ref=dst, send_sem=send, recv_sem=recv, device_id=target, device_id_type=MESH
    )


EARLY, LATE = (0, 4, 1), (3, 2, 5)
CROSS = (0, 1, 4)


def line_of(z):
    inner = ((z + 1) // 2) % 2
    near = flip_z(z, 1)
    second = 3 - (inner * z + (1 - inner) * near)
    third = 3 - (inner * near + (1 - inner) * z)
    return inner, (z, near, second, third)


def expand(packed, first, count):
    rows, lanes = packed.shape
    width = rows // 16 * count
    lane = lax.broadcasted_iota(jnp.int32, (lanes, width), 0)
    column = lax.broadcasted_iota(jnp.int32, (lanes, width), 1)
    pick = (lane == first + column % count).astype(BF16)
    wide = jnp.dot(packed, pick, preferred_element_type=F32)
    shard = lax.broadcasted_iota(jnp.int32, (rows, width), 0) // 16
    column = lax.broadcasted_iota(jnp.int32, (rows, width), 1) // count
    return jnp.sum(jnp.where(shard == column, wide, 0.0), axis=0, keepdims=True)


def rows_of(ref, block, count):
    return jnp.concatenate([ref[block + i] for i in range(count)], axis=0)


def window_bias(ref, block, count, start, stop):
    size = ref.shape[2]
    parts = []
    for i in range(count):
        spots = (block + i) * size + lax.broadcasted_iota(jnp.int32, (8, size), 1)
        inside = (spots >= start) & (spots < stop)
        parts.append(jnp.where(inside, ref[block + i], neg_big))
    return jnp.concatenate(parts, axis=1)[0:1]


def key_window(j, ranks, rank, docs, sizes, blocks):
    window = blocks // 2 + 1
    doc = docs[0, j * ranks + rank]
    start = 0
    stop = 0
    for i in range(sizes.shape[1]):
        size = sizes[0, i]
        start = start + size * (i < doc).astype(jnp.int32)
        stop = stop + size * (i <= doc).astype(jnp.int32)
    base = lax.min(lax.div(start, jnp.int32(KEYS)), jnp.int32(blocks - window))
    return start, stop, base, window


def columns(block):
    rows = block.shape[1]
    return jnp.concatenate([block, jnp.zeros((rows - 8, rows), F32)], axis=0).T


def front_kernel(own_rows, *refs):
    docs, sizes, lens = refs[:3]
    x_ref, og = refs[3:5]
    src = refs[5:10]
    keys, vals, bias = refs[10:13]
    first_out, o_low, att, tot, h_ref, q_ref, k_ref, v_ref, qh, gain_out, h2c, ogc = refs[13:25]
    dst = refs[25:30]
    kh, vh, bh = refs[30:33]
    oh, lh, mo, ml, loc, st, relay_k, relay_v = refs[33:41]
    own_sem, rs, sends, ko, kr, rr, kcs, qs, qr, os_, or_, pair = refs[41:]
    y, z, x, c = place()
    m = z * 4 + x * 2 + c
    ranks = 2
    chip = z * 2 + x
    rows = x_ref.shape[0]
    width = x_ref.shape[1]
    total = kh.shape[0]
    per = keys.shape[0]
    factor = WIDTH ** (-0.5) * LOG2E
    inner, line = line_of(z)
    y_peer, x_peer, c_peer = device(1 - y, z, x, c), device(y, z, 1 - x, c), device(y, z, x, 1 - c)
    near, across = device(y, flip_z(z, 1), x, c), device(y, 3 - z, x, c)
    plane = [
        (flip_z(z, dz), x if dx == 0 else 1 - x) for dz in (3, 2, 1, 0) for dx in (1, 0) if dz or dx
    ]
    pending = []
    inner_pending = []
    used = [0]

    def next_sem():
        used[0] += 1
        return sends.at[used[0] - 1]

    def go(copy):
        copy.start()
        pending.append(copy)

    def spot(p, zz, xx, cc, far=False):
        n = zz * 4 + xx * 2 + cc
        if p == 3:
            return dst[3].at[n], rs.at[n, 3]
        n = n + 16 * (1 - y if far or p == 5 else y)
        p = 2 if p == 5 else p
        return dst[p].at[n], rs.at[n, p]

    def push(place, target, source=None):
        view, sem = place
        go(remote(view if source is None else source, view, next_sem(), sem, target))

    def push_inner(jobs, target):
        copies = [
            remote(view if source is None else source, view, next_sem(), sem, target)
            for (view, sem), source in jobs
        ]
        inner_pending.extend(copies)

        @pl.when(inner == 1)
        def _():
            for copy in copies:
                copy.start()

    def arrived(place):
        view, sem = place
        remote(view, view, own_sem.at[0], sem, c_peer).wait_recv()

    def own_sends(group):
        jobs = []
        for p in group:
            source = None if p == 5 else src[2].at[y] if p == 2 else src[p]
            jobs.append((spot(p, z, x, c), source, p))
        push_inner([job[:2] for job in jobs], across)
        for view, source, p in jobs:
            push(view, near, source)
        for view, source, p in jobs:
            if p in CROSS:
                push(view, y_peer, source)
            push(view, x_peer, source)
            push(view, c_peer, source)

    def mirror():
        arrived(spot(5, z, x, c))
        own_sends((5,))

    def line_event(i, group):
        views = [(spot(p, line[i], x, c), p) for p in group]
        for view, p in views:
            arrived(view)
        push_inner([(view, None) for view, p in views], across if i == 1 else near)
        for view, p in views:
            if p in CROSS:
                push(view, y_peer)
            push(view, x_peer)
            push(view, c_peer)

    def x_event(i, group):
        for p in group:
            view = spot(p, line[i], 1 - x, c)
            arrived(view)
            if p in CROSS:
                push(view, y_peer)
            push(view, c_peer)

    def y_event(i, group):
        for p in group:
            view = spot(p, line[i], x, c, True)
            arrived(view)
            push(view, c_peer)

    def corner_event(i, group):
        for p in group:
            view = spot(p, line[i], 1 - x, c, True)
            arrived(view)
            push(view, c_peer)

    def core_events(group):
        for p in group:
            for far in (False, True) if p in CROSS else (False,):
                for zz in line:
                    for xx in (x, 1 - x):
                        arrived(spot(p, zz, xx, 1 - c, far))

    def block(ref, i):
        return ref.at[pl.ds(i * per, per)]

    def lanes(ref, i):
        at = pl.ds(pl.multiple_of(i * WIDTH, WIDTH), WIDTH)
        return ref.at[:, at] if len(ref.shape) == 2 else ref.at[:, :, at]

    beside = z * 4 + (1 - x) * 2 + c
    memory_x = [remote(bias, block(bh, m), next_sem(), kr.at[m, 2], x_peer)]
    memory_z = []
    for d in (3, 2, 1, 0):
        zz = flip_z(z, d)
        for p, (a, b, r) in enumerate(((keys, kh, relay_k), (vals, vh, relay_v))):
            view, sem = (r.at[d - 1], rr.at[d - 1, p]) if d else (block(b, m), kr.at[m, p])
            memory_x.append(remote(lanes(a, zz * 2 + 1 - x), view, next_sem(), sem, x_peer))
            if d:
                memory_z.append(
                    remote(lanes(a, zz * 2 + x), block(b, m), next_sem(), kr.at[m, p], device(y, zz, x, c))
                )
        if d:
            memory_z.append(remote(bias, block(bh, m), next_sem(), kr.at[m, 2], device(y, zz, x, c)))

    def relay():
        view = block(bh, beside)
        remote(view, view, ko.at[0], kr.at[beside, 2], x_peer).wait_recv()
        for d in (3, 2, 1):
            target = device(y, flip_z(z, d), x, c)
            for p, (b, r) in enumerate(((kh, relay_k), (vh, relay_v))):
                room = r.at[d - 1]
                remote(room, room, ko.at[0], rr.at[d - 1, p], x_peer).wait_recv()
                go(remote(room, block(b, beside), next_sem(), kr.at[beside, p], target))
            go(remote(view, view, next_sem(), kr.at[beside, 2], target))

    greet([device(y, a, b, c) for a, b in plane] + [y_peer, c_peer])
    own_sends(EARLY)
    push(spot(2, z, x, c), y_peer, src[2].at[1 - y])
    go(remote(og, ogc.at[1], pair.at[0], pair.at[1], y_peer))
    homes = [
        pltpu.make_async_copy(src[2].at[y] if p == 2 else src[p], spot(p, z, x, c)[0], own_sem.at[p])
        for p in range(5)
    ]
    for p, (a, b) in enumerate(((lanes(keys, chip), kh), (lanes(vals, chip), vh), (bias, bh))):
        homes.append(pltpu.make_async_copy(a, block(b, m), ko.at[p]))
    homes.append(pltpu.make_async_copy(og, ogc.at[0], own_sem.at[5]))
    for copy in homes:
        copy.start()

    for copy in memory_x:
        go(copy)

    @pl.when(inner == 0)
    def _():
        for copy in memory_z:
            copy.start()

    inputs = x_ref[...].astype(F32)
    normed = inputs * lax.rsqrt(jnp.mean(inputs * inputs, axis=-1, keepdims=True) + epsilon)

    line_event(1, EARLY)
    y_event(0, EARLY)
    line_event(2, EARLY)
    line_event(3, EARLY)

    @pl.when(inner == 1)
    def _():
        for copy in memory_z:
            copy.start()

    x_event(0, EARLY)
    relay()
    for p, (a, b) in enumerate(((lanes(keys, chip), kh), (lanes(vals, chip), vh), (bias, bh))):
        go(remote(a, block(b, m), kcs.at[7, p], kr.at[m, p], c_peer))
    own_sends((3, 2))
    mirror()
    for i in (1, 2, 3):
        y_event(i, EARLY)
    for i in (1, 2, 3):
        x_event(i, EARLY)
    for i in range(4):
        corner_event(i, EARLY)
    core_events(EARLY)
    for copy in homes:
        copy.wait()

    packed = dst[4][...].reshape(32 * 16, 128)
    gain = expand(packed, 0, own_rows)
    gain_out[...] = jnp.concatenate(
        [gain, expand(packed, own_rows, own_rows), jnp.zeros((6, width), F32)], axis=0
    )
    low = (normed * gain).astype(BF16)
    h_ref[...] = low
    for i, ref in enumerate((q_ref, k_ref, v_ref)):
        weight = dst[0][:, :, i * width : (i + 1) * width].reshape(width, width)
        ref[...] = jnp.dot(low, weight, preferred_element_type=F32).astype(BF16)

    others = [(chip + d) % 8 for d in range(1, 8)]
    peers = [{"dp": y, "mem": o * ranks + c} for o in others]
    for d, (o, peer) in enumerate(zip(others, peers)):
        go(remote(lanes(q_ref, o), qh.at[chip], qs.at[d], qr.at[chip], peer))
    mine = pltpu.make_async_copy(lanes(q_ref, chip), qh.at[chip], ko.at[0])
    mine.start()

    below = lax.broadcasted_iota(jnp.int32, (rows, rows), 1)
    ok = (below <= lax.broadcasted_iota(jnp.int32, (rows, rows), 0)) & (below < lens[0, 0])
    lane = lax.broadcasted_iota(jnp.int32, (rows, 128), 1)
    tops = jnp.zeros((rows, 128), F32)
    sums = jnp.zeros((rows, 128), F32)
    for i in range(HEADS):
        at = slice(i * WIDTH, (i + 1) * WIDTH)
        s = lax.dot_general(
            q_ref[:, at], k_ref[:, at], (((1,), (1,)), ((), ())), preferred_element_type=F32
        )
        s = jnp.where(ok, s * factor, neg_big)
        top = jnp.max(s, axis=1, keepdims=True)
        p = jnp.exp2(s - top)
        tops = jnp.where(lane == i, top, tops)
        sums = jnp.where(lane == i, jnp.sum(p, axis=1, keepdims=True), sums)
        loc[:, at] = jnp.dot(p.astype(BF16), v_ref[:, at], preferred_element_type=F32)
    st[0] = tops
    st[1] = sums
    for p in LATE:
        line_event(1, (p,))
    x_event(0, LATE)

    for i, (zz, xx) in reversed(list(enumerate(plane))):
        other = zz * 4 + xx * 2 + c
        for p, b in enumerate((kh, vh, bh)):
            view = block(b, other)
            if p < 2 or i < 6:
                remote(view, view, ko.at[p], kr.at[other, p], c_peer).wait_recv()
            go(remote(view, view, kcs.at[i, p], kr.at[other, p], c_peer))
    for zz, xx in [(z, x)] + plane[::-1]:
        other = zz * 4 + xx * 2 + 1 - c
        for p, b in enumerate((kh, vh, bh)):
            remote(block(b, other), block(b, other), ko.at[p], kr.at[other, p], c_peer).wait_recv()
    mine.wait()
    for o in others:
        remote(qh.at[o], qh.at[o], ko.at[0], qr.at[o], c_peer).wait_recv()

    def attend(d, _):
        j = (chip + d) % 8
        start, stop, base, window = key_window(j, ranks, c, docs, sizes, total)
        q = qh[j]
        parts = 3
        chunk = window // parts

        def step(t, carry):
            top, tsum, acc = carry
            at = base + t * chunk
            s = lax.dot_general(
                q, rows_of(kh, at, chunk), (((1,), (1,)), ((), ())), preferred_element_type=F32
            )
            s = s * factor + window_bias(bh, at, chunk, start, stop)
            best = jnp.maximum(top, jnp.max(s, axis=1, keepdims=True))
            p = jnp.exp2(s - best)
            keep = jnp.exp2(top - best)
            tsum = tsum * keep + jnp.sum(p, axis=1, keepdims=True)
            acc = acc * keep + jnp.dot(p.astype(BF16), rows_of(vh, at, chunk), preferred_element_type=F32)
            return best, tsum, acc

        top, tsum, acc = lax.fori_loop(
            0,
            parts,
            step,
            (jnp.full((rows, 1), neg_big, F32), jnp.zeros((rows, 1), F32), jnp.zeros((rows, WIDTH), F32)),
        )
        oh[j] = (acc / tsum).astype(BF16)
        lh[j] = jnp.broadcast_to(top + jnp.log2(tsum), (rows, rows)).T[0:8]
        return 0

    def answer(d):
        j = (chip + d) % 8
        peer = {"dp": y, "mem": j * ranks + c}
        go(remote(oh.at[j], lanes(mo, chip), os_.at[d, 0], or_.at[chip, 0], peer))
        go(remote(lh.at[j], ml.at[chip], os_.at[d, 1], or_.at[chip, 1], peer))

    for d, p in zip((1, 3, 5), LATE):
        lax.fori_loop(d, d + 2, attend, 0)
        answer(d)
        answer(d + 1)
        line_event(2, (p,))
    lax.fori_loop(7, 9, attend, 0)
    answer(7)
    backs = [
        pltpu.make_async_copy(oh.at[chip], lanes(mo, chip), ko.at[0]),
        pltpu.make_async_copy(lh.at[chip], ml.at[chip], ko.at[1]),
    ]
    for copy in backs:
        copy.start()
    x_event(1, LATE)
    for p in LATE:
        line_event(3, (p,))
        x_event(2, (p,))
    for o in others:
        remote(lanes(mo, o), lanes(mo, o), ko.at[0], or_.at[o, 0], c_peer).wait_recv()
        remote(ml.at[o], ml.at[o], ko.at[1], or_.at[o, 1], c_peer).wait_recv()
    for copy in backs:
        copy.wait()

    head_row = lax.broadcasted_iota(jnp.int32, (8, rows), 0)
    gathered = jnp.zeros((8, rows), F32)
    for i in range(HEADS):
        gathered = jnp.where(head_row == i, ml[i], gathered)
    mem_lse = columns(gathered)
    tops, sums = st[0], st[1]
    known = lane < HEADS
    loc_lse = jnp.where(known, tops + jnp.log2(jnp.where(known, sums, 1.0)), 0.0)
    best = jnp.maximum(loc_lse, mem_lse)
    whole = best + jnp.log2(jnp.exp2(loc_lse - best) + jnp.exp2(mem_lse - best))
    tot[...] = whole
    loc_scale = jnp.exp2(tops - whole)
    mem_scale = jnp.exp2(mem_lse - whole)
    for i in range(HEADS):
        at = slice(i * WIDTH, (i + 1) * WIDTH)
        value = loc[:, at] * loc_scale[:, i : i + 1] + mo[:, at].astype(F32) * mem_scale[:, i : i + 1]
        att[:, at] = value
        o_low[:, at] = value.astype(BF16)
    weight = dst[1][...].reshape(width, width)
    first = x_ref[...].astype(F32) + jnp.dot(o_low[...], weight, preferred_element_type=F32)
    first_out[...] = first
    normed_two = first * lax.rsqrt(jnp.mean(first * first, axis=-1, keepdims=True) + epsilon)
    h2c[0] = (normed_two * gain_out[1:2]).astype(BF16)
    go(remote(h2c.at[0], h2c.at[1], pair.at[2], pair.at[3], y_peer))
    x_event(3, LATE)
    core_events(LATE)
    remote(ogc.at[1], ogc.at[1], pair.at[0], pair.at[1], y_peer).wait_recv()
    remote(h2c.at[1], h2c.at[1], pair.at[2], pair.at[3], y_peer).wait_recv()
    for copy in memory_z:
        copy.wait_send()
    for copy in pending:
        copy.wait_send()

    @pl.when(inner == 1)
    def _():
        for copy in inner_pending:
            copy.wait_send()


def front(docs, sizes, lens, tokens, out_grad, pieces, keys, values, bias, own_rows):
    dma = pltpu.SemaphoreType.DMA
    rows, width = tokens.shape
    total = keys.shape[0] * 16
    shape = jax.ShapeDtypeStruct
    wide = shape((rows, width), BF16)
    outs = [
        shape((rows, width), F32),
        wide,
        shape((rows, width), F32),
        shape((rows, 128), F32),
        wide,
        wide,
        wide,
        wide,
        shape((8, rows, WIDTH), BF16),
        shape((8, width), F32),
        shape((2, rows, width), BF16),
        shape((2, rows, width), BF16),
    ]
    counts = (32, 32, 32, 16, 32)
    outs += [shape((n,) + a.shape[-2:], a.dtype) for n, a in zip(counts, pieces)]
    outs += [shape((total, KEYS, WIDTH), BF16)] * 2 + [shape((total, 8, KEYS), F32)]
    spaces = [VM] * 12 + [VM, VM, ANY, ANY, VM] + [VM] * 3
    return pl.pallas_call(
        functools.partial(front_kernel, own_rows),
        out_shape=outs,
        in_specs=[SM] * 3 + [VM] * 10,
        out_specs=spaces,
        scratch_shapes=[
            pltpu.VMEM((8, rows, WIDTH), BF16),
            pltpu.VMEM((8, 8, rows), F32),
            pltpu.VMEM((rows, width), BF16),
            pltpu.VMEM((8, 8, rows), F32),
            pltpu.VMEM((rows, width), F32),
            pltpu.VMEM((2, rows, 128), F32),
            pltpu.VMEM((3,) + keys.shape[:2] + (WIDTH,), BF16),
            pltpu.VMEM((3,) + keys.shape[:2] + (WIDTH,), BF16),
            dma((6,)),
            dma((32, 5)),
            dma((224,)),
            dma((3,)),
            dma((16, 3)),
            dma((3, 2)),
            dma((8, 3)),
            dma((7,)),
            dma((8,)),
            dma((8, 2)),
            dma((8, 2)),
            dma((4,)),
        ],
        compiler_params=pltpu.CompilerParams(
            collective_id=0, has_side_effects=True, vmem_limit_bytes=48 << 20
        ),
        name="front",
    )(docs, sizes, lens, tokens, out_grad, *pieces, keys, values, bias)


def key_span(j, ranks, docs, sizes, rank_ref):
    doc = docs[0, j * ranks + rank_ref[0]]
    start = jnp.int32(0)
    stop = jnp.int32(0)
    for i in range(sizes.shape[1]):
        size = sizes[0, i]
        start = start + jnp.where(i < doc, size, 0)
        stop = stop + jnp.where(i <= doc, size, 0)
    return start, stop


def forward_kernel(ranks, block, docs, sizes, rank_ref, q_ref, k_ref, v_ref, bias_ref, o_ref, lse_ref):
    j = pl.program_id(0)
    start, stop = key_span(j, ranks, docs, sizes, rank_ref)
    q = q_ref[0]
    factor = WIDTH ** (-0.5) * LOG2E

    def step(b, carry):
        top, total, acc = carry
        s = lax.dot_general(
            q, rows_of(k_ref, b * block, block), (((1,), (1,)), ((), ())), preferred_element_type=F32
        )
        s = s * factor + window_bias(bias_ref, b * block, block, start, stop)
        best = jnp.maximum(top, jnp.max(s, axis=1, keepdims=True))
        p = jnp.exp2(s - best)
        keep = jnp.exp2(top - best)
        total = total * keep + jnp.sum(p, axis=1, keepdims=True)
        acc = acc * keep + jnp.dot(
            p.astype(BF16), rows_of(v_ref, b * block, block), preferred_element_type=F32
        )
        return best, total, acc

    rows = q.shape[0]
    top, total, acc = lax.fori_loop(
        start // (block * KEYS),
        (stop + block * KEYS - 1) // (block * KEYS),
        step,
        (jnp.full((rows, 1), neg_big, F32), jnp.zeros((rows, 1), F32), jnp.zeros((rows, WIDTH), F32)),
    )
    o_ref[0] = (acc / total).astype(BF16)
    lse = jnp.broadcast_to(top + jnp.log2(total), (rows, rows))
    lse_ref[0] = lse.T[0:8]


def backward_kernel(
    ranks, block, docs, sizes, rank_ref, q_ref, do_ref, stat_ref, k_ref, v_ref, bias_ref, dq_ref
):
    j = pl.program_id(0)
    start, stop = key_span(j, ranks, docs, sizes, rank_ref)
    q, do = q_ref[0], do_ref[0]
    rows = q.shape[0]
    factor = WIDTH ** (-0.5) * LOG2E
    stat = stat_ref[0]
    lse = jnp.broadcast_to(stat[0:1], (rows, rows)).T[:, 0:1]
    delta = jnp.broadcast_to(stat[1:2], (rows, rows)).T[:, 0:1]

    def step(b, acc):
        keys = rows_of(k_ref, b * block, block)
        s = lax.dot_general(q, keys, (((1,), (1,)), ((), ())), preferred_element_type=F32)
        p = jnp.exp2(s * factor + (window_bias(bias_ref, b * block, block, start, stop) - lse))
        dp = lax.dot_general(do, rows_of(v_ref, b * block, block), (((1,), (1,)), ((), ())), preferred_element_type=F32)
        ds = (p * (dp - delta)).astype(BF16)
        return acc + jnp.dot(ds, keys, preferred_element_type=F32)

    acc = lax.fori_loop(
        start // (block * KEYS), (stop + block * KEYS - 1) // (block * KEYS), step, jnp.zeros((rows, WIDTH), F32)
    )
    dq_ref[0] = (acc * WIDTH ** (-0.5)).astype(BF16)


def memory_forward(ranks, docs, sizes, rank, q, kh, vh, bh):
    count, rows, _ = q.shape
    seg = pl.BlockSpec((1, rows, WIDTH), lambda j: (j, 0, 0))
    stat = pl.BlockSpec((1, 8, rows), lambda j: (j, 0, 0))
    block = 8
    return pl.pallas_call(
        functools.partial(forward_kernel, ranks, block),
        grid=(count,),
        out_shape=[
            jax.ShapeDtypeStruct((count, rows, WIDTH), BF16),
            jax.ShapeDtypeStruct((count, 8, rows), F32),
        ],
        in_specs=[SM, SM, SM, seg, VM, VM, VM],
        out_specs=[seg, stat],
        compiler_params=pltpu.CompilerParams(vmem_limit_bytes=48 << 20),
        name="memory_forward",
    )(docs, sizes, rank, q, kh, vh, bh)


def memory_backward(ranks, docs, sizes, rank, q, do, stats, kh, vh, bh):
    count, rows, _ = q.shape
    seg = pl.BlockSpec((1, rows, WIDTH), lambda j: (j, 0, 0))
    stat = pl.BlockSpec((1, 8, rows), lambda j: (j, 0, 0))
    block = 8
    return pl.pallas_call(
        functools.partial(backward_kernel, ranks, block),
        grid=(count,),
        out_shape=jax.ShapeDtypeStruct((count, rows, WIDTH), BF16),
        in_specs=[SM, SM, SM, seg, seg, stat, VM, VM, VM],
        out_specs=seg,
        compiler_params=pltpu.CompilerParams(vmem_limit_bytes=48 << 20),
        name="memory_backward",
    )(docs, sizes, rank, q, do, stats, kh, vh, bh)


DEPTH = 3


def contract(row, first, lanes):
    width = row.shape[1]
    count = width // 32
    shard = lax.broadcasted_iota(jnp.int32, (32, width), 0)
    column = lax.broadcasted_iota(jnp.int32, (32, width), 1)
    masked = jnp.where(column // count == shard, jnp.broadcast_to(row, (32, width)), 0.0)
    feature = lax.broadcasted_iota(jnp.int32, (width, lanes), 0)
    lane = lax.broadcasted_iota(jnp.int32, (width, lanes), 1)
    pick = (lane == first + feature % count).astype(F32)
    return jnp.dot(masked, pick, preferred_element_type=F32, precision=lax.Precision.HIGHEST)


def tiles_of(width):
    for count in (4, 3, 2, 1):
        if width % (count * 128) == 0 and width // count >= 512:
            return count, width // count
    return 1, width


def back_kernel(*refs):
    docs, sizes, lens = refs[:3]
    x_ref, gains, first, tot, att, dh_own, dh_far, out_own, out_far = refs[3:12]
    h, o, h2, dgu, hid, og = refs[12:18]
    q_ref, k_ref, v_ref, qh, kh, vh, bh = refs[18:25]
    w_in, w_out = refs[25:27]
    output, input_grad, g_q, g_k, g_v, g_o, g_gate, g_up, g_down, g_small = refs[27:37]
    stage, cores, firsts, seconds, lines = (refs[37 + 6 * i : 43 + 6 * i] for i in range(5))
    ht, ot, h2t, hidt, dqs, dkv, dql, das, dys, do, small, sst, doh, sth, dqo, dqm, wbuf = refs[67:84]
    dh_in, out_in, far_out, far_in = refs[84:88]
    cs, cr, fs, fr, ss, sr, zs, zr, own, dsend, drecv, qsend, qrecv, wsem, psend, precv = refs[88:]
    y, z, x, c = place()
    ranks = 2
    chip = z * 2 + x
    rows, width = x_ref.shape
    half = hid.shape[1]
    factor = WIDTH ** (-0.5) * LOG2E
    y_peer, x_peer, c_peer = device(1 - y, z, x, c), device(y, z, 1 - x, c), device(y, z, x, 1 - c)
    others = [(chip + d) % 8 for d in range(1, 8)]
    peers = [{"dp": y, "mem": p * ranks + c} for p in others]
    pending = []

    def go(copy):
        copy.start()
        pending.append(copy)

    def wait(dst, sem):
        remote(dst, dst, own.at[0], sem, c_peer).wait_recv()

    def lanes(ref, i):
        return ref.at[:, pl.ds(pl.multiple_of(i * WIDTH, WIDTH), WIDTH)]

    def load(source, i):
        copy = pltpu.make_async_copy(source, wbuf.at[i], wsem.at[i])
        copy.start()
        return copy

    def weight_part(i):
        return w_in.at[:, :, i * width : (i + 1) * width]

    greet(peers + [y_peer, c_peer])

    left = (ht, ht, ot, h2t, hidt)
    right = (dqs, dkv, das, dgu, og)
    order = [(k, d) for d in (3, 2, 1, 0) for k in (1, 0)]
    split = (3, 4)

    def used(i, group):
        return [p for p in group if p != 4 or order[i][0] == 0]

    def held(i, p):
        return i // 2 if p == 4 else i

    def produce(i, group):
        k, d = order[i]
        zz = flip_z(z, d)
        for p in used(i, group):
            u = zz if p == 4 else (1 - y if k else y) * 4 + zz
            room = stage[p].at[i % DEPTH]
            if p == 5:
                for n in range(4):
                    room[n] = small[u * 4 + n]
            else:
                size = 4 * stage[p].shape[2]
                block = left[p][pl.ds(pl.multiple_of(u * size, 32), size), :]
                count, tile = tiles_of(stage[p].shape[3])

                def some(t, _):
                    at = pl.ds(pl.multiple_of(t * tile, 128), tile)
                    part = jnp.dot(block, right[p][:, at], preferred_element_type=F32)
                    room[:, :, at] = part.astype(BF16).reshape(4, size // 4, tile)
                    return 0

                lax.fori_loop(0, count, some, 0)
            for xx in range(2):
                core_copy(i, p, xx).start()

    def core_copy(i, p, xx):
        return remote(
            stage[p].at[i % DEPTH, xx * 2 + 1 - c], cores[p].at[held(i, p), xx], cs.at[i, xx, p], cr.at[i, xx, p], c_peer
        )

    def merge(into, other):
        count, tile = tiles_of(into.shape[1])

        def some(t, _):
            at = pl.ds(pl.multiple_of(t * tile, 128), tile)
            into[:, at] = (into[:, at].astype(F32) + other[:, at].astype(F32)).astype(into.dtype)
            return 0

        lax.fori_loop(0, count, some, 0)

    def after_core(i, group):
        k, d = order[i]
        for p in used(i, group):
            for xx in (1 - x, x):
                into = cores[p].at[held(i, p), xx]
                wait(into, cr.at[i, xx, p])
                merge(into, stage[p].at[i % DEPTH, xx * 2 + c])
            if p in split:
                n = held(i, p)
                go(remote(cores[p].at[n, 1 - x], firsts[p].at[n], fs.at[i, 0, p], fr.at[i, 0, p], x_peer))
            elif k == 1:
                t = i // 2
                for xx in range(2):
                    go(remote(cores[p].at[i, xx], firsts[p].at[t + 4 * xx], fs.at[i, xx, p], fr.at[t, xx, p], y_peer))
            for xx in range(2):
                core_copy(i, p, xx).wait_send()

    def to_line(i, p):
        k, d = order[i]
        if d:
            n = d - 1 + 3 * k
            go(remote(cores[p].at[held(i, p), x], lines[p].at[n], zs.at[n, p], zr.at[n, p], device(y, flip_z(z, d), x, c)))

    def after_first(i, group):
        k, d = order[i]
        t = i // 2
        for p in used(i, group):
            if p in split:
                n = held(i, p)
                wait(firsts[p].at[n], fr.at[i, 0, p])
                merge(cores[p].at[n, x], firsts[p].at[n])
                to_line(i, p)
            elif k == 0:
                for xx in (1 - x, x):
                    room = firsts[p].at[t + 4 * xx]
                    wait(room, fr.at[t, xx, p])
                    merge(cores[p].at[i, xx], room)
                go(remote(cores[p].at[i, 1 - x], seconds[p].at[t], ss.at[t, p], sr.at[t, p], x_peer))

    def after_second(i, group):
        t = i // 2
        for p in group:
            wait(seconds[p].at[t], sr.at[t, p])
            merge(cores[p].at[i, x], seconds[p].at[t])
            to_line(i, p)

    def along(p, k, at):
        total = cores[p][held(7 - k, p), x, :, at].astype(F32)
        for d in range(3):
            total = total + lines[p][d + 3 * k, :, at].astype(F32)
        return total

    def line_wait(p, k):
        for d in range(3):
            wait(lines[p].at[d + 3 * k], zr.at[d + 3 * k, p])

    def finish(group):
        for p in group:
            line_wait(p, 0)
            outs = ((g_q,), (g_k, g_v), (g_o,), (), (g_down,), (g_small,))[p]
            for i, out in enumerate(outs):
                span = cores[p].shape[3] // len(outs)
                out[...] = along(p, 0, slice(i * span, (i + 1) * span))

    def attend(d, _):
        j = (chip + d) % 8
        start, stop, base, window = key_window(j, ranks, c, docs, sizes, kh.shape[0])
        q, dout, stat = qh[j], doh[j], sth[j]
        lse = jnp.broadcast_to(stat[0:1], (rows, rows)).T[:, 0:1]
        delta = jnp.broadcast_to(stat[1:2], (rows, rows)).T[:, 0:1]
        parts = 3
        chunk = window // parts

        def step(t, acc):
            at = base + t * chunk
            keys = rows_of(kh, at, chunk)
            s = lax.dot_general(q, keys, (((1,), (1,)), ((), ())), preferred_element_type=F32)
            p = jnp.exp2(s * factor + (window_bias(bh, at, chunk, start, stop) - lse))
            dp = lax.dot_general(
                dout, rows_of(vh, at, chunk), (((1,), (1,)), ((), ())), preferred_element_type=F32
            )
            ds = (p * (dp - delta)).astype(BF16)
            return acc + jnp.dot(ds, keys, preferred_element_type=F32)

        acc = lax.fori_loop(0, parts, step, jnp.zeros((rows, WIDTH), F32))
        dqo[j] = (acc * WIDTH ** (-0.5)).astype(BF16)
        return 0

    def answer(d):
        j = (chip + d) % 8
        go(remote(dqo.at[j], lanes(dqm, chip), qsend.at[d - 1], qrecv.at[chip], {"dp": y, "mem": j * ranks + c}))

    ffn, query, others_att, gain = (3, 4), (0,), (1, 2), (5,)
    go(remote(dh_far, dh_in, psend.at[0], precv.at[0], y_peer))
    go(remote(out_far, out_in, psend.at[1], precv.at[1], y_peer))
    load_out = load(w_out, 0)
    load_key = load(weight_part(1), 1)
    h2t[...] = h2[...].T
    produce(0, ffn)
    hidt[...] = hid[...].T
    produce(1, ffn)
    after_core(0, ffn)
    produce(2, ffn)
    after_core(1, ffn)

    wait(dh_in, precv.at[0])
    residual = first[...]
    inverse_two = lax.rsqrt(jnp.mean(residual * residual, axis=-1, keepdims=True) + epsilon)
    normed_two = residual * inverse_two
    dh2 = dh_own[...] + dh_in[...].astype(F32)
    pulled = contract(jnp.sum(dh2 * normed_two, axis=0, keepdims=True), width // 32, 128)
    small[...] = jnp.broadcast_to(pulled[:, None, :], small.shape)
    dn = dh2 * gains[1:2]
    dy = og[0:rows].astype(F32) + inverse_two * (
        dn - normed_two * jnp.mean(dn * normed_two, axis=-1, keepdims=True)
    )
    dys[...] = dy
    low = dy.astype(BF16)
    das[...] = low
    load_out.wait()
    do[...] = lax.dot_general(
        low, wbuf[0].reshape(width, width), (((1,), (1,)), ((), ())), preferred_element_type=F32
    ).astype(BF16)
    load_value = load(weight_part(2), 0)

    lane = lax.broadcasted_iota(jnp.int32, (rows, 128), 1)
    deltas = jnp.zeros((rows, 128), F32)
    for i in range(HEADS):
        at = slice(i * WIDTH, (i + 1) * WIDTH)
        part = jnp.sum(do[:, at].astype(F32) * att[:, at], axis=1, keepdims=True)
        deltas = jnp.where(lane == i, part, deltas)
    tot_rows, delta_rows = tot[...].T, deltas.T
    head_row = lax.broadcasted_iota(jnp.int32, (8, rows), 0)
    for i in range(HEADS):
        sst[i] = jnp.where(head_row == 0, tot_rows[i : i + 1], delta_rows[i : i + 1])
    for d, (p, peer) in enumerate(zip(others, peers)):
        go(remote(lanes(do, p), doh.at[chip], dsend.at[d, 0], drecv.at[chip, 0], peer))
        go(remote(sst.at[p], sth.at[chip], dsend.at[d, 1], drecv.at[chip, 1], peer))
    homes = [
        pltpu.make_async_copy(lanes(do, chip), doh.at[chip], own.at[1]),
        pltpu.make_async_copy(sst.at[chip], sth.at[chip], own.at[2]),
    ]
    for copy in homes:
        copy.start()
    ht[...] = h[...].T
    ot[...] = o[...].T
    produce(3, ffn)
    after_core(2, ffn)

    below = lax.broadcasted_iota(jnp.int32, (rows, rows), 1)
    ok = (below <= lax.broadcasted_iota(jnp.int32, (rows, rows), 0)) & (below < lens[0, 0])
    for i in range(HEADS):
        at = slice(i * WIDTH, (i + 1) * WIDTH)
        q, k, v, dout = q_ref[:, at], k_ref[:, at], v_ref[:, at], do[:, at]
        s = lax.dot_general(q, k, (((1,), (1,)), ((), ())), preferred_element_type=F32)
        p = jnp.where(ok, jnp.exp2(s * factor - tot[:, i : i + 1]), 0.0)
        dp = lax.dot_general(dout, v, (((1,), (1,)), ((), ())), preferred_element_type=F32)
        ds = (p * (dp - deltas[:, i : i + 1])).astype(BF16)
        dql[:, at] = jnp.dot(ds, k, preferred_element_type=F32) * WIDTH ** (-0.5)
        dk = lax.dot_general(ds, q, (((0,), (0,)), ((), ())), preferred_element_type=F32) * WIDTH ** (-0.5)
        dv = lax.dot_general(p.astype(BF16), dout, (((0,), (0,)), ((), ())), preferred_element_type=F32)
        dkv[:, at] = dk.astype(BF16)
        dkv[:, width + i * WIDTH : width + (i + 1) * WIDTH] = dv.astype(BF16)

    produce(0, others_att)
    produce(1, others_att)
    after_core(0, others_att)
    produce(2, others_att)
    after_core(1, others_att)
    after_core(2, others_att)
    for copy in homes:
        copy.wait()
    for p in others:
        wait(doh.at[p], drecv.at[p, 0])
        wait(sth.at[p], drecv.at[p, 1])
    lax.fori_loop(1, 3, attend, 0)
    answer(1)
    answer(2)
    after_first(0, ffn)
    after_core(3, ffn)
    produce(4, ffn)
    produce(3, others_att)
    produce(4, others_att)
    lax.fori_loop(3, 5, attend, 0)
    answer(3)
    answer(4)
    after_first(1, ffn)
    after_core(4, ffn)
    produce(5, ffn)
    after_core(3, others_att)
    after_core(4, others_att)
    after_first(1, others_att)
    lax.fori_loop(5, 7, attend, 0)
    answer(5)
    answer(6)
    after_first(2, ffn)
    after_core(5, ffn)
    produce(6, ffn)
    produce(5, others_att)
    produce(6, others_att)
    after_first(3, others_att)
    lax.fori_loop(7, 9, attend, 0)
    answer(7)
    back_copy = pltpu.make_async_copy(dqo.at[chip], lanes(dqm, chip), own.at[1])
    back_copy.start()
    after_first(3, ffn)
    after_core(6, ffn)
    produce(7, ffn)
    after_core(5, others_att)
    after_core(6, others_att)
    produce(7, others_att)
    after_second(1, others_att)
    after_core(7, ffn)
    wait(out_in, precv.at[1])
    output[...] = (residual + out_own[...] + out_in[...].astype(F32)).astype(BF16)
    load_key.wait()
    dh = lax.dot_general(
        dkv[:, :width], wbuf[1].reshape(width, width), (((1,), (1,)), ((), ())), preferred_element_type=F32
    )
    load_query = load(weight_part(0), 1)
    load_value.wait()
    dh = dh + lax.dot_general(
        dkv[:, width:], wbuf[0].reshape(width, width), (((1,), (1,)), ((), ())), preferred_element_type=F32
    )
    after_first(4, ffn)
    after_first(5, others_att)
    after_core(7, others_att)
    for p in others:
        wait(lanes(dqm, p), qrecv.at[p])
    back_copy.wait()
    dqs[...] = (dql[...] + dqm[...].astype(F32)).astype(BF16)
    produce(0, query)
    produce(1, query)
    after_core(0, query)
    produce(2, query)
    after_core(1, query)
    after_core(2, query)
    after_first(5, ffn)
    produce(3, query)
    produce(4, query)
    after_core(3, query)
    after_core(4, query)
    produce(5, query)
    produce(6, query)
    after_core(5, query)
    after_core(6, query)
    produce(7, query)
    after_core(7, query)
    after_second(3, others_att)
    after_first(7, others_att)

    load_query.wait()
    dh = dh + lax.dot_general(
        dqs[...], wbuf[1].reshape(width, width), (((1,), (1,)), ((), ())), preferred_element_type=F32
    )
    inputs = x_ref[...].astype(F32)
    inverse = lax.rsqrt(jnp.mean(inputs * inputs, axis=-1, keepdims=True) + epsilon)
    normed = inputs * inverse
    pulled = contract(jnp.sum(dh * normed, axis=0, keepdims=True), 0, 128)
    small[...] = small[...] + jnp.broadcast_to(pulled[:, None, :], small.shape)
    for i in range(8):
        produce(i, gain)
        if i:
            after_core(i - 1, gain)
    after_core(7, gain)
    after_first(6, ffn)
    after_first(1, query)
    after_first(7, ffn)
    after_first(3, query)
    for i in (1, 3, 5, 7):
        after_first(i, gain)
    dn = dh * gains[0:1]
    input_grad[...] = (
        dys[...] + inverse * (dn - normed * jnp.mean(dn * normed, axis=-1, keepdims=True))
    ).astype(BF16)
    after_second(5, others_att)
    after_first(5, query)
    after_second(1, query)
    after_first(7, query)
    after_second(7, others_att)
    after_second(3, query)
    for i in (1, 3, 5):
        after_second(i, gain)

    line_wait(3, 1)
    far_out[...] = along(3, 1, slice(0, 2 * half)).astype(BF16)
    go(remote(far_out, far_in, psend.at[2], precv.at[2], y_peer))
    after_second(5, query)
    after_second(7, query)
    after_second(7, gain)
    line_wait(3, 0)
    near_at = pl.ds(pl.multiple_of(y * half, 128), half)
    far_at = pl.ds(pl.multiple_of((1 - y) * half, 128), half)
    g_gate[:, near_at] = along(3, 0, slice(0, half))
    g_up[:, near_at] = along(3, 0, slice(half, 2 * half))
    finish((4, 1, 2))
    wait(far_in, precv.at[2])
    g_gate[:, far_at] = far_in[:, :half].astype(F32)
    g_up[:, far_at] = far_in[:, half:].astype(F32)
    finish((0, 5))
    for copy in pending:
        copy.wait_send()


def back(scalars, f32_args, bf16_args, heads_args, weights):
    dma = pltpu.SemaphoreType.DMA
    x = f32_args[0]
    h, o, h2, dgu, hid, og = bf16_args
    rows, width = x.shape
    half = hid.shape[1]
    own = width // 32
    down = half // 16
    shapes = [
        ((own, width), BF16),
        ((own, 2 * width), BF16),
        ((own, width), BF16),
        ((own, 2 * half), BF16),
        ((down, width), BF16),
        ((8, 128), F32),
    ]

    def buffers(*leads):
        return [pltpu.VMEM(lead + s, t) for lead, (s, t) in zip(leads, shapes)]

    none = (1,)

    shape = jax.ShapeDtypeStruct
    outs = [shape((rows, width), BF16)] * 2 + [shape((own, width), F32)] * 4
    outs += [shape((own, 2 * half), F32)] * 2 + [shape((down, width), F32), shape((8, 128), F32)]
    return pl.pallas_call(
        back_kernel,
        out_shape=outs,
        in_specs=[SM] * 3 + [VM] * 22 + [ANY] * 2,
        out_specs=[VM] * 10,
        scratch_shapes=buffers(*[(DEPTH, 4)] * 6)
        + buffers(*[(8, 2)] * 4, (4, 2), (8, 2))
        + buffers(*[(8,)] * 4, (4,), (8,))
        + buffers((4,), (4,), (4,), none, none, (4,))
        + buffers((3,), (3,), (3,), (6,), (3,), (3,))
        + [
            pltpu.VMEM((width, rows), BF16),
            pltpu.VMEM((width, rows), BF16),
            pltpu.VMEM((width, 2 * rows), BF16),
            pltpu.VMEM((half, 2 * rows), BF16),
            pltpu.VMEM((rows, width), BF16),
            pltpu.VMEM((rows, 2 * width), BF16),
            pltpu.VMEM((rows, width), F32),
            pltpu.VMEM((rows, width), BF16),
            pltpu.VMEM((rows, width), F32),
            pltpu.VMEM((rows, width), BF16),
            pltpu.VMEM((32, 8, 128), F32),
            pltpu.VMEM((8, 8, rows), F32),
            pltpu.VMEM((8, rows, WIDTH), BF16),
            pltpu.VMEM((8, 8, rows), F32),
            pltpu.VMEM((8, rows, WIDTH), BF16),
            pltpu.VMEM((rows, width), BF16),
            pltpu.VMEM((2, 32, own, width), BF16),
            pltpu.VMEM((rows, width), BF16),
            pltpu.VMEM((rows, width), BF16),
            pltpu.VMEM((own, 2 * half), BF16),
            pltpu.VMEM((own, 2 * half), BF16),
            dma((8, 2, 6)),
            dma((8, 2, 6)),
            dma((8, 2, 6)),
            dma((8, 2, 6)),
            dma((4, 6)),
            dma((4, 6)),
            dma((6, 6)),
            dma((6, 6)),
            dma((3,)),
            dma((7, 2)),
            dma((8, 2)),
            dma((7,)),
            dma((8,)),
            dma((2,)),
            dma((3,)),
            dma((3,)),
        ],
        compiler_params=pltpu.CompilerParams(
            collective_id=1, has_side_effects=True, vmem_limit_bytes=38 << 20
        ),
        name="back",
    )(*scalars, *f32_args, *bf16_args, *heads_args, *weights)


def settle_kernel(*refs):
    n = len(refs) // 2
    copies = [pltpu.make_async_copy(refs[i], refs[n + i], refs[2 * n].at[i]) for i in range(n)]
    for copy in copies:
        copy.start()
    for copy in copies:
        copy.wait()


def settle(arrays):
    return pl.pallas_call(
        settle_kernel,
        out_shape=[jax.ShapeDtypeStruct(a.shape, a.dtype) for a in arrays],
        in_specs=[VM] * len(arrays),
        out_specs=[ANY] * len(arrays),
        scratch_shapes=[pltpu.SemaphoreType.DMA((len(arrays),))],
        compiler_params=pltpu.CompilerParams(vmem_limit_bytes=8 << 20),
        name="settle",
    )(*arrays)


def gather_plain(pieces, keys, values, bias, ranks):
    full = [lax.all_gather(a, ("dp", "mem"), axis=0, tiled=False) for a in pieces]

    def spread(a):
        blocks = a.reshape(a.shape[0], HEADS, WIDTH).transpose(1, 0, 2)
        return lax.all_to_all(jnp.repeat(blocks, ranks, axis=0), "mem", 0, 0, tiled=True)

    return full + [
        spread(keys).reshape(-1, KEYS, WIDTH),
        spread(values).reshape(-1, KEYS, WIDTH),
        lax.all_gather(bias, "mem", axis=0, tiled=True),
    ]


def to_heads_plain(x, ranks):
    rank = lax.axis_index("mem") % ranks
    blocks = x if x.ndim == 3 else x.reshape(x.shape[0], HEADS, WIDTH).transpose(1, 0, 2)
    wide = jnp.where((jnp.arange(ranks) == rank)[None, :, None, None], blocks[:, None], 0)
    wide = wide.reshape((-1,) + blocks.shape[1:])
    got = lax.all_to_all(wide, "mem", 0, 0, tiled=True)
    return lax.dynamic_index_in_dim(got.reshape((-1, ranks) + blocks.shape[1:]), rank, 1, keepdims=False)


def to_tokens_plain(x, ranks, wide_out):
    rank = lax.axis_index("mem") % ranks
    wide = jnp.where((jnp.arange(ranks) == rank)[None, :, None, None], x[:, None], 0)
    got = lax.all_to_all(wide.reshape((-1,) + x.shape[1:]), "mem", 0, 0, tiled=True)
    got = lax.dynamic_index_in_dim(got.reshape((-1, ranks) + x.shape[1:]), rank, 1, keepdims=False)
    return got.transpose(1, 0, 2).reshape(x.shape[1], -1) if wide_out else got


def reduce_plain(h, dqkv, o, da, h2, dgu, hid, og, small):
    outs = []
    for a, b in ((h, dqkv), (o, da), (h2, dgu), (hid, og)):
        full = jnp.dot(a.T, b, preferred_element_type=F32)
        outs.append(lax.psum_scatter(full, ("dp", "mem"), scatter_dimension=0, tiled=True))
    outs.append(lax.psum_scatter(small, ("dp", "mem"), scatter_dimension=0, tiled=False))
    return outs


def normalize(values):
    inverse = lax.rsqrt(jnp.mean(values * values, axis=-1, keepdims=True) + epsilon)
    return (values * inverse, inverse)


def norm_back(grad_scaled, normed, inverse, gain_full):
    gain_grad = jnp.sum(grad_scaled * normed, axis=0)
    grad_normed = grad_scaled * gain_full
    grad_values = inverse * (
        grad_normed - normed * jnp.mean(grad_normed * normed, axis=-1, keepdims=True)
    )
    return (gain_grad, grad_values)


def feed_forward(normed_low, out_grad, gate_up, down):
    units = down.shape[0]
    both = jnp.dot(normed_low, gate_up, preferred_element_type=F32)
    gate, up = both[:, :units], both[:, units:]
    sigmoid_gate = jax.nn.sigmoid(gate)
    activated = gate * sigmoid_gate
    hidden = (activated * up).astype(BF16)
    grad_hidden = jnp.dot(out_grad, down.T, preferred_element_type=F32)
    grad_gate_up = jnp.concatenate(
        [
            (grad_hidden * up * sigmoid_gate * (1.0 + gate * (1.0 - sigmoid_gate))).astype(BF16),
            (grad_hidden * activated).astype(BF16),
        ],
        axis=1,
    )
    return hidden, grad_gate_up


def shards(
    tokens,
    gain_attn,
    w_query,
    w_key,
    w_value,
    w_out,
    gain_ffn,
    w_gate,
    w_up,
    w_down,
    mem_keys,
    mem_values,
    out_grad,
    key_mask,
    mem_sizes,
    seg_doc,
    seg_len,
):
    seg_rows, model_width = tokens.shape
    mem_count = lax.axis_size("mem")
    dp_count = lax.axis_size("dp")
    devices = mem_count * dp_count
    ranks = mem_count // HEADS
    direct = dp_count == 2 and mem_count == 16
    factor = WIDTH ** (-0.5)
    ff_width = w_gate.shape[1]
    own = gain_attn.shape[0]
    down_rows = w_down.shape[0]

    half = ff_width // 2
    if direct:
        joined = jnp.stack(
            [
                jnp.concatenate([w_gate[:, i * half : (i + 1) * half], w_up[:, i * half : (i + 1) * half]], axis=1)
                for i in range(2)
            ]
        )
    else:
        joined = jnp.concatenate([w_gate, w_up], axis=1)
    pieces = [
        jnp.concatenate([w_query, w_key, w_value], axis=1),
        w_out,
        joined,
        w_down,
        jnp.pad(jnp.concatenate([gain_attn, gain_ffn])[None], ((0, 15), (0, 128 - 2 * own))),
    ]
    bias = jnp.where(key_mask == 1, 0.0, neg_big).astype(F32).reshape(-1, 1, KEYS)
    bias = jnp.broadcast_to(bias, (bias.shape[0], 8, KEYS))
    rank = (lax.axis_index("mem") % ranks).reshape(1).astype(jnp.int32)
    if direct:
        split = (-1, KEYS, model_width)
        done = front(
            seg_doc,
            mem_sizes,
            seg_len,
            tokens,
            out_grad,
            pieces,
            mem_keys.reshape(split),
            mem_values.reshape(split),
            bias,
            own,
        )
        first, attended_low, attended, whole, normed_low, queries, keys_local, values_local = done[:8]
        q_heads, gains, pair_normed, pair_grad, joined_w, out_full, gate_up, down, _, kh, vh, bh = done[8:]
        pair_normed = pair_normed.reshape(2 * seg_rows, model_width)
        pair_grad = pair_grad.reshape(2 * seg_rows, model_width)
        gate_up = gate_up.reshape(model_width, 2 * half)
        down = down.reshape(half, model_width)
        hidden, grad_gate_up = feed_forward(pair_normed, pair_grad, gate_up, down)
        partial = jnp.dot(hidden, down, preferred_element_type=F32)
        grad_partial = jnp.dot(grad_gate_up, gate_up.T, preferred_element_type=F32)
        sums = back(
            (seg_doc, mem_sizes, seg_len),
            (
                tokens,
                gains,
                first,
                whole,
                attended,
                grad_partial[:seg_rows],
                grad_partial[seg_rows:].astype(BF16),
                partial[:seg_rows],
                partial[seg_rows:].astype(BF16),
            ),
            (normed_low, attended_low, pair_normed, grad_gate_up, hidden, pair_grad),
            (queries, keys_local, values_local, q_heads, kh, vh, bh),
            (joined_w, out_full),
        )
        small = sums[9]
        output, input_grad, g_q, g_k, g_v, g_o, g_gate, g_up, g_down = settle(sums[:9])
        return (
            output,
            input_grad,
            small[0, :own],
            g_q,
            g_k,
            g_v,
            g_o,
            small[0, own : 2 * own],
            g_gate,
            g_up,
            g_down,
        )

    inputs = tokens.astype(F32)
    normed_one, inverse_one = normalize(inputs)
    gathered = gather_plain(pieces, mem_keys, mem_values, bias, ranks)
    joined_w, out_full, gate_up, down_full, gains, kh, vh, bh = gathered
    gain_one = gains[:, 0, :own].reshape(-1).astype(F32)
    gain_two = gains[:, 0, own : 2 * own].reshape(-1).astype(F32)
    joined_w = joined_w.reshape(model_width, -1)
    out_full = out_full.reshape(model_width, -1)
    gate_up = gate_up.reshape(model_width, -1)
    down_full = down_full.reshape(ff_width, -1)
    normed_low = (normed_one * gain_one).astype(BF16)
    projected = jnp.dot(normed_low, joined_w, preferred_element_type=F32).astype(BF16)
    queries = projected[:, :model_width]
    keys_local = projected[:, model_width : 2 * model_width]
    values_local = projected[:, 2 * model_width :]
    query_heads = queries.reshape(seg_rows, HEADS, WIDTH)
    key_heads = keys_local.reshape(seg_rows, HEADS, WIDTH)
    value_heads = values_local.reshape(seg_rows, HEADS, WIDTH)
    positions = lax.iota(jnp.int32, seg_rows)
    local_ok = (positions[None, :] <= positions[:, None]) & (positions[None, :] < seg_len[0, 0])
    local_ok = local_ok[None]
    local_scores = (
        jnp.einsum("ihd,jhd->hij", query_heads, key_heads, preferred_element_type=F32) * factor
    )
    local_masked = jnp.where(local_ok, local_scores, neg_big)
    q_heads = to_heads_plain(queries, ranks)
    o_mem, lse_mem = memory_forward(ranks, seg_doc, mem_sizes, rank, q_heads, kh, vh, bh)
    mem_o = to_tokens_plain(o_mem, ranks, True).reshape(seg_rows, HEADS, WIDTH).astype(F32)
    mem_lse = to_tokens_plain(lse_mem, ranks, False)[:, 0, :] / LOG2E
    local_top = jnp.max(local_masked, axis=2)
    local_total = jnp.sum(
        jnp.where(local_ok, jnp.exp(local_masked - local_top[:, :, None]), 0.0), axis=2
    )
    local_lse = local_top + jnp.log(local_total)
    best = jnp.maximum(local_lse, mem_lse)
    log_total = best + jnp.log(jnp.exp(local_lse - best) + jnp.exp(mem_lse - best))
    local_probs = jnp.where(local_ok, jnp.exp(local_masked - log_total[:, :, None]), 0.0)
    local_low = local_probs.astype(BF16)
    attended = (
        jnp.einsum("hij,jhd->ihd", local_low, value_heads, preferred_element_type=F32)
        + mem_o * jnp.exp(mem_lse - log_total).T[..., None]
    )
    attended_low = attended.reshape(seg_rows, model_width).astype(BF16)
    first = inputs + jnp.dot(attended_low, out_full, preferred_element_type=F32)

    normed_two, inverse_two = normalize(first)
    normed_two_low = (normed_two * gain_two).astype(BF16)
    hidden, grad_gate_up = feed_forward(normed_two_low, out_grad, gate_up, down_full)
    output = (first + jnp.dot(hidden, down_full, preferred_element_type=F32)).astype(BF16)
    grad_normed_two = jnp.dot(grad_gate_up, gate_up.T, preferred_element_type=F32)
    grad_gain_two, grad_first_norm = norm_back(grad_normed_two, normed_two, inverse_two, gain_two)
    grad_first = out_grad.astype(F32) + grad_first_norm

    grad_branch = grad_first.astype(BF16)
    grad_attended = jnp.dot(grad_branch, out_full.T, preferred_element_type=F32).astype(BF16)
    grad_att_heads = grad_attended.reshape(seg_rows, HEADS, WIDTH)
    delta = jnp.sum(grad_att_heads.astype(F32) * attended, axis=-1).T
    stats = jnp.pad(jnp.stack([log_total * LOG2E, delta], axis=1), ((0, 0), (0, 6), (0, 0)))
    do_heads = to_heads_plain(grad_attended, ranks)
    stat_heads = to_heads_plain(stats, ranks)
    dq_heads = memory_backward(
        ranks, seg_doc, mem_sizes, rank, q_heads, do_heads, stat_heads, kh, vh, bh
    )
    grad_query_memory = to_tokens_plain(dq_heads, ranks, True)

    grad_value_heads = jnp.einsum(
        "hij,ihd->jhd", local_low, grad_att_heads, preferred_element_type=F32
    )
    grad_local_probs = jnp.einsum(
        "ihd,jhd->hij", grad_att_heads, value_heads, preferred_element_type=F32
    )
    grad_local_scores = (local_probs * (grad_local_probs - delta[:, :, None])).astype(BF16)
    grad_query_heads = (
        jnp.einsum("hij,jhd->ihd", grad_local_scores, key_heads, preferred_element_type=F32)
        * factor
    )
    grad_key_heads = (
        jnp.einsum("hij,ihd->jhd", grad_local_scores, query_heads, preferred_element_type=F32)
        * factor
    )
    grad_queries = grad_query_heads.reshape(seg_rows, model_width) + grad_query_memory.astype(F32)
    grad_joined = jnp.concatenate(
        [
            grad_queries,
            grad_key_heads.reshape(seg_rows, model_width),
            grad_value_heads.reshape(seg_rows, model_width),
        ],
        axis=1,
    ).astype(BF16)
    grad_normed_one = jnp.dot(grad_joined, joined_w.T, preferred_element_type=F32)
    grad_gain_one, grad_input_norm = norm_back(grad_normed_one, normed_one, inverse_one, gain_one)
    input_grad = (grad_first + grad_input_norm).astype(BF16)

    small = jnp.stack([grad_gain_one.reshape(devices, own), grad_gain_two.reshape(devices, own)], axis=1)
    small = jnp.pad(small, ((0, 0), (0, 6), (0, 128 - own)))
    attn_sums, out_sums, ffn_sums, down_sums, small_sums = reduce_plain(
        normed_low, grad_joined, attended_low, grad_branch, normed_two_low, grad_gate_up, hidden, out_grad, small
    )
    return (
        output,
        input_grad,
        small_sums[0, :own],
        attn_sums[:, :model_width],
        attn_sums[:, model_width : 2 * model_width],
        attn_sums[:, 2 * model_width : 3 * model_width],
        out_sums,
        small_sums[1, :own],
        ffn_sums[:, :ff_width],
        ffn_sums[:, ff_width:],
        down_sums,
    )


def solution(mesh):
    rows = P(("dp", "mem"), None)
    vector = P(("dp", "mem"))
    in_specs = (
        (rows, vector) + (rows,) * 4 + (vector,) + (rows,) * 6
        + (P("dp", "mem"), P("dp", None), P("dp", None), P("dp", "mem"))
    )
    out_specs = (rows, rows, vector) + (rows,) * 4 + (vector,) + (rows,) * 3
    return jax.shard_map(shards, mesh=mesh, in_specs=in_specs, out_specs=out_specs, check_vma=False)
```

```python
import functools
import math

import jax
import jax.numpy as jnp
from jax import lax
from jax.experimental import pallas as pl
from jax.experimental.pallas import tpu as pltpu
from jax.sharding import PartitionSpec as P

HEADS = 8
WIDTH = 128
KEYS = 128
epsilon = 1e-05
neg_big = -1e30
LOG2E = 1.4426950408889634
VMEM_MAX = 67043328
MESH = pl.DeviceIdType.MESH
F32 = jnp.float32
BF16 = jnp.bfloat16

ANY = pl.BlockSpec(memory_space=pl.ANY)
VM = pl.BlockSpec(memory_space=pltpu.VMEM)
SM = pl.BlockSpec(memory_space=pltpu.SMEM)


def place():
    m = lax.axis_index("mem")
    return lax.axis_index("dp"), m // 4, (m // 2) % 2, m % 2


def device(y, z, x, c):
    return {"dp": y, "mem": z * 4 + x * 2 + c}


def flip_z(z, d):
    return (z, z + 1 - 2 * (z % 2), (z + 2) % 4, 3 - z)[d]


def greet(targets):
    barrier = pltpu.get_barrier_semaphore()
    for target in targets:
        pl.semaphore_signal(barrier, inc=1, device_id=target, device_id_type=MESH)
    pl.semaphore_wait(barrier, len(targets))


def remote(src, dst, send, recv, target):
    return pltpu.make_async_remote_copy(
        src_ref=src, dst_ref=dst, send_sem=send, recv_sem=recv, device_id=target, device_id_type=MESH
    )


EARLY, LATE = (0, 4, 1), (3, 2, 5)
CROSS = (0, 1, 4)


def line_of(z):
    inner = ((z + 1) // 2) % 2
    near = flip_z(z, 1)
    second = 3 - (inner * z + (1 - inner) * near)
    third = 3 - (inner * near + (1 - inner) * z)
    return inner, (z, near, second, third)


def expand(packed, first, count):
    rows, lanes = packed.shape
    width = rows // 16 * count
    lane = lax.broadcasted_iota(jnp.int32, (lanes, width), 0)
    column = lax.broadcasted_iota(jnp.int32, (lanes, width), 1)
    pick = (lane == first + column % count).astype(BF16)
    wide = jnp.dot(packed, pick, preferred_element_type=F32)
    shard = lax.broadcasted_iota(jnp.int32, (rows, width), 0) // 16
    column = lax.broadcasted_iota(jnp.int32, (rows, width), 1) // count
    return jnp.sum(jnp.where(shard == column, wide, 0.0), axis=0, keepdims=True)


def rows_of(ref, block, count):
    return jnp.concatenate([ref[block + i] for i in range(count)], axis=0)


def window_bias(ref, block, count, start, stop):
    size = ref.shape[2]
    parts = []
    for i in range(count):
        spots = (block + i) * size + lax.broadcasted_iota(jnp.int32, (8, size), 1)
        inside = (spots >= start) & (spots < stop)
        parts.append(jnp.where(inside, ref[block + i], neg_big))
    return jnp.concatenate(parts, axis=1)[0:1]


def key_window(j, ranks, rank, docs, sizes, blocks):
    window = blocks // 2 + 1
    doc = docs[0, j * ranks + rank]
    start = 0
    stop = 0
    for i in range(sizes.shape[1]):
        size = sizes[0, i]
        start = start + size * (i < doc).astype(jnp.int32)
        stop = stop + size * (i <= doc).astype(jnp.int32)
    base = lax.min(lax.div(start, jnp.int32(KEYS)), jnp.int32(blocks - window))
    return start, stop, base, window


def columns(block):
    rows = block.shape[1]
    return jnp.concatenate([block, jnp.zeros((rows - 8, rows), F32)], axis=0).T


def front_kernel(own_rows, *refs):
    docs, sizes, lens = refs[:3]
    x_ref, og = refs[3:5]
    src = refs[5:10]
    keys, vals, bias = refs[10:13]
    first_out, o_low, att, tot, h_ref, q_ref, k_ref, v_ref, qh, gain_out, h2c, ogc = refs[13:25]
    dst = refs[25:30]
    kh, vh, bh = refs[30:33]
    oh, lh, mo, ml, loc, st, relay_k, relay_v = refs[33:41]
    own_sem, rs, sends, ko, kr, rr, kcs, qs, qr, os_, or_, pair = refs[41:]
    y, z, x, c = place()
    m = z * 4 + x * 2 + c
    ranks = 2
    chip = z * 2 + x
    rows = x_ref.shape[0]
    width = x_ref.shape[1]
    total = kh.shape[0]
    per = keys.shape[0]
    factor = WIDTH ** (-0.5) * LOG2E
    inner, line = line_of(z)
    y_peer, x_peer, c_peer = device(1 - y, z, x, c), device(y, z, 1 - x, c), device(y, z, x, 1 - c)
    near, across = device(y, flip_z(z, 1), x, c), device(y, 3 - z, x, c)
    plane = [
        (flip_z(z, dz), x if dx == 0 else 1 - x) for dz in (3, 2, 1, 0) for dx in (1, 0) if dz or dx
    ]
    pending = []
    inner_pending = []
    used = [0]

    def next_sem():
        used[0] += 1
        return sends.at[used[0] - 1]

    def go(copy):
        copy.start()
        pending.append(copy)

    def spot(p, zz, xx, cc, far=False):
        n = zz * 4 + xx * 2 + cc
        if p == 3:
            return dst[3].at[n], rs.at[n, 3]
        n = n + 16 * (1 - y if far or p == 5 else y)
        p = 2 if p == 5 else p
        return dst[p].at[n], rs.at[n, p]

    def push(place, target, source=None):
        view, sem = place
        go(remote(view if source is None else source, view, next_sem(), sem, target))

    def push_inner(jobs, target):
        copies = [
            remote(view if source is None else source, view, next_sem(), sem, target)
            for (view, sem), source in jobs
        ]
        inner_pending.extend(copies)

        @pl.when(inner == 1)
        def _():
            for copy in copies:
                copy.start()

    def arrived(place):
        view, sem = place
        remote(view, view, own_sem.at[0], sem, c_peer).wait_recv()

    def own_sends(group):
        jobs = []
        for p in group:
            source = None if p == 5 else src[2].at[y] if p == 2 else src[p]
            jobs.append((spot(p, z, x, c), source, p))
        push_inner([job[:2] for job in jobs], across)
        for view, source, p in jobs:
            push(view, near, source)
        for view, source, p in jobs:
            if p in CROSS:
                push(view, y_peer, source)
            push(view, x_peer, source)
            push(view, c_peer, source)

    def mirror():
        arrived(spot(5, z, x, c))
        own_sends((5,))

    def line_event(i, group):
        views = [(spot(p, line[i], x, c), p) for p in group]
        for view, p in views:
            arrived(view)
        push_inner([(view, None) for view, p in views], across if i == 1 else near)
        for view, p in views:
            if p in CROSS:
                push(view, y_peer)
            push(view, x_peer)
            push(view, c_peer)

    def x_event(i, group):
        for p in group:
            view = spot(p, line[i], 1 - x, c)
            arrived(view)
            if p in CROSS:
                push(view, y_peer)
            push(view, c_peer)

    def y_event(i, group):
        for p in group:
            view = spot(p, line[i], x, c, True)
            arrived(view)
            push(view, c_peer)

    def corner_event(i, group):
        for p in group:
            view = spot(p, line[i], 1 - x, c, True)
            arrived(view)
            push(view, c_peer)

    def core_events(group):
        for p in group:
            for far in (False, True) if p in CROSS else (False,):
                for zz in line:
                    for xx in (x, 1 - x):
                        arrived(spot(p, zz, xx, 1 - c, far))

    def block(ref, i):
        return ref.at[pl.ds(i * per, per)]

    def lanes(ref, i):
        at = pl.ds(pl.multiple_of(i * WIDTH, WIDTH), WIDTH)
        return ref.at[:, at] if len(ref.shape) == 2 else ref.at[:, :, at]

    beside = z * 4 + (1 - x) * 2 + c
    memory_x = [remote(bias, block(bh, m), next_sem(), kr.at[m, 2], x_peer)]
    memory_z = []
    for d in (3, 2, 1, 0):
        zz = flip_z(z, d)
        for p, (a, b, r) in enumerate(((keys, kh, relay_k), (vals, vh, relay_v))):
            view, sem = (r.at[d - 1], rr.at[d - 1, p]) if d else (block(b, m), kr.at[m, p])
            memory_x.append(remote(lanes(a, zz * 2 + 1 - x), view, next_sem(), sem, x_peer))
            if d:
                memory_z.append(
                    remote(lanes(a, zz * 2 + x), block(b, m), next_sem(), kr.at[m, p], device(y, zz, x, c))
                )
        if d:
            memory_z.append(remote(bias, block(bh, m), next_sem(), kr.at[m, 2], device(y, zz, x, c)))

    def relay():
        view = block(bh, beside)
        remote(view, view, ko.at[0], kr.at[beside, 2], x_peer).wait_recv()
        for d in (3, 2, 1):
            target = device(y, flip_z(z, d), x, c)
            for p, (b, r) in enumerate(((kh, relay_k), (vh, relay_v))):
                room = r.at[d - 1]
                remote(room, room, ko.at[0], rr.at[d - 1, p], x_peer).wait_recv()
                go(remote(room, block(b, beside), next_sem(), kr.at[beside, p], target))
            go(remote(view, view, next_sem(), kr.at[beside, 2], target))

    greet([device(y, a, b, c) for a, b in plane] + [y_peer, c_peer])
    own_sends(EARLY)
    push(spot(2, z, x, c), y_peer, src[2].at[1 - y])
    go(remote(og, ogc.at[1], pair.at[0], pair.at[1], y_peer))
    homes = [
        pltpu.make_async_copy(src[2].at[y] if p == 2 else src[p], spot(p, z, x, c)[0], own_sem.at[p])
        for p in range(5)
    ]
    for p, (a, b) in enumerate(((lanes(keys, chip), kh), (lanes(vals, chip), vh), (bias, bh))):
        homes.append(pltpu.make_async_copy(a, block(b, m), ko.at[p]))
    homes.append(pltpu.make_async_copy(og, ogc.at[0], own_sem.at[5]))
    for copy in homes:
        copy.start()

    for copy in memory_x:
        go(copy)

    @pl.when(inner == 0)
    def _():
        for copy in memory_z:
            copy.start()

    inputs = x_ref[...].astype(F32)
    normed = inputs * lax.rsqrt(jnp.mean(inputs * inputs, axis=-1, keepdims=True) + epsilon)

    line_event(1, EARLY)
    y_event(0, EARLY)
    line_event(2, EARLY)
    line_event(3, EARLY)

    @pl.when(inner == 1)
    def _():
        for copy in memory_z:
            copy.start()

    x_event(0, EARLY)
    relay()
    for p, (a, b) in enumerate(((lanes(keys, chip), kh), (lanes(vals, chip), vh), (bias, bh))):
        go(remote(a, block(b, m), kcs.at[7, p], kr.at[m, p], c_peer))
    own_sends((3, 2))
    mirror()
    for i in (1, 2, 3):
        y_event(i, EARLY)
    for i in (1, 2, 3):
        x_event(i, EARLY)
    for i in range(4):
        corner_event(i, EARLY)
    core_events(EARLY)
    for copy in homes:
        copy.wait()

    packed = dst[4][...].reshape(32 * 16, 128)
    gain = expand(packed, 0, own_rows)
    gain_out[...] = jnp.concatenate(
        [gain, expand(packed, own_rows, own_rows), jnp.zeros((6, width), F32)], axis=0
    )
    low = (normed * gain).astype(BF16)
    h_ref[...] = low
    for i, ref in enumerate((q_ref, k_ref, v_ref)):
        weight = dst[0][:, :, i * width : (i + 1) * width].reshape(width, width)
        ref[...] = jnp.dot(low, weight, preferred_element_type=F32).astype(BF16)

    others = [(chip + d) % 8 for d in range(1, 8)]
    peers = [{"dp": y, "mem": o * ranks + c} for o in others]
    for d, (o, peer) in enumerate(zip(others, peers)):
        go(remote(lanes(q_ref, o), qh.at[chip], qs.at[d], qr.at[chip], peer))
    mine = pltpu.make_async_copy(lanes(q_ref, chip), qh.at[chip], ko.at[0])
    mine.start()

    below = lax.broadcasted_iota(jnp.int32, (rows, rows), 1)
    ok = (below <= lax.broadcasted_iota(jnp.int32, (rows, rows), 0)) & (below < lens[0, 0])
    lane = lax.broadcasted_iota(jnp.int32, (rows, 128), 1)
    tops = jnp.zeros((rows, 128), F32)
    sums = jnp.zeros((rows, 128), F32)
    for i in range(HEADS):
        at = slice(i * WIDTH, (i + 1) * WIDTH)
        s = lax.dot_general(
            q_ref[:, at], k_ref[:, at], (((1,), (1,)), ((), ())), preferred_element_type=F32
        )
        s = jnp.where(ok, s * factor, neg_big)
        top = jnp.max(s, axis=1, keepdims=True)
        p = jnp.exp2(s - top)
        tops = jnp.where(lane == i, top, tops)
        sums = jnp.where(lane == i, jnp.sum(p, axis=1, keepdims=True), sums)
        loc[:, at] = jnp.dot(p.astype(BF16), v_ref[:, at], preferred_element_type=F32)
    st[0] = tops
    st[1] = sums
    for p in LATE:
        line_event(1, (p,))
    x_event(0, LATE)

    for i, (zz, xx) in reversed(list(enumerate(plane))):
        other = zz * 4 + xx * 2 + c
        for p, b in enumerate((kh, vh, bh)):
            view = block(b, other)
            if p < 2 or i < 6:
                remote(view, view, ko.at[p], kr.at[other, p], c_peer).wait_recv()
            go(remote(view, view, kcs.at[i, p], kr.at[other, p], c_peer))
    for zz, xx in [(z, x)] + plane[::-1]:
        other = zz * 4 + xx * 2 + 1 - c
        for p, b in enumerate((kh, vh, bh)):
            remote(block(b, other), block(b, other), ko.at[p], kr.at[other, p], c_peer).wait_recv()
    mine.wait()
    for o in others:
        remote(qh.at[o], qh.at[o], ko.at[0], qr.at[o], c_peer).wait_recv()

    def attend(d, _):
        j = (chip + d) % 8
        start, stop, base, window = key_window(j, ranks, c, docs, sizes, total)
        q = qh[j]
        parts = 3
        chunk = window // parts

        def step(t, carry):
            top, tsum, acc = carry
            at = base + t * chunk
            s = lax.dot_general(
                q, rows_of(kh, at, chunk), (((1,), (1,)), ((), ())), preferred_element_type=F32
            )
            s = s * factor + window_bias(bh, at, chunk, start, stop)
            best = jnp.maximum(top, jnp.max(s, axis=1, keepdims=True))
            p = jnp.exp2(s - best)
            keep = jnp.exp2(top - best)
            tsum = tsum * keep + jnp.sum(p, axis=1, keepdims=True)
            acc = acc * keep + jnp.dot(p.astype(BF16), rows_of(vh, at, chunk), preferred_element_type=F32)
            return best, tsum, acc

        top, tsum, acc = lax.fori_loop(
            0,
            parts,
            step,
            (jnp.full((rows, 1), neg_big, F32), jnp.zeros((rows, 1), F32), jnp.zeros((rows, WIDTH), F32)),
        )
        oh[j] = (acc / tsum).astype(BF16)
        lh[j] = jnp.broadcast_to(top + jnp.log2(tsum), (rows, rows)).T[0:8]
        return 0

    def answer(d):
        j = (chip + d) % 8
        peer = {"dp": y, "mem": j * ranks + c}
        go(remote(oh.at[j], lanes(mo, chip), os_.at[d, 0], or_.at[chip, 0], peer))
        go(remote(lh.at[j], ml.at[chip], os_.at[d, 1], or_.at[chip, 1], peer))

    line_event(2, LATE[:1])
    for i, d in enumerate((1, 3, 5)):
        lax.fori_loop(d, d + 2, attend, 0)
        answer(d)
        answer(d + 1)
        if i < 2:
            line_event(2, LATE[i + 1 : i + 2])
        x_event(1, LATE[i : i + 1])
    lax.fori_loop(7, 9, attend, 0)
    answer(7)
    backs = [
        pltpu.make_async_copy(oh.at[chip], lanes(mo, chip), ko.at[0]),
        pltpu.make_async_copy(lh.at[chip], ml.at[chip], ko.at[1]),
    ]
    for copy in backs:
        copy.start()
    for p in LATE:
        line_event(3, (p,))
        x_event(2, (p,))
    for o in others:
        remote(lanes(mo, o), lanes(mo, o), ko.at[0], or_.at[o, 0], c_peer).wait_recv()
        remote(ml.at[o], ml.at[o], ko.at[1], or_.at[o, 1], c_peer).wait_recv()
    for copy in backs:
        copy.wait()

    head_row = lax.broadcasted_iota(jnp.int32, (8, rows), 0)
    gathered = jnp.zeros((8, rows), F32)
    for i in range(HEADS):
        gathered = jnp.where(head_row == i, ml[i], gathered)
    mem_lse = columns(gathered)
    tops, sums = st[0], st[1]
    known = lane < HEADS
    loc_lse = jnp.where(known, tops + jnp.log2(jnp.where(known, sums, 1.0)), 0.0)
    best = jnp.maximum(loc_lse, mem_lse)
    whole = best + jnp.log2(jnp.exp2(loc_lse - best) + jnp.exp2(mem_lse - best))
    tot[...] = whole
    loc_scale = jnp.exp2(tops - whole)
    mem_scale = jnp.exp2(mem_lse - whole)
    for i in range(HEADS):
        at = slice(i * WIDTH, (i + 1) * WIDTH)
        value = loc[:, at] * loc_scale[:, i : i + 1] + mo[:, at].astype(F32) * mem_scale[:, i : i + 1]
        att[:, at] = value
        o_low[:, at] = value.astype(BF16)
    weight = dst[1][...].reshape(width, width)
    first = x_ref[...].astype(F32) + jnp.dot(o_low[...], weight, preferred_element_type=F32)
    first_out[...] = first
    normed_two = first * lax.rsqrt(jnp.mean(first * first, axis=-1, keepdims=True) + epsilon)
    h2c[0] = (normed_two * gain_out[1:2]).astype(BF16)
    go(remote(h2c.at[0], h2c.at[1], pair.at[2], pair.at[3], y_peer))
    x_event(3, LATE)
    core_events(LATE)
    remote(ogc.at[1], ogc.at[1], pair.at[0], pair.at[1], y_peer).wait_recv()
    remote(h2c.at[1], h2c.at[1], pair.at[2], pair.at[3], y_peer).wait_recv()
    for copy in memory_z:
        copy.wait_send()
    for copy in pending:
        copy.wait_send()

    @pl.when(inner == 1)
    def _():
        for copy in inner_pending:
            copy.wait_send()


def front(docs, sizes, lens, tokens, out_grad, pieces, keys, values, bias, own_rows):
    dma = pltpu.SemaphoreType.DMA
    rows, width = tokens.shape
    total = keys.shape[0] * 16
    shape = jax.ShapeDtypeStruct
    wide = shape((rows, width), BF16)
    outs = [
        shape((rows, width), F32),
        wide,
        shape((rows, width), F32),
        shape((rows, 128), F32),
        wide,
        wide,
        wide,
        wide,
        shape((8, rows, WIDTH), BF16),
        shape((8, width), F32),
        shape((2, rows, width), BF16),
        shape((2, rows, width), BF16),
    ]
    counts = (32, 32, 32, 16, 32)
    outs += [shape((n,) + a.shape[-2:], a.dtype) for n, a in zip(counts, pieces)]
    outs += [shape((total, KEYS, WIDTH), BF16)] * 2 + [shape((total, 8, KEYS), F32)]
    spaces = [VM] * 12 + [VM, VM, ANY, ANY, VM] + [VM] * 3
    return pl.pallas_call(
        functools.partial(front_kernel, own_rows),
        out_shape=outs,
        in_specs=[SM] * 3 + [VM] * 10,
        out_specs=spaces,
        scratch_shapes=[
            pltpu.VMEM((8, rows, WIDTH), BF16),
            pltpu.VMEM((8, 8, rows), F32),
            pltpu.VMEM((rows, width), BF16),
            pltpu.VMEM((8, 8, rows), F32),
            pltpu.VMEM((rows, width), F32),
            pltpu.VMEM((2, rows, 128), F32),
            pltpu.VMEM((3,) + keys.shape[:2] + (WIDTH,), BF16),
            pltpu.VMEM((3,) + keys.shape[:2] + (WIDTH,), BF16),
            dma((6,)),
            dma((32, 5)),
            dma((224,)),
            dma((3,)),
            dma((16, 3)),
            dma((3, 2)),
            dma((8, 3)),
            dma((7,)),
            dma((8,)),
            dma((8, 2)),
            dma((8, 2)),
            dma((4,)),
        ],
        compiler_params=pltpu.CompilerParams(
            collective_id=0, has_side_effects=True, vmem_limit_bytes=48 << 20
        ),
        name="front",
    )(docs, sizes, lens, tokens, out_grad, *pieces, keys, values, bias)


def key_span(j, ranks, docs, sizes, rank_ref):
    doc = docs[0, j * ranks + rank_ref[0]]
    start = jnp.int32(0)
    stop = jnp.int32(0)
    for i in range(sizes.shape[1]):
        size = sizes[0, i]
        start = start + jnp.where(i < doc, size, 0)
        stop = stop + jnp.where(i <= doc, size, 0)
    return start, stop


def forward_kernel(ranks, block, docs, sizes, rank_ref, q_ref, k_ref, v_ref, bias_ref, o_ref, lse_ref):
    j = pl.program_id(0)
    start, stop = key_span(j, ranks, docs, sizes, rank_ref)
    q = q_ref[0]
    factor = WIDTH ** (-0.5) * LOG2E

    def step(b, carry):
        top, total, acc = carry
        s = lax.dot_general(
            q, rows_of(k_ref, b * block, block), (((1,), (1,)), ((), ())), preferred_element_type=F32
        )
        s = s * factor + window_bias(bias_ref, b * block, block, start, stop)
        best = jnp.maximum(top, jnp.max(s, axis=1, keepdims=True))
        p = jnp.exp2(s - best)
        keep = jnp.exp2(top - best)
        total = total * keep + jnp.sum(p, axis=1, keepdims=True)
        acc = acc * keep + jnp.dot(
            p.astype(BF16), rows_of(v_ref, b * block, block), preferred_element_type=F32
        )
        return best, total, acc

    rows = q.shape[0]
    top, total, acc = lax.fori_loop(
        start // (block * KEYS),
        (stop + block * KEYS - 1) // (block * KEYS),
        step,
        (jnp.full((rows, 1), neg_big, F32), jnp.zeros((rows, 1), F32), jnp.zeros((rows, WIDTH), F32)),
    )
    o_ref[0] = (acc / total).astype(BF16)
    lse = jnp.broadcast_to(top + jnp.log2(total), (rows, rows))
    lse_ref[0] = lse.T[0:8]


def backward_kernel(
    ranks, block, docs, sizes, rank_ref, q_ref, do_ref, stat_ref, k_ref, v_ref, bias_ref, dq_ref
):
    j = pl.program_id(0)
    start, stop = key_span(j, ranks, docs, sizes, rank_ref)
    q, do = q_ref[0], do_ref[0]
    rows = q.shape[0]
    factor = WIDTH ** (-0.5) * LOG2E
    stat = stat_ref[0]
    lse = jnp.broadcast_to(stat[0:1], (rows, rows)).T[:, 0:1]
    delta = jnp.broadcast_to(stat[1:2], (rows, rows)).T[:, 0:1]

    def step(b, acc):
        keys = rows_of(k_ref, b * block, block)
        s = lax.dot_general(q, keys, (((1,), (1,)), ((), ())), preferred_element_type=F32)
        p = jnp.exp2(s * factor + (window_bias(bias_ref, b * block, block, start, stop) - lse))
        dp = lax.dot_general(do, rows_of(v_ref, b * block, block), (((1,), (1,)), ((), ())), preferred_element_type=F32)
        ds = (p * (dp - delta)).astype(BF16)
        return acc + jnp.dot(ds, keys, preferred_element_type=F32)

    acc = lax.fori_loop(
        start // (block * KEYS), (stop + block * KEYS - 1) // (block * KEYS), step, jnp.zeros((rows, WIDTH), F32)
    )
    dq_ref[0] = (acc * WIDTH ** (-0.5)).astype(BF16)


def memory_forward(ranks, docs, sizes, rank, q, kh, vh, bh):
    count, rows, _ = q.shape
    seg = pl.BlockSpec((1, rows, WIDTH), lambda j: (j, 0, 0))
    stat = pl.BlockSpec((1, 8, rows), lambda j: (j, 0, 0))
    block = 8
    return pl.pallas_call(
        functools.partial(forward_kernel, ranks, block),
        grid=(count,),
        out_shape=[
            jax.ShapeDtypeStruct((count, rows, WIDTH), BF16),
            jax.ShapeDtypeStruct((count, 8, rows), F32),
        ],
        in_specs=[SM, SM, SM, seg, VM, VM, VM],
        out_specs=[seg, stat],
        compiler_params=pltpu.CompilerParams(vmem_limit_bytes=48 << 20),
        name="memory_forward",
    )(docs, sizes, rank, q, kh, vh, bh)


def memory_backward(ranks, docs, sizes, rank, q, do, stats, kh, vh, bh):
    count, rows, _ = q.shape
    seg = pl.BlockSpec((1, rows, WIDTH), lambda j: (j, 0, 0))
    stat = pl.BlockSpec((1, 8, rows), lambda j: (j, 0, 0))
    block = 8
    return pl.pallas_call(
        functools.partial(backward_kernel, ranks, block),
        grid=(count,),
        out_shape=jax.ShapeDtypeStruct((count, rows, WIDTH), BF16),
        in_specs=[SM, SM, SM, seg, seg, stat, VM, VM, VM],
        out_specs=seg,
        compiler_params=pltpu.CompilerParams(vmem_limit_bytes=48 << 20),
        name="memory_backward",
    )(docs, sizes, rank, q, do, stats, kh, vh, bh)


DEPTH = 3


def contract(row, first, lanes):
    width = row.shape[1]
    count = width // 32
    shard = lax.broadcasted_iota(jnp.int32, (32, width), 0)
    column = lax.broadcasted_iota(jnp.int32, (32, width), 1)
    masked = jnp.where(column // count == shard, jnp.broadcast_to(row, (32, width)), 0.0)
    feature = lax.broadcasted_iota(jnp.int32, (width, lanes), 0)
    lane = lax.broadcasted_iota(jnp.int32, (width, lanes), 1)
    pick = (lane == first + feature % count).astype(F32)
    return jnp.dot(masked, pick, preferred_element_type=F32, precision=lax.Precision.HIGHEST)


def tiles_of(width):
    for count in (4, 3, 2, 1):
        if width % (count * 128) == 0 and width // count >= 512:
            return count, width // count
    return 1, width


def back_kernel(*refs):
    docs, sizes, lens = refs[:3]
    x_ref, gains, first, tot, att, dh_own, dh_far, out_own, out_far = refs[3:12]
    h, o, h2, dgu, hid, og = refs[12:18]
    q_ref, k_ref, v_ref, qh, kh, vh, bh = refs[18:25]
    w_in, w_out = refs[25:27]
    output, input_grad, g_q, g_k, g_v, g_o, g_gate, g_up, g_down, g_small = refs[27:37]
    stage, cores, firsts, seconds, lines = (refs[37 + 6 * i : 43 + 6 * i] for i in range(5))
    ht, ot, h2t, hidt, dqs, dkv, dql, das, dys, do, small, sst, doh, sth, dqo, dqm, wbuf = refs[67:84]
    dh_in, out_in, far_out, far_in = refs[84:88]
    cs, cr, fs, fr, ss, sr, zs, zr, own, dsend, drecv, qsend, qrecv, wsem, psend, precv = refs[88:]
    y, z, x, c = place()
    ranks = 2
    chip = z * 2 + x
    rows, width = x_ref.shape
    half = hid.shape[1]
    factor = WIDTH ** (-0.5) * LOG2E
    y_peer, x_peer, c_peer = device(1 - y, z, x, c), device(y, z, 1 - x, c), device(y, z, x, 1 - c)
    others = [(chip + d) % 8 for d in range(1, 8)]
    peers = [{"dp": y, "mem": p * ranks + c} for p in others]
    pending = []

    def go(copy):
        copy.start()
        pending.append(copy)

    def wait(dst, sem):
        remote(dst, dst, own.at[0], sem, c_peer).wait_recv()

    def lanes(ref, i):
        return ref.at[:, pl.ds(pl.multiple_of(i * WIDTH, WIDTH), WIDTH)]

    def load(source, i):
        copy = pltpu.make_async_copy(source, wbuf.at[i], wsem.at[i])
        copy.start()
        return copy

    def weight_part(i):
        return w_in.at[:, :, i * width : (i + 1) * width]

    greet(peers + [y_peer, c_peer])

    left = (ht, ht, ot, h2t, hidt)
    right = (dqs, dkv, das, dgu, og)
    order = [(k, d) for d in (3, 2, 1, 0) for k in (1, 0)]
    split = (3, 4)

    def used(i, group):
        return [p for p in group if p != 4 or order[i][0] == 0]

    def held(i, p):
        return i // 2 if p == 4 else i

    def produce(i, group):
        k, d = order[i]
        zz = flip_z(z, d)
        for p in used(i, group):
            u = zz if p == 4 else (1 - y if k else y) * 4 + zz
            room = stage[p].at[i % DEPTH]
            if p == 5:
                for n in range(4):
                    room[n] = small[u * 4 + n]
            else:
                size = 4 * stage[p].shape[2]
                block = left[p][pl.ds(pl.multiple_of(u * size, 32), size), :]
                count, tile = tiles_of(stage[p].shape[3])

                def some(t, _):
                    at = pl.ds(pl.multiple_of(t * tile, 128), tile)
                    part = jnp.dot(block, right[p][:, at], preferred_element_type=F32)
                    room[:, :, at] = part.astype(BF16).reshape(4, size // 4, tile)
                    return 0

                lax.fori_loop(0, count, some, 0)
            for xx in range(2):
                core_copy(i, p, xx).start()

    def core_copy(i, p, xx):
        return remote(
            stage[p].at[i % DEPTH, xx * 2 + 1 - c], cores[p].at[held(i, p), xx], cs.at[i, xx, p], cr.at[i, xx, p], c_peer
        )

    def merge(into, other):
        count, tile = tiles_of(into.shape[1])

        def some(t, _):
            at = pl.ds(pl.multiple_of(t * tile, 128), tile)
            into[:, at] = (into[:, at].astype(F32) + other[:, at].astype(F32)).astype(into.dtype)
            return 0

        lax.fori_loop(0, count, some, 0)

    def after_core(i, group):
        k, d = order[i]
        for p in used(i, group):
            for xx in (1 - x, x):
                into = cores[p].at[held(i, p), xx]
                wait(into, cr.at[i, xx, p])
                merge(into, stage[p].at[i % DEPTH, xx * 2 + c])
            if p in split:
                n = held(i, p)
                go(remote(cores[p].at[n, 1 - x], firsts[p].at[n], fs.at[i, 0, p], fr.at[i, 0, p], x_peer))
            elif k == 1:
                t = i // 2
                for xx in range(2):
                    go(remote(cores[p].at[i, xx], firsts[p].at[t + 4 * xx], fs.at[i, xx, p], fr.at[t, xx, p], y_peer))
            for xx in range(2):
                core_copy(i, p, xx).wait_send()

    def to_line(i, p):
        k, d = order[i]
        if d:
            n = d - 1 + 3 * k
            go(remote(cores[p].at[held(i, p), x], lines[p].at[n], zs.at[n, p], zr.at[n, p], device(y, flip_z(z, d), x, c)))

    def after_first(i, group):
        k, d = order[i]
        t = i // 2
        for p in used(i, group):
            if p in split:
                n = held(i, p)
                wait(firsts[p].at[n], fr.at[i, 0, p])
                merge(cores[p].at[n, x], firsts[p].at[n])
                to_line(i, p)
            elif k == 0:
                for xx in (1 - x, x):
                    room = firsts[p].at[t + 4 * xx]
                    wait(room, fr.at[t, xx, p])
                    merge(cores[p].at[i, xx], room)
                go(remote(cores[p].at[i, 1 - x], seconds[p].at[t], ss.at[t, p], sr.at[t, p], x_peer))

    def after_second(i, group):
        t = i // 2
        for p in group:
            wait(seconds[p].at[t], sr.at[t, p])
            merge(cores[p].at[i, x], seconds[p].at[t])
            to_line(i, p)

    def along(p, k, at):
        total = cores[p][held(7 - k, p), x, :, at].astype(F32)
        for d in range(3):
            total = total + lines[p][d + 3 * k, :, at].astype(F32)
        return total

    def line_wait(p, k):
        for d in range(3):
            wait(lines[p].at[d + 3 * k], zr.at[d + 3 * k, p])

    def finish(group):
        for p in group:
            line_wait(p, 0)
            outs = ((g_q,), (g_k, g_v), (g_o,), (), (g_down,), (g_small,))[p]
            for i, out in enumerate(outs):
                span = cores[p].shape[3] // len(outs)
                out[...] = along(p, 0, slice(i * span, (i + 1) * span))

    def attend(d, _):
        j = (chip + d) % 8
        start, stop, base, window = key_window(j, ranks, c, docs, sizes, kh.shape[0])
        q, dout, stat = qh[j], doh[j], sth[j]
        lse = jnp.broadcast_to(stat[0:1], (rows, rows)).T[:, 0:1]
        delta = jnp.broadcast_to(stat[1:2], (rows, rows)).T[:, 0:1]
        parts = 3
        chunk = window // parts

        def step(t, acc):
            at = base + t * chunk
            keys = rows_of(kh, at, chunk)
            s = lax.dot_general(q, keys, (((1,), (1,)), ((), ())), preferred_element_type=F32)
            p = jnp.exp2(s * factor + (window_bias(bh, at, chunk, start, stop) - lse))
            dp = lax.dot_general(
                dout, rows_of(vh, at, chunk), (((1,), (1,)), ((), ())), preferred_element_type=F32
            )
            ds = (p * (dp - delta)).astype(BF16)
            return acc + jnp.dot(ds, keys, preferred_element_type=F32)

        acc = lax.fori_loop(0, parts, step, jnp.zeros((rows, WIDTH), F32))
        dqo[j] = (acc * WIDTH ** (-0.5)).astype(BF16)
        return 0

    def answer(d):
        j = (chip + d) % 8
        go(remote(dqo.at[j], lanes(dqm, chip), qsend.at[d - 1], qrecv.at[chip], {"dp": y, "mem": j * ranks + c}))

    ffn, query, others_att, gain = (3, 4), (0,), (1, 2), (5,)
    go(remote(dh_far, dh_in, psend.at[0], precv.at[0], y_peer))
    go(remote(out_far, out_in, psend.at[1], precv.at[1], y_peer))
    load_out = load(w_out, 0)
    load_key = load(weight_part(1), 1)
    h2t[...] = h2[...].T
    produce(0, ffn)
    hidt[...] = hid[...].T
    produce(1, ffn)
    after_core(0, ffn)
    produce(2, ffn)
    after_core(1, ffn)

    wait(dh_in, precv.at[0])
    residual = first[...]
    inverse_two = lax.rsqrt(jnp.mean(residual * residual, axis=-1, keepdims=True) + epsilon)
    normed_two = residual * inverse_two
    dh2 = dh_own[...] + dh_in[...].astype(F32)
    pulled = contract(jnp.sum(dh2 * normed_two, axis=0, keepdims=True), width // 32, 128)
    small[...] = jnp.broadcast_to(pulled[:, None, :], small.shape)
    dn = dh2 * gains[1:2]
    dy = og[0:rows].astype(F32) + inverse_two * (
        dn - normed_two * jnp.mean(dn * normed_two, axis=-1, keepdims=True)
    )
    dys[...] = dy
    low = dy.astype(BF16)
    das[...] = low
    load_out.wait()
    do[...] = lax.dot_general(
        low, wbuf[0].reshape(width, width), (((1,), (1,)), ((), ())), preferred_element_type=F32
    ).astype(BF16)
    load_value = load(weight_part(2), 0)

    lane = lax.broadcasted_iota(jnp.int32, (rows, 128), 1)
    deltas = jnp.zeros((rows, 128), F32)
    for i in range(HEADS):
        at = slice(i * WIDTH, (i + 1) * WIDTH)
        part = jnp.sum(do[:, at].astype(F32) * att[:, at], axis=1, keepdims=True)
        deltas = jnp.where(lane == i, part, deltas)
    tot_rows, delta_rows = tot[...].T, deltas.T
    head_row = lax.broadcasted_iota(jnp.int32, (8, rows), 0)
    for i in range(HEADS):
        sst[i] = jnp.where(head_row == 0, tot_rows[i : i + 1], delta_rows[i : i + 1])
    for d, (p, peer) in enumerate(zip(others, peers)):
        go(remote(lanes(do, p), doh.at[chip], dsend.at[d, 0], drecv.at[chip, 0], peer))
        go(remote(sst.at[p], sth.at[chip], dsend.at[d, 1], drecv.at[chip, 1], peer))
    homes = [
        pltpu.make_async_copy(lanes(do, chip), doh.at[chip], own.at[1]),
        pltpu.make_async_copy(sst.at[chip], sth.at[chip], own.at[2]),
    ]
    for copy in homes:
        copy.start()
    ht[...] = h[...].T
    ot[...] = o[...].T
    produce(3, ffn)
    after_core(2, ffn)

    below = lax.broadcasted_iota(jnp.int32, (rows, rows), 1)
    ok = (below <= lax.broadcasted_iota(jnp.int32, (rows, rows), 0)) & (below < lens[0, 0])
    for i in range(HEADS):
        at = slice(i * WIDTH, (i + 1) * WIDTH)
        q, k, v, dout = q_ref[:, at], k_ref[:, at], v_ref[:, at], do[:, at]
        s = lax.dot_general(q, k, (((1,), (1,)), ((), ())), preferred_element_type=F32)
        p = jnp.where(ok, jnp.exp2(s * factor - tot[:, i : i + 1]), 0.0)
        dp = lax.dot_general(dout, v, (((1,), (1,)), ((), ())), preferred_element_type=F32)
        ds = (p * (dp - deltas[:, i : i + 1])).astype(BF16)
        dql[:, at] = jnp.dot(ds, k, preferred_element_type=F32) * WIDTH ** (-0.5)
        dk = lax.dot_general(ds, q, (((0,), (0,)), ((), ())), preferred_element_type=F32) * WIDTH ** (-0.5)
        dv = lax.dot_general(p.astype(BF16), dout, (((0,), (0,)), ((), ())), preferred_element_type=F32)
        dkv[:, at] = dk.astype(BF16)
        dkv[:, width + i * WIDTH : width + (i + 1) * WIDTH] = dv.astype(BF16)

    produce(0, others_att)
    produce(1, others_att)
    after_core(0, others_att)
    produce(2, others_att)
    after_core(1, others_att)
    after_core(2, others_att)
    for copy in homes:
        copy.wait()
    for p in others:
        wait(doh.at[p], drecv.at[p, 0])
        wait(sth.at[p], drecv.at[p, 1])
    lax.fori_loop(1, 3, attend, 0)
    answer(1)
    answer(2)
    after_first(0, ffn)
    after_core(3, ffn)
    produce(4, ffn)
    produce(3, others_att)
    produce(4, others_att)
    lax.fori_loop(3, 5, attend, 0)
    answer(3)
    answer(4)
    after_first(1, ffn)
    after_core(4, ffn)
    produce(5, ffn)
    after_core(3, others_att)
    after_core(4, others_att)
    after_first(1, others_att)
    lax.fori_loop(5, 7, attend, 0)
    answer(5)
    answer(6)
    after_first(2, ffn)
    after_core(5, ffn)
    produce(6, ffn)
    produce(5, others_att)
    produce(6, others_att)
    after_first(3, others_att)
    lax.fori_loop(7, 9, attend, 0)
    answer(7)
    back_copy = pltpu.make_async_copy(dqo.at[chip], lanes(dqm, chip), own.at[1])
    back_copy.start()
    after_first(3, ffn)
    after_core(6, ffn)
    produce(7, ffn)
    after_core(5, others_att)
    after_core(6, others_att)
    produce(7, others_att)
    after_second(1, others_att)
    after_core(7, ffn)
    wait(out_in, precv.at[1])
    output[...] = (residual + out_own[...] + out_in[...].astype(F32)).astype(BF16)
    load_key.wait()
    dh = lax.dot_general(
        dkv[:, :width], wbuf[1].reshape(width, width), (((1,), (1,)), ((), ())), preferred_element_type=F32
    )
    load_query = load(weight_part(0), 1)
    load_value.wait()
    dh = dh + lax.dot_general(
        dkv[:, width:], wbuf[0].reshape(width, width), (((1,), (1,)), ((), ())), preferred_element_type=F32
    )
    after_first(4, ffn)
    after_first(5, others_att)
    after_core(7, others_att)
    for p in others:
        wait(lanes(dqm, p), qrecv.at[p])
    back_copy.wait()
    dqs[...] = (dql[...] + dqm[...].astype(F32)).astype(BF16)
    produce(0, query)
    produce(1, query)
    after_core(0, query)
    produce(2, query)
    after_core(1, query)
    after_core(2, query)
    after_first(5, ffn)
    produce(3, query)
    produce(4, query)
    after_core(3, query)
    after_core(4, query)
    produce(5, query)
    produce(6, query)
    after_core(5, query)
    after_core(6, query)
    produce(7, query)
    after_core(7, query)
    after_second(3, others_att)
    after_first(7, others_att)

    load_query.wait()
    dh = dh + lax.dot_general(
        dqs[...], wbuf[1].reshape(width, width), (((1,), (1,)), ((), ())), preferred_element_type=F32
    )
    inputs = x_ref[...].astype(F32)
    inverse = lax.rsqrt(jnp.mean(inputs * inputs, axis=-1, keepdims=True) + epsilon)
    normed = inputs * inverse
    pulled = contract(jnp.sum(dh * normed, axis=0, keepdims=True), 0, 128)
    small[...] = small[...] + jnp.broadcast_to(pulled[:, None, :], small.shape)
    for i in range(8):
        produce(i, gain)
        if i:
            after_core(i - 1, gain)
    after_core(7, gain)
    after_first(6, ffn)
    after_first(1, query)
    after_first(7, ffn)
    after_first(3, query)
    for i in (1, 3, 5, 7):
        after_first(i, gain)
    dn = dh * gains[0:1]
    input_grad[...] = (
        dys[...] + inverse * (dn - normed * jnp.mean(dn * normed, axis=-1, keepdims=True))
    ).astype(BF16)
    after_second(5, others_att)
    after_first(5, query)
    after_second(1, query)
    after_first(7, query)
    after_second(7, others_att)
    after_second(3, query)
    for i in (1, 3, 5):
        after_second(i, gain)

    line_wait(3, 1)
    far_out[...] = along(3, 1, slice(0, 2 * half)).astype(BF16)
    go(remote(far_out, far_in, psend.at[2], precv.at[2], y_peer))
    after_second(5, query)
    after_second(7, query)
    after_second(7, gain)
    line_wait(3, 0)
    near_at = pl.ds(pl.multiple_of(y * half, 128), half)
    far_at = pl.ds(pl.multiple_of((1 - y) * half, 128), half)
    g_gate[:, near_at] = along(3, 0, slice(0, half))
    g_up[:, near_at] = along(3, 0, slice(half, 2 * half))
    finish((4, 1, 2))
    wait(far_in, precv.at[2])
    g_gate[:, far_at] = far_in[:, :half].astype(F32)
    g_up[:, far_at] = far_in[:, half:].astype(F32)
    finish((0, 5))
    for copy in pending:
        copy.wait_send()


def back(scalars, f32_args, bf16_args, heads_args, weights):
    dma = pltpu.SemaphoreType.DMA
    x = f32_args[0]
    h, o, h2, dgu, hid, og = bf16_args
    rows, width = x.shape
    half = hid.shape[1]
    own = width // 32
    down = half // 16
    shapes = [
        ((own, width), BF16),
        ((own, 2 * width), BF16),
        ((own, width), BF16),
        ((own, 2 * half), BF16),
        ((down, width), BF16),
        ((8, 128), F32),
    ]

    def buffers(*leads):
        return [pltpu.VMEM(lead + s, t) for lead, (s, t) in zip(leads, shapes)]

    none = (1,)

    shape = jax.ShapeDtypeStruct
    outs = [shape((rows, width), BF16)] * 2 + [shape((own, width), F32)] * 4
    outs += [shape((own, 2 * half), F32)] * 2 + [shape((down, width), F32), shape((8, 128), F32)]
    return pl.pallas_call(
        back_kernel,
        out_shape=outs,
        in_specs=[SM] * 3 + [VM] * 22 + [ANY] * 2,
        out_specs=[VM] * 10,
        scratch_shapes=buffers(*[(DEPTH, 4)] * 6)
        + buffers(*[(8, 2)] * 4, (4, 2), (8, 2))
        + buffers(*[(8,)] * 4, (4,), (8,))
        + buffers((4,), (4,), (4,), none, none, (4,))
        + buffers((3,), (3,), (3,), (6,), (3,), (3,))
        + [
            pltpu.VMEM((width, rows), BF16),
            pltpu.VMEM((width, rows), BF16),
            pltpu.VMEM((width, 2 * rows), BF16),
            pltpu.VMEM((half, 2 * rows), BF16),
            pltpu.VMEM((rows, width), BF16),
            pltpu.VMEM((rows, 2 * width), BF16),
            pltpu.VMEM((rows, width), F32),
            pltpu.VMEM((rows, width), BF16),
            pltpu.VMEM((rows, width), F32),
            pltpu.VMEM((rows, width), BF16),
            pltpu.VMEM((32, 8, 128), F32),
            pltpu.VMEM((8, 8, rows), F32),
            pltpu.VMEM((8, rows, WIDTH), BF16),
            pltpu.VMEM((8, 8, rows), F32),
            pltpu.VMEM((8, rows, WIDTH), BF16),
            pltpu.VMEM((rows, width), BF16),
            pltpu.VMEM((2, 32, own, width), BF16),
            pltpu.VMEM((rows, width), BF16),
            pltpu.VMEM((rows, width), BF16),
            pltpu.VMEM((own, 2 * half), BF16),
            pltpu.VMEM((own, 2 * half), BF16),
            dma((8, 2, 6)),
            dma((8, 2, 6)),
            dma((8, 2, 6)),
            dma((8, 2, 6)),
            dma((4, 6)),
            dma((4, 6)),
            dma((6, 6)),
            dma((6, 6)),
            dma((3,)),
            dma((7, 2)),
            dma((8, 2)),
            dma((7,)),
            dma((8,)),
            dma((2,)),
            dma((3,)),
            dma((3,)),
        ],
        compiler_params=pltpu.CompilerParams(
            collective_id=1, has_side_effects=True, vmem_limit_bytes=38 << 20
        ),
        name="back",
    )(*scalars, *f32_args, *bf16_args, *heads_args, *weights)


def settle_kernel(*refs):
    n = len(refs) // 2
    copies = [pltpu.make_async_copy(refs[i], refs[n + i], refs[2 * n].at[i]) for i in range(n)]
    for copy in copies:
        copy.start()
    for copy in copies:
        copy.wait()


def settle(arrays):
    return pl.pallas_call(
        settle_kernel,
        out_shape=[jax.ShapeDtypeStruct(a.shape, a.dtype) for a in arrays],
        in_specs=[VM] * len(arrays),
        out_specs=[ANY] * len(arrays),
        scratch_shapes=[pltpu.SemaphoreType.DMA((len(arrays),))],
        compiler_params=pltpu.CompilerParams(vmem_limit_bytes=8 << 20),
        name="settle",
    )(*arrays)


def gather_plain(pieces, keys, values, bias, ranks):
    full = [lax.all_gather(a, ("dp", "mem"), axis=0, tiled=False) for a in pieces]

    def spread(a):
        blocks = a.reshape(a.shape[0], HEADS, WIDTH).transpose(1, 0, 2)
        return lax.all_to_all(jnp.repeat(blocks, ranks, axis=0), "mem", 0, 0, tiled=True)

    return full + [
        spread(keys).reshape(-1, KEYS, WIDTH),
        spread(values).reshape(-1, KEYS, WIDTH),
        lax.all_gather(bias, "mem", axis=0, tiled=True),
    ]


def to_heads_plain(x, ranks):
    rank = lax.axis_index("mem") % ranks
    blocks = x if x.ndim == 3 else x.reshape(x.shape[0], HEADS, WIDTH).transpose(1, 0, 2)
    wide = jnp.where((jnp.arange(ranks) == rank)[None, :, None, None], blocks[:, None], 0)
    wide = wide.reshape((-1,) + blocks.shape[1:])
    got = lax.all_to_all(wide, "mem", 0, 0, tiled=True)
    return lax.dynamic_index_in_dim(got.reshape((-1, ranks) + blocks.shape[1:]), rank, 1, keepdims=False)


def to_tokens_plain(x, ranks, wide_out):
    rank = lax.axis_index("mem") % ranks
    wide = jnp.where((jnp.arange(ranks) == rank)[None, :, None, None], x[:, None], 0)
    got = lax.all_to_all(wide.reshape((-1,) + x.shape[1:]), "mem", 0, 0, tiled=True)
    got = lax.dynamic_index_in_dim(got.reshape((-1, ranks) + x.shape[1:]), rank, 1, keepdims=False)
    return got.transpose(1, 0, 2).reshape(x.shape[1], -1) if wide_out else got


def reduce_plain(h, dqkv, o, da, h2, dgu, hid, og, small):
    outs = []
    for a, b in ((h, dqkv), (o, da), (h2, dgu), (hid, og)):
        full = jnp.dot(a.T, b, preferred_element_type=F32)
        outs.append(lax.psum_scatter(full, ("dp", "mem"), scatter_dimension=0, tiled=True))
    outs.append(lax.psum_scatter(small, ("dp", "mem"), scatter_dimension=0, tiled=False))
    return outs


def normalize(values):
    inverse = lax.rsqrt(jnp.mean(values * values, axis=-1, keepdims=True) + epsilon)
    return (values * inverse, inverse)


def norm_back(grad_scaled, normed, inverse, gain_full):
    gain_grad = jnp.sum(grad_scaled * normed, axis=0)
    grad_normed = grad_scaled * gain_full
    grad_values = inverse * (
        grad_normed - normed * jnp.mean(grad_normed * normed, axis=-1, keepdims=True)
    )
    return (gain_grad, grad_values)


def feed_forward(normed_low, out_grad, gate_up, down):
    units = down.shape[0]
    both = jnp.dot(normed_low, gate_up, preferred_element_type=F32)
    gate, up = both[:, :units], both[:, units:]
    sigmoid_gate = jax.nn.sigmoid(gate)
    activated = gate * sigmoid_gate
    hidden = (activated * up).astype(BF16)
    grad_hidden = jnp.dot(out_grad, down.T, preferred_element_type=F32)
    grad_gate_up = jnp.concatenate(
        [
            (grad_hidden * up * sigmoid_gate * (1.0 + gate * (1.0 - sigmoid_gate))).astype(BF16),
            (grad_hidden * activated).astype(BF16),
        ],
        axis=1,
    )
    return hidden, grad_gate_up


def shards(
    tokens,
    gain_attn,
    w_query,
    w_key,
    w_value,
    w_out,
    gain_ffn,
    w_gate,
    w_up,
    w_down,
    mem_keys,
    mem_values,
    out_grad,
    key_mask,
    mem_sizes,
    seg_doc,
    seg_len,
):
    seg_rows, model_width = tokens.shape
    mem_count = lax.axis_size("mem")
    dp_count = lax.axis_size("dp")
    devices = mem_count * dp_count
    ranks = mem_count // HEADS
    direct = dp_count == 2 and mem_count == 16
    factor = WIDTH ** (-0.5)
    ff_width = w_gate.shape[1]
    own = gain_attn.shape[0]
    down_rows = w_down.shape[0]

    half = ff_width // 2
    if direct:
        joined = jnp.stack(
            [
                jnp.concatenate([w_gate[:, i * half : (i + 1) * half], w_up[:, i * half : (i + 1) * half]], axis=1)
                for i in range(2)
            ]
        )
    else:
        joined = jnp.concatenate([w_gate, w_up], axis=1)
    pieces = [
        jnp.concatenate([w_query, w_key, w_value], axis=1),
        w_out,
        joined,
        w_down,
        jnp.pad(jnp.concatenate([gain_attn, gain_ffn])[None], ((0, 15), (0, 128 - 2 * own))),
    ]
    bias = jnp.where(key_mask == 1, 0.0, neg_big).astype(F32).reshape(-1, 1, KEYS)
    bias = jnp.broadcast_to(bias, (bias.shape[0], 8, KEYS))
    rank = (lax.axis_index("mem") % ranks).reshape(1).astype(jnp.int32)
    if direct:
        split = (-1, KEYS, model_width)
        done = front(
            seg_doc,
            mem_sizes,
            seg_len,
            tokens,
            out_grad,
            pieces,
            mem_keys.reshape(split),
            mem_values.reshape(split),
            bias,
            own,
        )
        first, attended_low, attended, whole, normed_low, queries, keys_local, values_local = done[:8]
        q_heads, gains, pair_normed, pair_grad, joined_w, out_full, gate_up, down, _, kh, vh, bh = done[8:]
        pair_normed = pair_normed.reshape(2 * seg_rows, model_width)
        pair_grad = pair_grad.reshape(2 * seg_rows, model_width)
        gate_up = gate_up.reshape(model_width, 2 * half)
        down = down.reshape(half, model_width)
        hidden, grad_gate_up = feed_forward(pair_normed, pair_grad, gate_up, down)
        partial = jnp.dot(hidden, down, preferred_element_type=F32)
        grad_partial = jnp.dot(grad_gate_up, gate_up.T, preferred_element_type=F32)
        sums = back(
            (seg_doc, mem_sizes, seg_len),
            (
                tokens,
                gains,
                first,
                whole,
                attended,
                grad_partial[:seg_rows],
                grad_partial[seg_rows:].astype(BF16),
                partial[:seg_rows],
                partial[seg_rows:].astype(BF16),
            ),
            (normed_low, attended_low, pair_normed, grad_gate_up, hidden, pair_grad),
            (queries, keys_local, values_local, q_heads, kh, vh, bh),
            (joined_w, out_full),
        )
        small = sums[9]
        output, input_grad, g_q, g_k, g_v, g_o, g_gate, g_up, g_down = settle(sums[:9])
        return (
            output,
            input_grad,
            small[0, :own],
            g_q,
            g_k,
            g_v,
            g_o,
            small[0, own : 2 * own],
            g_gate,
            g_up,
            g_down,
        )

    inputs = tokens.astype(F32)
    normed_one, inverse_one = normalize(inputs)
    gathered = gather_plain(pieces, mem_keys, mem_values, bias, ranks)
    joined_w, out_full, gate_up, down_full, gains, kh, vh, bh = gathered
    gain_one = gains[:, 0, :own].reshape(-1).astype(F32)
    gain_two = gains[:, 0, own : 2 * own].reshape(-1).astype(F32)
    joined_w = joined_w.reshape(model_width, -1)
    out_full = out_full.reshape(model_width, -1)
    gate_up = gate_up.reshape(model_width, -1)
    down_full = down_full.reshape(ff_width, -1)
    normed_low = (normed_one * gain_one).astype(BF16)
    projected = jnp.dot(normed_low, joined_w, preferred_element_type=F32).astype(BF16)
    queries = projected[:, :model_width]
    keys_local = projected[:, model_width : 2 * model_width]
    values_local = projected[:, 2 * model_width :]
    query_heads = queries.reshape(seg_rows, HEADS, WIDTH)
    key_heads = keys_local.reshape(seg_rows, HEADS, WIDTH)
    value_heads = values_local.reshape(seg_rows, HEADS, WIDTH)
    positions = lax.iota(jnp.int32, seg_rows)
    local_ok = (positions[None, :] <= positions[:, None]) & (positions[None, :] < seg_len[0, 0])
    local_ok = local_ok[None]
    local_scores = (
        jnp.einsum("ihd,jhd->hij", query_heads, key_heads, preferred_element_type=F32) * factor
    )
    local_masked = jnp.where(local_ok, local_scores, neg_big)
    q_heads = to_heads_plain(queries, ranks)
    o_mem, lse_mem = memory_forward(ranks, seg_doc, mem_sizes, rank, q_heads, kh, vh, bh)
    mem_o = to_tokens_plain(o_mem, ranks, True).reshape(seg_rows, HEADS, WIDTH).astype(F32)
    mem_lse = to_tokens_plain(lse_mem, ranks, False)[:, 0, :] / LOG2E
    local_top = jnp.max(local_masked, axis=2)
    local_total = jnp.sum(
        jnp.where(local_ok, jnp.exp(local_masked - local_top[:, :, None]), 0.0), axis=2
    )
    local_lse = local_top + jnp.log(local_total)
    best = jnp.maximum(local_lse, mem_lse)
    log_total = best + jnp.log(jnp.exp(local_lse - best) + jnp.exp(mem_lse - best))
    local_probs = jnp.where(local_ok, jnp.exp(local_masked - log_total[:, :, None]), 0.0)
    local_low = local_probs.astype(BF16)
    attended = (
        jnp.einsum("hij,jhd->ihd", local_low, value_heads, preferred_element_type=F32)
        + mem_o * jnp.exp(mem_lse - log_total).T[..., None]
    )
    attended_low = attended.reshape(seg_rows, model_width).astype(BF16)
    first = inputs + jnp.dot(attended_low, out_full, preferred_element_type=F32)

    normed_two, inverse_two = normalize(first)
    normed_two_low = (normed_two * gain_two).astype(BF16)
    hidden, grad_gate_up = feed_forward(normed_two_low, out_grad, gate_up, down_full)
    output = (first + jnp.dot(hidden, down_full, preferred_element_type=F32)).astype(BF16)
    grad_normed_two = jnp.dot(grad_gate_up, gate_up.T, preferred_element_type=F32)
    grad_gain_two, grad_first_norm = norm_back(grad_normed_two, normed_two, inverse_two, gain_two)
    grad_first = out_grad.astype(F32) + grad_first_norm

    grad_branch = grad_first.astype(BF16)
    grad_attended = jnp.dot(grad_branch, out_full.T, preferred_element_type=F32).astype(BF16)
    grad_att_heads = grad_attended.reshape(seg_rows, HEADS, WIDTH)
    delta = jnp.sum(grad_att_heads.astype(F32) * attended, axis=-1).T
    stats = jnp.pad(jnp.stack([log_total * LOG2E, delta], axis=1), ((0, 0), (0, 6), (0, 0)))
    do_heads = to_heads_plain(grad_attended, ranks)
    stat_heads = to_heads_plain(stats, ranks)
    dq_heads = memory_backward(
        ranks, seg_doc, mem_sizes, rank, q_heads, do_heads, stat_heads, kh, vh, bh
    )
    grad_query_memory = to_tokens_plain(dq_heads, ranks, True)

    grad_value_heads = jnp.einsum(
        "hij,ihd->jhd", local_low, grad_att_heads, preferred_element_type=F32
    )
    grad_local_probs = jnp.einsum(
        "ihd,jhd->hij", grad_att_heads, value_heads, preferred_element_type=F32
    )
    grad_local_scores = (local_probs * (grad_local_probs - delta[:, :, None])).astype(BF16)
    grad_query_heads = (
        jnp.einsum("hij,jhd->ihd", grad_local_scores, key_heads, preferred_element_type=F32)
        * factor
    )
    grad_key_heads = (
        jnp.einsum("hij,ihd->jhd", grad_local_scores, query_heads, preferred_element_type=F32)
        * factor
    )
    grad_queries = grad_query_heads.reshape(seg_rows, model_width) + grad_query_memory.astype(F32)
    grad_joined = jnp.concatenate(
        [
            grad_queries,
            grad_key_heads.reshape(seg_rows, model_width),
            grad_value_heads.reshape(seg_rows, model_width),
        ],
        axis=1,
    ).astype(BF16)
    grad_normed_one = jnp.dot(grad_joined, joined_w.T, preferred_element_type=F32)
    grad_gain_one, grad_input_norm = norm_back(grad_normed_one, normed_one, inverse_one, gain_one)
    input_grad = (grad_first + grad_input_norm).astype(BF16)

    small = jnp.stack([grad_gain_one.reshape(devices, own), grad_gain_two.reshape(devices, own)], axis=1)
    small = jnp.pad(small, ((0, 0), (0, 6), (0, 128 - own)))
    attn_sums, out_sums, ffn_sums, down_sums, small_sums = reduce_plain(
        normed_low, grad_joined, attended_low, grad_branch, normed_two_low, grad_gate_up, hidden, out_grad, small
    )
    return (
        output,
        input_grad,
        small_sums[0, :own],
        attn_sums[:, :model_width],
        attn_sums[:, model_width : 2 * model_width],
        attn_sums[:, 2 * model_width : 3 * model_width],
        out_sums,
        small_sums[1, :own],
        ffn_sums[:, :ff_width],
        ffn_sums[:, ff_width:],
        down_sums,
    )


def solution(mesh):
    rows = P(("dp", "mem"), None)
    vector = P(("dp", "mem"))
    in_specs = (
        (rows, vector) + (rows,) * 4 + (vector,) + (rows,) * 6
        + (P("dp", "mem"), P("dp", None), P("dp", None), P("dp", "mem"))
    )
    out_specs = (rows, rows, vector) + (rows,) * 4 + (vector,) + (rows,) * 3
    return jax.shard_map(shards, mesh=mesh, in_specs=in_specs, out_specs=out_specs, check_vma=False)
```
